32 devices in a mesh: row: 16 (over z, y, x), col: 2 (over core).
Axes of the slice: x: 2, y: 2, z: 4, core: 2. Of those that a mesh axis runs over, the one named last changes fastest.
Arguments:
- object_field: float32 [2, 8192, 1024], P(None, 'row', 'col'), may hold values from -13 to 13
- probe_modes: float32 [2, 2, 256, 256], replicated, may hold values from -5 to 5
- scan_offsets: int32 [16, 2, 2, 6], P('row', 'col'), may hold values from 0 to 7936, as said below
- scan_counts: int32 [16, 2], P('row', 'col'), may hold values from 1 to 6, as said below
- amplitudes: bfloat16 [16, 2, 6, 256, 256], P('row', 'col'), may hold values from 0 to 2.5
Outputs:
- object_new: float32 [2, 8192, 1024], P(None, 'row', 'col')
- probe_new: float32 [2, 2, 256, 256], replicated
The draws below stay inside these ranges and needn't reach their ends.
Inputs may be any that keep to these rules, and one draw needn't show every extreme that they name: `scan_counts`: some tile has exactly 6 live positions. `scan_offsets`: each patch of 256 x 256 pixels lies inside the object, and its centre (top-left plus 256 // 2 in each direction) lies in the slot's own tile.
All inputs are finite; a program needn't handle non-finite values.
Results may differ from the reference program's by a relative error of at most 0.0003.
Values sent between devices are 32-bit elements; how exact they have to be, the bound alone decides.
No kernel may reach another device: no remote copies, remote signals or barrier semaphores. Data moves between devices by JAX's collectives and lax.ppermute only.
A program may use at most 64 MiB of HBM per device.

```python
import jax
import jax.numpy as jnp
from jax import lax

PROBE = 256
MODES = 2
TILE_H = 512
TILE_W = 512
SLOTS = 6
TILES_R = 16
TILES_C = 2
HEIGHT = 8192
WIDTH = 1024


def scan_plan(key):
    base_key = jax.random.fold_in(key, 7)
    key_list = jax.random.split(base_key, 4)
    tile_count = TILES_R * TILES_C
    rank_draw = jax.random.randint(key_list[0], (tile_count,), 0, SLOTS)
    live_counts = 1 + rank_draw * rank_draw // SLOTS
    busiest = jax.random.randint(key_list[1], (), 0, tile_count)
    live_counts = jnp.where(jnp.arange(tile_count) == busiest, SLOTS, live_counts)
    live_counts = live_counts.astype(jnp.int32).reshape(TILES_R, TILES_C)
    centre_rows = jnp.arange(TILES_R, dtype=jnp.int32)[:, None, None] * TILE_H + jax.random.randint(key_list[2], (TILES_R, TILES_C, SLOTS), 0, TILE_H)
    centre_cols = jnp.arange(TILES_C, dtype=jnp.int32)[None, :, None] * TILE_W + jax.random.randint(key_list[3], (TILES_R, TILES_C, SLOTS), 0, TILE_W)
    top_edge = jnp.clip(centre_rows - PROBE // 2, 0, HEIGHT - PROBE)
    left_edge = jnp.clip(centre_cols - PROBE // 2, 0, WIDTH - PROBE)
    offsets = jnp.stack([top_edge, left_edge], axis=2).astype(jnp.int32)
    return (offsets, live_counts)


def draw_scan_offsets(key, part):
    return scan_plan(key)[0]


def draw_scan_counts(key, part):
    return scan_plan(key)[1]


def draw_object_field(key, part):
    key_list = jax.random.split(jax.random.fold_in(key, 11), 2)
    row_place = jnp.arange(HEIGHT, dtype=jnp.float32) / HEIGHT
    entries = jax.random.truncated_normal(key_list[0], -4.0, 4.0, (2, HEIGHT, WIDTH), jnp.float32)
    row_scale = 10.0 ** (0.5 * row_place - 0.25)
    col_scale = 10.0 ** (0.5 * jax.random.uniform(key_list[1], (WIDTH,), jnp.float32) - 0.25)
    return entries * row_scale[None, :, None] * col_scale[None, None, :]


def levels(stream_key, shape, cuts, low, high):
    def one(dim, shards_of):
        draws = jax.random.uniform(jax.random.fold_in(jax.random.fold_in(stream_key, 6), dim), (shards_of,), jnp.float32, low / len(cuts), high / len(cuts))
        return jnp.repeat(jnp.exp(draws), shape[dim] // shards_of).reshape((-1,) + (1,) * (len(shape) - dim - 1))

    loudness = one(*cuts[0])
    for cut in cuts[1:]:
        loudness = loudness * one(*cut)
    return loudness


def noise(key, dims, width, reach, kind=jnp.bfloat16):
    return jnp.clip(width * jax.random.normal(key, dims, jnp.float32), -reach, reach).astype(kind)


def setup_inputs(seed: int = 0) -> dict:
    arg_keys = jax.random.split(jax.random.key(seed), 6)
    object_field = draw_object_field(jax.random.fold_in(arg_keys[5], 71), 0)
    probe_modes = noise(arg_keys[1], (2, MODES, PROBE, PROBE), 1.0, 5.0, jnp.float32)
    scan_offsets = draw_scan_offsets(jax.random.fold_in(arg_keys[5], 71), 0)
    scan_counts = draw_scan_counts(jax.random.fold_in(arg_keys[5], 71), 0)
    amplitudes = jnp.clip(2.5 * jax.random.uniform(arg_keys[4], (TILES_R, TILES_C, SLOTS, PROBE, PROBE), jnp.float32) ** levels(arg_keys[4], (TILES_R, TILES_C, SLOTS, PROBE, PROBE), ((0, 16), (1, 2)), -0.2, 0.2), 0.0, 2.5).astype(jnp.bfloat16)
    return {"object_field": object_field, "probe_modes": probe_modes, "scan_offsets": scan_offsets, "scan_counts": scan_counts, "amplitudes": amplitudes}


def reference(object_field, probe_modes, scan_offsets, scan_counts, amplitudes):
    float_type = object_field.dtype
    object_complex = lax.complex(object_field[0], object_field[1])
    probe_complex = lax.complex(probe_modes[0], probe_modes[1])
    probe_power = lax.optimization_barrier(jnp.sum(probe_modes[0] * probe_modes[0] + probe_modes[1] * probe_modes[1], axis=0))
    slot_total = TILES_R * TILES_C * SLOTS
    offset_rows = jnp.transpose(scan_offsets, (0, 1, 3, 2)).reshape(slot_total, 2)
    live_flags = (jnp.arange(SLOTS, dtype=jnp.int32)[None, None, :] < scan_counts[:, :, None]).reshape(slot_total)
    amplitude_rows = amplitudes.reshape(slot_total, PROBE, PROBE)

    def visit_slot(position, state_tuple):
        object_grad, lighting, probe_grad, probe_norm = state_tuple
        row_start = offset_rows[position, 0]
        col_start = offset_rows[position, 1]
        weight_live = live_flags[position].astype(float_type)
        patch_field = lax.dynamic_slice(object_complex, (row_start, col_start), (PROBE, PROBE))
        far_field = jnp.fft.fft2(probe_complex * patch_field[None], norm='ortho')
        intensity = lax.optimization_barrier(jnp.sum(far_field.real * far_field.real + far_field.imag * far_field.imag, axis=0))
        factor = amplitude_rows[position].astype(float_type) / jnp.sqrt(jnp.maximum(intensity, 0.25)) - 1.0
        back_field = jnp.fft.ifft2(far_field * factor[None], norm='ortho')
        update = lax.optimization_barrier(jnp.sum(jnp.conj(probe_complex) * back_field, axis=0)) * weight_live
        window = lax.dynamic_slice(object_grad, (row_start, col_start), (PROBE, PROBE))
        object_grad = lax.dynamic_update_slice(object_grad, window + update, (row_start, col_start))
        shade = lax.dynamic_slice(lighting, (row_start, col_start), (PROBE, PROBE))
        lighting = lax.dynamic_update_slice(lighting, shade + probe_power * weight_live, (row_start, col_start))
        probe_grad = probe_grad + jnp.conj(patch_field)[None] * back_field * weight_live
        probe_norm = probe_norm + (patch_field.real * patch_field.real + patch_field.imag * patch_field.imag) * weight_live
        return (object_grad, lighting, probe_grad, probe_norm)
    initial = (jnp.zeros_like(object_complex), jnp.zeros((HEIGHT, WIDTH), float_type), jnp.zeros_like(probe_complex), jnp.zeros((PROBE, PROBE), float_type))
    object_grad, lighting, probe_grad, probe_norm = lax.fori_loop(0, slot_total, visit_slot, initial)
    object_next = object_complex + object_grad / (lighting + 1.0)
    probe_next = probe_complex + probe_grad / (probe_norm + 1.0)[None]
    return (jnp.stack([object_next.real, object_next.imag]), jnp.stack([probe_next.real, probe_next.imag]))
```

```python
import functools
import math

import jax
import jax.numpy as jnp
import numpy as np
from jax import lax
from jax.experimental import pallas as pl
from jax.experimental.pallas import tpu as pltpu
from jax.sharding import PartitionSpec as P

F32 = jnp.float32
BF16 = jnp.bfloat16
LANES = 128


def split_host(table):
    high = table.astype(BF16)
    low = (table - high.astype(np.float64)).astype(BF16)
    return high, low


def dft_tables(edge):
    half = edge // 2
    scale = 1.0 / math.sqrt(edge)
    n = np.arange(half)[:, None]
    k = np.arange(half)[None, :]
    right, left = [], []
    for parity in (0, 1):
        angle = (n * (2 * k + parity) % edge) * (2.0 * np.pi / edge)
        cosine, sine = np.cos(angle) * scale, np.sin(angle) * scale
        w = np.block([[cosine, -sine], [sine, cosine]])
        right.append(w)
        left.append(w.T)
    mats = [right[0], right[1], left[0], left[1]]
    as_right = []
    as_left = []
    for m in mats:
        high, low = split_host(m)
        as_right.append(np.concatenate([high, high, low], axis=0))
        as_left.append(np.concatenate([high, high, low], axis=1))
    return (
        np.stack([as_right[0], as_right[1], as_right[2], as_right[3]]),
        np.stack([as_left[2], as_left[3], as_left[0], as_left[1]]),
    )


def split_parts(x):
    high = x.astype(BF16)
    low = (x - high.astype(F32)).astype(BF16)
    return high, low


def right_dot(x, table):
    high, low = split_parts(x)
    return jnp.dot(jnp.concatenate([high, low, high], axis=1), table, preferred_element_type=F32)


def left_dot(table, x):
    high, low = split_parts(x)
    return jnp.dot(table, jnp.concatenate([high, low, high], axis=0), preferred_element_type=F32)


def slots_kernel(
    phase,
    geometry,
    meta,
    tile,
    left,
    right,
    top,
    bottom,
    probe,
    amps,
    rights,
    lefts,
    probe_in,
    *refs,
):
    tile_rows, tile_cols, margin, edge, modes = geometry
    tiles = tile_cols // LANES
    side = margin // LANES
    half = edge // 2
    outs, scratch = refs[:-4], refs[-4:]
    ext, acc, amp_buf, sems = scratch
    if phase == 0:
        mid_out, left_out, right_out, lit_mid, lit_top, lit_bottom, lit_left, lit_right, probe_out = outs
    else:
        mid_out, top_out, bottom_out, left_out, right_out, probe_out = outs
    count = meta[2, 0]

    loads = []

    def load(src, dst):
        copy = pltpu.make_async_copy(src, dst, sems.at[len(loads)])
        copy.start()
        loads.append(copy)

    body = pl.ds(margin, tile_rows)
    for t in range(tiles):
        load(tile.at[:, :, pl.ds(t * LANES, LANES)], ext.at[side + t, :, body, :])
    if phase == 0:
        load(left, ext.at[0, :, body, :])
        load(right, ext.at[side + tiles, :, body, :])
    else:
        load(left, ext.at[0])
        load(right, ext.at[side + tiles])
        for t in range(tiles):
            load(top.at[:, :, pl.ds(t * LANES, LANES)], ext.at[side + t, :, pl.ds(0, margin), :])
            load(
                bottom.at[:, :, pl.ds(t * LANES, LANES)],
                ext.at[side + t, :, pl.ds(margin + tile_rows, margin), :],
            )
    acc[...] = jnp.zeros_like(acc)
    probe_out[...] = probe_in[...]
    for copy in loads:
        copy.wait()

    lane = lax.broadcasted_iota(jnp.int32, (edge, LANES), 1)
    power = [
        sum(
            probe[c, k, :, pl.ds(t * LANES, LANES)] * probe[c, k, :, pl.ds(t * LANES, LANES)]
            for c in range(2)
            for k in range(modes)
        )
        for t in range(2)
    ] if phase == 0 else None

    def add_window(channel, parts, row, block, shift):
        keep = lane >= shift
        first = pltpu.roll(parts[0], shift, 1)
        second = pltpu.roll(parts[1], shift, 1)
        rows = pl.ds(row, edge)
        zero = jnp.zeros_like(first)
        acc[block, channel, rows, :] += jnp.where(keep, first, zero)
        acc[block + 1, channel, rows, :] += jnp.where(keep, second, first)
        acc[block + 2, channel, rows, :] += jnp.where(keep, zero, second)

    def visit(slot, carry):
        row = meta[0, slot]
        col = meta[1, slot]
        block = col // LANES
        shift = col - block * LANES
        interior = jnp.logical_and(row >= margin, row + edge <= margin + tile_rows)
        chosen = interior if phase == 0 else jnp.logical_not(interior)

        if phase == 0:
            add_window(2, power, row, block, shift)

        @pl.when(chosen)
        def _():
            fetch = pltpu.make_async_copy(amps.at[slot], amp_buf, sems.at[len(loads)])
            fetch.start()
            back_shift = lax.rem(LANES - shift, LANES)
            keep = lane < LANES - shift
            patch = []
            for c in range(2):
                rolled = [
                    pltpu.roll(ext[block + t, c, pl.ds(row, edge), :], back_shift, 1)
                    for t in range(3)
                ]
                patch.append([jnp.where(keep, rolled[t], rolled[t + 1]) for t in range(2)])

            def probe_at(c, k, t):
                return probe[c, k, :, pl.ds(t * LANES, LANES)]

            evens, odds = [], []
            for k in range(modes):
                re = [probe_at(0, k, t) * patch[0][t] - probe_at(1, k, t) * patch[1][t] for t in range(2)]
                im = [probe_at(0, k, t) * patch[1][t] + probe_at(1, k, t) * patch[0][t] for t in range(2)]
                even = right_dot(jnp.concatenate([re[0] + re[1], im[0] + im[1]], axis=1), rights[0])
                odd = right_dot(jnp.concatenate([re[0] - re[1], im[0] - im[1]], axis=1), rights[1])
                evens.append(even)
                odds.append(odd)
            far = []
            for k in range(modes):
                re = jnp.concatenate([evens[k][:, :half], odds[k][:, :half]], axis=1)
                im = jnp.concatenate([evens[k][:, half:], odds[k][:, half:]], axis=1)
                far.append(
                    [
                        left_dot(
                            lefts[0],
                            jnp.concatenate([re[:half] + re[half:], im[:half] + im[half:]], axis=0),
                        ),
                        left_dot(
                            lefts[1],
                            jnp.concatenate([re[:half] - re[half:], im[:half] - im[half:]], axis=0),
                        ),
                    ]
                )
            fetch.wait()
            factor = []
            for p in range(2):
                total = sum(
                    far[k][p][:half] * far[k][p][:half] + far[k][p][half:] * far[k][p][half:]
                    for k in range(modes)
                )
                amp = amp_buf[pl.ds(p * half, half), :].astype(F32)
                one = amp / jnp.sqrt(jnp.maximum(total, 0.25)) - 1.0
                factor.append(jnp.concatenate([one, one], axis=0))
            update = [[None, None], [None, None]]
            for k in range(modes):
                even = left_dot(lefts[2], far[k][0] * factor[0])
                odd = left_dot(lefts[3], far[k][1] * factor[1])
                plus, minus = even + odd, even - odd
                re = jnp.concatenate([plus[:half], minus[:half]], axis=0)
                im = jnp.concatenate([plus[half:], minus[half:]], axis=0)
                even = right_dot(jnp.concatenate([re[:, :half], im[:, :half]], axis=1), rights[2])
                odd = right_dot(jnp.concatenate([re[:, half:], im[:, half:]], axis=1), rights[3])
                plus, minus = even + odd, even - odd
                back_re = [plus[:, :half], minus[:, :half]]
                back_im = [plus[:, half:], minus[:, half:]]
                for t in range(2):
                    pr, pi = probe_at(0, k, t), probe_at(1, k, t)
                    u_re = pr * back_re[t] + pi * back_im[t]
                    u_im = pr * back_im[t] - pi * back_re[t]
                    update[0][t] = u_re if k == 0 else update[0][t] + u_re
                    update[1][t] = u_im if k == 0 else update[1][t] + u_im
                    lanes = pl.ds(t * LANES, LANES)
                    xr, xi = patch[0][t], patch[1][t]
                    probe_out[k, :, lanes] += xr * back_re[t] + xi * back_im[t]
                    probe_out[modes + k, :, lanes] += xr * back_im[t] - xi * back_re[t]
            for t in range(2):
                lanes = pl.ds(t * LANES, LANES)
                probe_out[2 * modes, :, lanes] += patch[0][t] * patch[0][t] + patch[1][t] * patch[1][t]
            for c in range(2):
                add_window(c, update[c], row, block, shift)

        return carry

    lax.fori_loop(0, count, visit, 0)

    stores = []

    def store(src, dst):
        copy = pltpu.make_async_copy(src, dst, sems.at[len(stores)])
        copy.start()
        stores.append(copy)

    def store_all(chan, mid, above, below, west, east):
        for t in range(tiles):
            cols = pl.ds(t * LANES, LANES)
            store(acc.at[side + t, chan, body, :], mid.at[:, :, cols])
            if above is not None:
                store(acc.at[side + t, chan, pl.ds(0, margin), :], above.at[:, :, cols])
                store(acc.at[side + t, chan, pl.ds(margin + tile_rows, margin), :], below.at[:, :, cols])
        if above is not None:
            store(acc.at[0, chan], west)
            store(acc.at[side + tiles, chan], east)
        else:
            store(acc.at[0, chan, body, :], west)
            store(acc.at[side + tiles, chan, body, :], east)

    grads = pl.ds(0, 2)
    if phase == 0:
        store_all(grads, mid_out, None, None, left_out, right_out)
        store_all(pl.ds(2, 1), lit_mid, lit_top, lit_bottom, lit_left, lit_right)
    else:
        store_all(grads, mid_out, top_out, bottom_out, left_out, right_out)
    for copy in stores:
        copy.wait()


def run_slots(phase, geometry, meta, tile, left, right, top, bottom, probe, amps, tables, probe_in):
    tile_rows, tile_cols, margin, edge, modes = geometry
    rows_all = tile_rows + 2 * margin
    tiles = tile_cols // LANES
    anywhere = pl.BlockSpec(memory_space=pl.ANY)
    vmem = pl.BlockSpec(memory_space=pltpu.VMEM)
    smem = pl.BlockSpec(memory_space=pltpu.SMEM)

    def shape(*dims):
        return jax.ShapeDtypeStruct(dims, F32)

    probe_shape = shape(2 * modes + 1, edge, edge)
    if phase == 0:
        outs = [shape(2, tile_rows, tile_cols), shape(2, tile_rows, margin), shape(2, tile_rows, margin)]
        lead = 1
        outs += [
            shape(lead, tile_rows, tile_cols),
            shape(lead, margin, tile_cols),
            shape(lead, margin, tile_cols),
            shape(lead, rows_all, margin),
            shape(lead, rows_all, margin),
        ]
    else:
        lead = 2
        outs = [
            shape(lead, tile_rows, tile_cols),
            shape(lead, margin, tile_cols),
            shape(lead, margin, tile_cols),
            shape(lead, rows_all, margin),
            shape(lead, rows_all, margin),
        ]
    out_specs = [anywhere] * len(outs) + [vmem]
    outs.append(probe_shape)
    channels = 3 if phase == 0 else 2
    blocks = tiles + 3
    kernel = functools.partial(slots_kernel, phase, geometry)
    return pl.pallas_call(
        kernel,
        out_shape=outs,
        in_specs=[smem, anywhere, anywhere, anywhere, anywhere, anywhere, vmem, anywhere, vmem, vmem, vmem],
        out_specs=out_specs,
        scratch_shapes=[
            pltpu.VMEM((blocks, 2, rows_all, LANES), F32),
            pltpu.VMEM((blocks, channels, rows_all, LANES), F32),
            pltpu.VMEM((edge, edge), BF16),
            pltpu.SemaphoreType.DMA((40,)),
        ],
        compiler_params=pltpu.CompilerParams(vmem_limit_bytes=48 * 1024 * 1024),
        cost_estimate=pl.CostEstimate(flops=int(1e10), bytes_accessed=20_000_000, transcendentals=0),
        name=f"slots_{phase}",
    )(meta, tile, left, right, top, bottom, probe, amps, tables[0], tables[1], probe_in)


def shift_both(low, high, axis):
    count = lax.axis_size(axis)
    up = [(i, i + 1) for i in range(count - 1)]
    down = [(i + 1, i) for i in range(count - 1)]
    return lax.ppermute(high, axis, up), lax.ppermute(low, axis, down)


def bits_of(count):
    return count.bit_length() - 1


def all_reduce_finish(stack, finish, stages):
    def index_of(axis, bits):
        place = lax.axis_index(axis)
        index = jnp.int32(0)
        for position, bit in enumerate(bits):
            index = index + (((place >> bit) & 1) << position)
        return index

    def partner_perm(axis, bits, member):
        mask = sum(((member >> position) & 1) << bit for position, bit in enumerate(bits))
        return [(i, i ^ mask) for i in range(lax.axis_size(axis))]

    start = jnp.int32(0)
    for axis, bits in stages:
        group = 1 << len(bits)
        rows = stack.shape[1] // group
        index = index_of(axis, bits)
        total = lax.dynamic_slice_in_dim(stack, index * rows, rows, axis=1)
        pieces = []
        for member in range(1, group):
            piece = lax.dynamic_slice_in_dim(stack, (index ^ member) * rows, rows, axis=1)
            pieces.append(lax.ppermute(piece, axis, partner_perm(axis, bits, member)))
        for piece in pieces:
            total = total + piece
        start = start + index * rows
        stack = total
    shard = finish(stack, start)
    for axis, bits in reversed(stages):
        group = 1 << len(bits)
        rows = shard.shape[1]
        index = index_of(axis, bits)
        pieces = [shard]
        for member in range(1, group):
            pieces.append(lax.ppermute(shard, axis, partner_perm(axis, bits, member)))
        if group == 2:
            shard = jnp.where(
                index == 0,
                jnp.concatenate(pieces, axis=1),
                jnp.concatenate(pieces[::-1], axis=1),
            )
        else:
            whole = jnp.zeros((shard.shape[0], rows * group, shard.shape[2]), F32)
            for member in range(group):
                whole = lax.dynamic_update_slice_in_dim(
                    whole, pieces[member], (index ^ member) * rows, axis=1
                )
            shard = whole
    return shard


def stages_of(rows, cols):
    stages = [("col", (bit,)) for bit in range(bits_of(cols))]
    row_bits = list(range(1, bits_of(rows))) + [0]
    while row_bits:
        take, row_bits = row_bits[:1], row_bits[1:]
        stages.append(("row", tuple(take)))
    return stages


def on_device(object_field, probe_modes, scan_offsets, scan_counts, amplitudes):
    tile_rows = object_field.shape[1]
    tile_cols = object_field.shape[2]
    modes = probe_modes.shape[1]
    edge = probe_modes.shape[-1]
    margin = edge // 2
    slots = amplitudes.shape[2]
    geometry = (tile_rows, tile_cols, margin, edge, modes)
    anchor = jnp.stack(
        [lax.axis_index("row") * tile_rows - margin, lax.axis_index("col") * tile_cols - margin]
    )
    places = scan_offsets[0, 0] - anchor[:, None].astype(jnp.int32)
    meta = jnp.concatenate([places, jnp.broadcast_to(scan_counts[0, 0], (1, slots))], axis=0)

    top, bottom = shift_both(object_field[:, :margin], object_field[:, tile_rows - margin :], "row")
    left, right = shift_both(
        object_field[:, :, :margin], object_field[:, :, tile_cols - margin :], "col"
    )
    tables = tuple(jnp.asarray(t) for t in dft_tables(edge))
    order = np.concatenate([np.arange(0, edge, 2), np.arange(1, edge, 2)])
    select = jnp.asarray(np.eye(edge)[order].astype(BF16))
    amps = jnp.einsum("ui,sij->suj", select, amplitudes[0, 0], preferred_element_type=BF16)
    amps = jnp.einsum("suj,vj->suv", amps, select, preferred_element_type=BF16)

    none = jnp.zeros((2 * modes + 1, edge, edge), F32)
    first = run_slots(
        0, geometry, meta, object_field, left, right, top[:1, :8, :128], bottom[:1, :8, :128], probe_modes, amps, tables, none
    ) if False else run_slots(
        0, geometry, meta, object_field, left, right, left, right, probe_modes, amps, tables, none
    )
    grad_a, left_a, right_a, lit_mid, lit_top, lit_bottom, lit_left, lit_right, probe_a = first

    corner = jnp.concatenate([top, bottom], axis=1)
    corner_left, corner_right = shift_both(
        corner[:, :, :margin], corner[:, :, tile_cols - margin :], "col"
    )

    def tall(corners, mid):
        return jnp.concatenate([corners[:, :margin], mid, corners[:, margin:]], axis=1)

    second = run_slots(
        1,
        geometry,
        meta,
        object_field,
        tall(corner_left, left),
        tall(corner_right, right),
        top,
        bottom,
        probe_modes,
        amps,
        tables,
        probe_a,
    )
    grad_b, top_b, bottom_b, left_b, right_b, probe_sum = second

    pad = ((0, 0), (margin, margin), (0, 0))
    west = jnp.concatenate([left_b + jnp.pad(left_a, pad), lit_left], axis=0)
    east = jnp.concatenate([right_b + jnp.pad(right_a, pad), lit_right], axis=0)
    from_west, from_east = shift_both(west, east, "col")
    add_cols = jnp.concatenate(
        [from_west, jnp.zeros((3, tile_rows + 2 * margin, tile_cols - 2 * margin), F32), from_east],
        axis=2,
    )
    above = jnp.concatenate([top_b, lit_top], axis=0) + add_cols[:, :margin]
    below = jnp.concatenate([bottom_b, lit_bottom], axis=0) + add_cols[:, margin + tile_rows :]
    from_above, from_below = shift_both(above, below, "row")

    def finish(stack, start):
        rows = stack.shape[1]
        old = lax.dynamic_slice_in_dim(
            probe_modes.reshape(2 * modes, edge, edge), start, rows, axis=1
        )
        return old + stack[: 2 * modes] / (stack[2 * modes :] + 1.0)

    stages = stages_of(lax.axis_size("row"), lax.axis_size("col"))
    probe_new = all_reduce_finish(probe_sum, finish, stages).reshape(probe_modes.shape)

    mid = jnp.concatenate([grad_a + grad_b, lit_mid], axis=0) + add_cols[:, margin : margin + tile_rows]
    add_rows = jnp.concatenate(
        [from_above, jnp.zeros((3, tile_rows - 2 * margin, tile_cols), F32), from_below], axis=1
    )
    mid = mid + add_rows
    object_new = object_field + mid[:2] / (mid[2:] + 1.0)
    return object_new, probe_new


def solution(mesh):
    in_specs = (
        P(None, "row", "col"),
        P(),
        P("row", "col", None, None),
        P("row", "col"),
        P("row", "col", None, None, None),
    )
    out_specs = (P(None, "row", "col"), P())
    return jax.shard_map(
        on_device, mesh=mesh, in_specs=in_specs, out_specs=out_specs, check_vma=False
    )
```

```python
import functools
import math

import jax
import jax.numpy as jnp
import numpy as np
from jax import lax
from jax.experimental import pallas as pl
from jax.experimental.pallas import tpu as pltpu
from jax.sharding import PartitionSpec as P


F32 = jnp.float32
BF16 = jnp.bfloat16
LANES = 128


def split_host(table):
    high = table.astype(BF16)
    low = (table - high.astype(np.float64)).astype(BF16)
    return high, low


def dft_tables(edge):
    half = edge // 2
    scale = 1.0 / math.sqrt(edge)
    n = np.arange(half)[:, None]
    k = np.arange(half)[None, :]
    right, left = [], []
    for parity in (0, 1):
        angle = (n * (2 * k + parity) % edge) * (2.0 * np.pi / edge)
        cosine, sine = np.cos(angle) * scale, np.sin(angle) * scale
        w = np.block([[cosine, -sine], [sine, cosine]])
        right.append(w)
        left.append(w.T)
    mats = [right[0], right[1], left[0], left[1]]
    as_right = []
    as_left = []
    for m in mats:
        high, low = split_host(m)
        as_right.append(np.concatenate([high, high, low], axis=0))
        as_left.append(np.concatenate([high, high, low], axis=1))
    return (
        np.stack([as_right[0], as_right[1], as_right[2], as_right[3]]),
        np.stack([as_left[2], as_left[3], as_left[0], as_left[1]]),
    )


def split_parts(x):
    high = x.astype(BF16)
    low = (x - high.astype(F32)).astype(BF16)
    return high, low


def right_dot(x, table):
    high, low = split_parts(x)
    return jnp.dot(jnp.concatenate([high, low, high], axis=1), table, preferred_element_type=F32)


def left_dot(table, x):
    high, low = split_parts(x)
    return jnp.dot(table, jnp.concatenate([high, low, high], axis=0), preferred_element_type=F32)


VMEM = pltpu.VMEM
ANYWHERE = pl.BlockSpec(memory_space=pl.ANY)
IN_VMEM = pl.BlockSpec(memory_space=pltpu.VMEM)
IN_SMEM = pl.BlockSpec(memory_space=pltpu.SMEM)
MIB = 1024 * 1024


def shape(*dims):
    return jax.ShapeDtypeStruct(dims, F32)


def aligned(start, size):
    return pl.ds(pl.multiple_of(start, size) if size % 8 == 0 else start, size)


def copy_all(pairs, sems):
    copies = []
    for number, (src, dst) in enumerate(pairs):
        copy = pltpu.make_async_copy(src, dst, sems.at[number])
        copy.start()
        copies.append(copy)
    return copies


def pack_kernel(margin, tile, top, bottom, left, right, sems):
    rows, cols = tile.shape[1:]
    copies = copy_all(
        [
            (tile.at[:, pl.ds(0, margin), :], top),
            (tile.at[:, pl.ds(rows - margin, margin), :], bottom),
            (tile.at[:, :, pl.ds(0, margin)], left),
            (tile.at[:, :, pl.ds(cols - margin, margin)], right),
        ],
        sems,
    )
    for copy in copies:
        copy.wait()


def pack_edges(tile, margin):
    rows, cols = tile.shape[1:]
    return pl.pallas_call(
        functools.partial(pack_kernel, margin),
        out_shape=[shape(2, margin, cols)] * 2 + [shape(2, rows, margin)] * 2,
        in_specs=[ANYWHERE],
        out_specs=[IN_VMEM] * 4,
        scratch_shapes=[pltpu.SemaphoreType.DMA((4,))],
        compiler_params=pltpu.CompilerParams(vmem_limit_bytes=8 * MIB),
        name="pack_edges",
    )(tile)


def add_window(acc, channel, parts, row, block, shift, edge):
    lane = lax.broadcasted_iota(jnp.int32, (edge, LANES), 1)
    keep = lane >= shift
    first = pltpu.roll(parts[0], shift, 1)
    second = pltpu.roll(parts[1], shift, 1)
    rows = pl.ds(row, edge)
    zero = jnp.zeros_like(first)
    last = jnp.minimum(block + 2, acc.shape[0] - 1)
    acc[block, channel, rows, :] += jnp.where(keep, first, zero)
    acc[block + 1, channel, rows, :] += jnp.where(keep, second, first)
    acc[last, channel, rows, :] += jnp.where(keep, zero, second)


def slot_body(slot, row, col, ext, acc, sums, probe, amps, rights, lefts):
    edge = probe.shape[-1]
    modes = probe.shape[1]
    half = edge // 2
    block = col // LANES
    shift = col - block * LANES
    lane = lax.broadcasted_iota(jnp.int32, (edge, LANES), 1)
    back_shift = lax.rem(LANES - shift, LANES)
    keep = lane < LANES - shift
    last = jnp.minimum(block + 2, ext.shape[0] - 1)
    patch = []
    for c in range(2):
        rolled = [
            pltpu.roll(ext[b, c, pl.ds(row, edge), :], back_shift, 1) for b in (block, block + 1, last)
        ]
        patch.append([jnp.where(keep, rolled[t], rolled[t + 1]) for t in range(2)])

    def probe_at(c, k, t):
        return probe[c, k, :, pl.ds(t * LANES, LANES)]

    evens, odds = [], []
    for k in range(modes):
        re = [probe_at(0, k, t) * patch[0][t] - probe_at(1, k, t) * patch[1][t] for t in range(2)]
        im = [probe_at(0, k, t) * patch[1][t] + probe_at(1, k, t) * patch[0][t] for t in range(2)]
        evens.append(right_dot(jnp.concatenate([re[0] + re[1], im[0] + im[1]], axis=1), rights[0]))
        odds.append(right_dot(jnp.concatenate([re[0] - re[1], im[0] - im[1]], axis=1), rights[1]))
    far = []
    for k in range(modes):
        re = jnp.concatenate([evens[k][:, :half], odds[k][:, :half]], axis=1)
        im = jnp.concatenate([evens[k][:, half:], odds[k][:, half:]], axis=1)
        plus = jnp.concatenate([re[:half] + re[half:], im[:half] + im[half:]], axis=0)
        minus = jnp.concatenate([re[:half] - re[half:], im[:half] - im[half:]], axis=0)
        far.append([left_dot(lefts[0], plus), left_dot(lefts[1], minus)])
    factor = []
    for p in range(2):
        total = sum(
            far[k][p][:half] * far[k][p][:half] + far[k][p][half:] * far[k][p][half:]
            for k in range(modes)
        )
        amp = amps[slot, pl.ds(p * half, half), :].astype(F32)
        one = amp / jnp.sqrt(jnp.maximum(total, 0.25)) - 1.0
        factor.append(jnp.concatenate([one, one], axis=0))
    update = [[None, None], [None, None]]
    for k in range(modes):
        even = left_dot(lefts[2], far[k][0] * factor[0])
        odd = left_dot(lefts[3], far[k][1] * factor[1])
        plus, minus = even + odd, even - odd
        re = jnp.concatenate([plus[:half], minus[:half]], axis=0)
        im = jnp.concatenate([plus[half:], minus[half:]], axis=0)
        even = right_dot(jnp.concatenate([re[:, :half], im[:, :half]], axis=1), rights[2])
        odd = right_dot(jnp.concatenate([re[:, half:], im[:, half:]], axis=1), rights[3])
        plus, minus = even + odd, even - odd
        back_re = [plus[:, :half], minus[:, :half]]
        back_im = [plus[:, half:], minus[:, half:]]
        for t in range(2):
            pr, pi = probe_at(0, k, t), probe_at(1, k, t)
            u_re = pr * back_re[t] + pi * back_im[t]
            u_im = pr * back_im[t] - pi * back_re[t]
            update[0][t] = u_re if k == 0 else update[0][t] + u_re
            update[1][t] = u_im if k == 0 else update[1][t] + u_im
            lanes = pl.ds(t * LANES, LANES)
            xr, xi = patch[0][t], patch[1][t]
            sums[k, :, lanes] += xr * back_re[t] + xi * back_im[t]
            sums[modes + k, :, lanes] += xr * back_im[t] - xi * back_re[t]
    for t in range(2):
        lanes = pl.ds(t * LANES, LANES)
        sums[2 * modes, :, lanes] += patch[0][t] * patch[0][t] + patch[1][t] * patch[1][t]
    for c in range(2):
        add_window(acc, c, update[c], row, block, shift, edge)


def interior_kernel(margin, meta, tile, left, right, probe, amps, rights, lefts, ext, acc, sums, sems):
    tile_rows, tile_cols = tile.shape[1:]
    tiles = tile_cols // LANES
    edge = probe.shape[-1]
    modes = probe.shape[1]
    body = pl.ds(margin, tile_rows)
    pairs = [(left, ext.at[0, :, body, :]), (right, ext.at[tiles + 1, :, body, :])]
    for t in range(tiles):
        pairs.append((tile.at[:, :, pl.ds(t * LANES, LANES)], ext.at[1 + t, :, body, :]))
    copies = copy_all(pairs, sems)
    acc[...] = jnp.zeros_like(acc)
    sums[...] = jnp.zeros_like(sums)
    for copy in copies:
        copy.wait()

    def visit(slot, carry):
        row, col = meta[0, slot], meta[1, slot]
        block = col // LANES
        power = [
            sum(
                probe[c, k, :, pl.ds(t * LANES, LANES)] * probe[c, k, :, pl.ds(t * LANES, LANES)]
                for c in range(2)
                for k in range(modes)
            )
            for t in range(2)
        ]
        add_window(acc, 2, power, row, block, col - block * LANES, edge)

        @pl.when(jnp.logical_and(row >= margin, row + edge <= margin + tile_rows))
        def _():
            slot_body(slot, row, col, ext, acc, sums, probe, amps, rights, lefts)

        return carry

    lax.fori_loop(0, meta[2, 0], visit, 0)


def boundary_kernel(
    margin,
    meta,
    top,
    bottom,
    corner_left,
    corner_right,
    probe,
    amps,
    rights,
    lefts,
    ext_in,
    acc_in,
    sums_in,
    ext,
    acc,
    west,
    east,
    keep,
    send,
    sums,
    sems,
):
    tiles = acc.shape[0] - 2
    tile_rows = acc.shape[2] - 2 * margin
    edge = probe.shape[-1]
    above, below = pl.ds(0, margin), pl.ds(margin + tile_rows, margin)
    pairs = []
    for t in range(tiles):
        cols = pl.ds(t * LANES, LANES)
        pairs.append((top.at[:, :, cols], ext.at[1 + t, :, above, :]))
        pairs.append((bottom.at[:, :, cols], ext.at[1 + t, :, below, :]))
    for side, corner in ((0, corner_left), (tiles + 1, corner_right)):
        pairs.append((corner.at[0], ext.at[side, :, above, :]))
        pairs.append((corner.at[1], ext.at[side, :, below, :]))
    copies = copy_all(pairs, sems)
    sums[...] = sums_in[...]
    for copy in copies:
        copy.wait()

    def visit(slot, carry):
        row, col = meta[0, slot], meta[1, slot]

        @pl.when(jnp.logical_or(row < margin, row + edge > margin + tile_rows))
        def _():
            slot_body(slot, row, col, ext, acc, sums, probe, amps, rights, lefts)

        return carry

    lax.fori_loop(0, meta[2, 0], visit, 0)
    west[...] = acc[0]
    east[...] = acc[tiles + 1]
    rows = keep.shape[1]
    index = meta[2, 1]
    keep[...] = sums[:, aligned(index * rows, rows), :]
    send[...] = sums[:, aligned((1 - index) * rows, rows), :]


def run_interior(meta, tile, left, right, probe, amps, tables, margin):
    tile_rows, tile_cols = tile.shape[1:]
    edge = probe.shape[-1]
    modes = probe.shape[1]
    blocks, rows = tile_cols // LANES + 2, tile_rows + 2 * margin
    return pl.pallas_call(
        functools.partial(interior_kernel, margin),
        out_shape=[
            shape(blocks, 2, rows, LANES),
            shape(blocks, 3, rows, LANES),
            shape(2 * modes + 1, edge, edge),
        ],
        in_specs=[IN_SMEM, ANYWHERE, ANYWHERE, ANYWHERE] + [IN_VMEM] * 4,
        out_specs=[IN_VMEM] * 3,
        scratch_shapes=[pltpu.SemaphoreType.DMA((blocks,))],
        compiler_params=pltpu.CompilerParams(vmem_limit_bytes=KERNEL_VMEM),
        cost_estimate=pl.CostEstimate(flops=int(1e10), bytes_accessed=20_000_000, transcendentals=0),
        name="slots_interior",
    )(meta, tile, left, right, probe, amps, tables[0], tables[1])


KERNEL_VMEM = 10 * MIB


def run_boundary(meta, top, bottom, corner_left, corner_right, probe, amps, tables, ext, acc, sums, margin):
    edge = probe.shape[-1]
    modes = probe.shape[1]
    part = shape(2 * modes + 1, edge // 2, edge)
    return pl.pallas_call(
        functools.partial(boundary_kernel, margin),
        out_shape=[
            shape(*ext.shape),
            shape(*acc.shape),
            shape(*acc.shape[1:]),
            shape(*acc.shape[1:]),
            part,
            part,
        ],
        in_specs=[IN_SMEM] + [ANYWHERE] * 4 + [IN_VMEM] * 7,
        out_specs=[IN_VMEM] * 6,
        scratch_shapes=[VMEM(sums.shape, F32), pltpu.SemaphoreType.DMA((2 * ext.shape[0],))],
        input_output_aliases={9: 0, 10: 1},
        compiler_params=pltpu.CompilerParams(vmem_limit_bytes=KERNEL_VMEM),
        cost_estimate=pl.CostEstimate(flops=int(1e10), bytes_accessed=20_000_000, transcendentals=0),
        name="slots_boundary",
    )(meta, top, bottom, corner_left, corner_right, probe, amps, tables[0], tables[1], ext, acc, sums)


def small_call(kernel, outs, in_specs, limit=4 * MIB, scratch=(), out_specs=None):
    return pl.pallas_call(
        kernel,
        out_shape=outs,
        in_specs=in_specs,
        out_specs=out_specs if out_specs is not None else [IN_VMEM] * len(outs),
        scratch_shapes=list(scratch),
        compiler_params=pltpu.CompilerParams(vmem_limit_bytes=limit),
    )


def fold_kernel(margin, acc, from_west, from_east, above, below):
    tiles = acc.shape[0] - 2
    rows = acc.shape[2]
    for out, part in ((above, pl.ds(0, margin)), (below, pl.ds(rows - margin, margin))):
        for t in range(tiles):
            value = acc[1 + t, :, part, :]
            if t == 0:
                value = value + from_west[:, part, :]
            if t == tiles - 1:
                value = value + from_east[:, part, :]
            out[t] = value


def object_kernel(margin, ext, acc, from_west, from_east, from_above, from_below, out, stage, sems):
    tiles = acc.shape[0] - 2
    tile_rows = acc.shape[2] - 2 * margin
    copies = []
    for t in range(tiles):
        for start in range(0, tile_rows, margin):
            rows = pl.ds(margin + start, margin)
            total = acc[1 + t, :, rows, :]
            if t == 0:
                total = total + from_west[:, rows, :]
            if t == tiles - 1:
                total = total + from_east[:, rows, :]
            if start == 0:
                total = total + from_above[t]
            if start == tile_rows - margin:
                total = total + from_below[t]
            scale = 1.0 / (total[2] + 1.0)
            for c in range(2):
                stage[t, c, pl.ds(start, margin), :] = ext[1 + t, c, rows, :] + total[c] * scale
        copy = pltpu.make_async_copy(stage.at[t], out.at[:, :, pl.ds(t * LANES, LANES)], sems.at[t])
        copy.start()
        copies.append(copy)
    for copy in copies:
        copy.wait()


def combine_kernel(inputs, stage, meta, *refs):
    ins, outs = refs[:inputs], refs[inputs:]
    index = meta[0, stage]
    rows = outs[0].shape[1]
    for member, out in enumerate(outs):
        part = aligned(jnp.bitwise_xor(index, member) * rows, rows)
        if len(outs) == 1:
            part = slice(None)
        value = ins[0][:, part, :]
        for other in ins[1:]:
            value = value + other[:, part, :]
        out[...] = value


def combine(places, stage, parts, group):
    planes, rows, cols = parts[0].shape
    if (rows // group) % 8:
        total = sum(parts[1:], parts[0])
        if group == 1:
            return [total]
        rows = rows // group
        return [
            lax.dynamic_slice_in_dim(total, jnp.bitwise_xor(places[0, stage], m) * rows, rows, axis=1)
            for m in range(group)
        ]
    return small_call(
        functools.partial(combine_kernel, len(parts), stage),
        [shape(planes, rows // group, cols)] * group,
        [IN_SMEM] + [IN_VMEM] * len(parts),
    )(places, *parts)


def place_kernel(group, stage, meta, *refs):
    ins, out = refs[:group], refs[group]
    index = meta[0, stage]
    rows = ins[0].shape[1]
    for member, piece in enumerate(ins):
        out[:, aligned(jnp.bitwise_xor(index, member) * rows, rows), :] = piece[...]


def place(places, stage, parts):
    planes, rows, cols = parts[0].shape
    if rows % 8:
        whole = jnp.zeros((planes, rows * len(parts), cols), F32)
        for m, piece in enumerate(parts):
            at = jnp.bitwise_xor(places[0, stage], m) * rows
            whole = lax.dynamic_update_slice_in_dim(whole, piece, at, axis=1)
        return whole
    return small_call(
        functools.partial(place_kernel, len(parts), stage),
        [shape(planes, rows * len(parts), cols)],
        [IN_SMEM] + [IN_VMEM] * len(parts),
    )(places, *parts)[0]


def finish_kernel(inputs, meta, probe, *refs):
    ins, out = refs[:inputs], refs[inputs]
    total = ins[0][...]
    for other in ins[1:]:
        total = total + other[...]
    planes, rows = out.shape[:2]
    old = probe[:, aligned(meta[1, 0], rows), :]
    out[...] = old + total[:planes] / (total[planes:] + 1.0)


def finish(places, probe, parts):
    planes, rows, cols = parts[0].shape
    if rows % 8:
        total = sum(parts[1:], parts[0])
        old = lax.dynamic_slice_in_dim(probe, places[1, 0], rows, axis=1)
        return old + total[:-1] / (total[-1:] + 1.0)
    return small_call(
        functools.partial(finish_kernel, len(parts)),
        [shape(planes - 1, rows, cols)],
        [IN_SMEM] + [IN_VMEM] * (1 + len(parts)),
    )(places, probe, *parts)[0]


def shift_both(low, high, axis):
    count = lax.axis_size(axis)
    up = [(i, i + 1) for i in range(count - 1)]
    down = [(i + 1, i) for i in range(count - 1)]
    from_low = lax.ppermute(high, axis, up)
    from_high = lax.ppermute(low, axis, down)
    return from_low, from_high


def member_perm(axis, bits, member):
    mask = sum(((member >> position) & 1) << bit for position, bit in enumerate(bits))
    return [(i, i ^ mask) for i in range(lax.axis_size(axis))]


def member_index(axis, bits):
    where = lax.axis_index(axis)
    return sum(((where >> bit) & 1) << position for position, bit in enumerate(bits))


def stages_of(rows, cols):
    stages = [("col", (bit,)) for bit in range(cols.bit_length() - 1)]
    bits = list(range(1, rows.bit_length() - 1))
    if len(bits) > 1:
        stages.append(("row", (bits[0], bits[1])))
        bits = bits[2:]
    stages += [("row", (bit,)) for bit in bits]
    return stages, ("row", (0,))


def step(object_field, probe_modes, scan_offsets, scan_counts, amplitudes):
    tile_rows, tile_cols = object_field.shape[1:]
    modes = probe_modes.shape[1]
    edge = probe_modes.shape[-1]
    margin = edge // 2
    slots = amplitudes.shape[2]
    stages, last = stages_of(lax.axis_size("row"), lax.axis_size("col"))

    top, bottom, left, right = pack_edges(object_field, margin)
    above, below = shift_both(top, bottom, "row")
    west, east = shift_both(left, right, "col")

    anchor = [
        lax.axis_index("row") * tile_rows - margin,
        lax.axis_index("col") * tile_cols - margin,
    ]
    indices = [member_index(axis, bits) for axis, bits in stages]
    offsets = scan_offsets[0, 0]
    row_of = offsets[0] - anchor[0]
    col_of = offsets[1] - anchor[1]
    counts = jnp.stack([scan_counts[0, 0], indices[0]] + [jnp.int32(0)] * (slots - 2))
    meta = jnp.stack([row_of, col_of, counts]).astype(jnp.int32)
    start, rows = jnp.int32(0), edge
    for index, (axis, bits) in zip(indices, stages):
        rows = rows >> len(bits)
        start = start + index * rows
    places = jnp.stack(
        [jnp.stack(indices), jnp.stack([start] + [jnp.int32(0)] * (len(stages) - 1))]
    ).astype(jnp.int32)

    tables = tuple(jnp.asarray(t) for t in dft_tables(edge))
    order = np.concatenate([np.arange(0, edge, 2), np.arange(1, edge, 2)])
    select = jnp.asarray(np.eye(edge)[order].astype(BF16))
    amps = jnp.einsum("ui,sij->suj", select, amplitudes[0, 0], preferred_element_type=BF16)
    amps = jnp.einsum("suj,vj->suv", amps, select, preferred_element_type=BF16)

    ext, acc, sums = run_interior(meta, object_field, west, east, probe_modes, amps, tables, margin)

    corners = jnp.stack([above, below])
    corner_west, corner_east = shift_both(
        corners[..., :margin], corners[..., tile_cols - margin :], "col"
    )

    ext, acc, fold_west, fold_east, keep, send = run_boundary(
        meta, above, below, corner_west, corner_east, probe_modes, amps, tables, ext, acc, sums, margin
    )

    parts = [keep]
    for number, (axis, bits) in enumerate(stages):
        if number:
            parts = combine(places, number, parts, 1 << len(bits))
            mine, pieces = parts[0], parts[1:]
        else:
            mine, pieces = keep, [send]
        parts = [mine] + [
            lax.ppermute(piece, axis, member_perm(axis, bits, member + 1))
            for member, piece in enumerate(pieces)
        ]
    total = combine(places, 0, parts, 1)[0] if len(parts) > 1 else parts[0]
    parts = [total, lax.ppermute(total, last[0], member_perm(*last, 1))]
    flat = probe_modes.reshape(2 * modes, edge, edge)
    shard = finish(places, flat, parts)
    for number, (axis, bits) in reversed(list(enumerate(stages))):
        pieces = [shard] + [
            lax.ppermute(shard, axis, member_perm(axis, bits, member))
            for member in range(1, 1 << len(bits))
        ]
        shard = place(places, number, pieces)
    probe_new = shard.reshape(probe_modes.shape)

    from_west, from_east = shift_both(fold_west, fold_east, "col")
    strip = shape(tile_cols // LANES, 3, margin, LANES)
    out_above, out_below = small_call(
        functools.partial(fold_kernel, margin), [strip, strip], [IN_VMEM] * 3
    )(acc, from_west, from_east)
    from_above, from_below = shift_both(out_above, out_below, "row")
    object_new = small_call(
        functools.partial(object_kernel, margin),
        [shape(2, tile_rows, tile_cols)],
        [IN_VMEM] * 6,
        limit=8 * MIB,
        scratch=(
            VMEM((tile_cols // LANES, 2, tile_rows, LANES), F32),
            pltpu.SemaphoreType.DMA((tile_cols // LANES,)),
        ),
        out_specs=[ANYWHERE],
    )(ext, acc, from_west, from_east, from_above, from_below)[0]
    return object_new, probe_new


def solution(mesh):
    in_specs = (
        P(None, "row", "col"),
        P(),
        P("row", "col", None, None),
        P("row", "col"),
        P("row", "col", None, None, None),
    )
    out_specs = (P(None, "row", "col"), P())
    return jax.shard_map(step, mesh=mesh, in_specs=in_specs, out_specs=out_specs, check_vma=False)
```

```python
import functools
import math

import jax
import jax.numpy as jnp
import numpy as np
from jax import lax
from jax.experimental import pallas as pl
from jax.experimental.pallas import tpu as pltpu
from jax.sharding import PartitionSpec as P


F32 = jnp.float32
BF16 = jnp.bfloat16
LANES = 128


def split_host(table):
    high = table.astype(BF16)
    low = (table - high.astype(np.float64)).astype(BF16)
    return high, low


def dft_tables(edge):
    half = edge // 2
    scale = 1.0 / math.sqrt(edge)
    n = np.arange(half)[:, None]
    k = np.arange(half)[None, :]
    right, left = [], []
    for parity in (0, 1):
        angle = (n * (2 * k + parity) % edge) * (2.0 * np.pi / edge)
        cosine, sine = np.cos(angle) * scale, np.sin(angle) * scale
        w = np.block([[cosine, -sine], [sine, cosine]])
        right.append(w)
        left.append(w.T)
    mats = [right[0], right[1], left[0], left[1]]
    as_right = []
    as_left = []
    for m in mats:
        high, low = split_host(m)
        as_right.append(np.concatenate([high, high, low], axis=0))
        as_left.append(np.concatenate([high, high, low], axis=1))
    return (
        np.stack([as_right[0], as_right[1], as_right[2], as_right[3]]),
        np.stack([as_left[2], as_left[3], as_left[0], as_left[1]]),
    )


def split_parts(x):
    high = x.astype(BF16)
    low = (x - high.astype(F32)).astype(BF16)
    return high, low


def right_dot(x, table):
    high, low = split_parts(x)
    return jnp.dot(jnp.concatenate([high, low, high], axis=1), table, preferred_element_type=F32)


def left_dot(table, x):
    high, low = split_parts(x)
    return jnp.dot(table, jnp.concatenate([high, low, high], axis=0), preferred_element_type=F32)


VMEM = pltpu.VMEM
ANYWHERE = pl.BlockSpec(memory_space=pl.ANY)
IN_VMEM = pl.BlockSpec(memory_space=pltpu.VMEM)
IN_SMEM = pl.BlockSpec(memory_space=pltpu.SMEM)
MIB = 1024 * 1024
IN_HBM = pl.BlockSpec(memory_space=pltpu.HBM)


def in_hbm(x):
    return pltpu.with_memory_space_constraint(x, pltpu.HBM)


def shape(*dims):
    return jax.ShapeDtypeStruct(dims, F32)


def aligned(start, size):
    return pl.ds(pl.multiple_of(start, size) if size % 8 == 0 else start, size)


def copy_all(pairs, sems):
    copies = []
    for number, (src, dst) in enumerate(pairs):
        copy = pltpu.make_async_copy(src, dst, sems.at[number])
        copy.start()
        copies.append(copy)
    return copies


class Frame:
    def __init__(self, tile_rows, tile_cols, margin, sides):
        self.tile_rows, self.tile_cols, self.margin, self.sides = tile_rows, tile_cols, margin, sides
        self.tiles = tile_cols // LANES
        self.row = lax.axis_index("row")
        self.col = lax.axis_index("col")
        self.body = pl.ds(margin, tile_rows)

    def side_is_east(self, number):
        if self.sides == 2:
            return jnp.int32(number)
        return 1 - (self.col & 1)

    def side_block(self, number):
        return self.side_is_east(number) * (self.tiles + 1)

    def side_target(self, number):
        return 1 + self.side_is_east(number) * (self.tiles - 1)

    def side_cols(self, number):
        start = self.side_is_east(number) * (self.tile_cols - self.margin)
        return pl.ds(pl.multiple_of(start, LANES), self.margin)

    def is_below(self, number):
        return jnp.bitwise_xor(1 - (self.row & 1), number)

    def strip_rows(self, number):
        start = self.is_below(number) * (self.tile_rows - self.margin)
        return pl.ds(pl.multiple_of(start, self.margin), self.margin)

    def halo_rows(self, number):
        start = self.is_below(number) * (self.tile_rows + self.margin)
        return pl.ds(pl.multiple_of(start, self.margin), self.margin)

    def place_of(self, offsets, slot):
        return (
            offsets[0, 0, 0, slot] - self.row * self.tile_rows + self.margin,
            offsets[0, 0, 1, slot] - self.col * self.tile_cols + self.margin,
        )


def small_call(kernel, outs, in_specs, limit=4 * MIB, scratch=(), out_specs=None, aliases=None, cost=None):
    return pl.pallas_call(
        kernel,
        out_shape=outs,
        in_specs=in_specs,
        out_specs=out_specs if out_specs is not None else [IN_VMEM] * len(outs),
        scratch_shapes=list(scratch),
        input_output_aliases=aliases or {},
        compiler_params=pltpu.CompilerParams(vmem_limit_bytes=limit),
        cost_estimate=pl.CostEstimate(flops=cost, bytes_accessed=1_000_000, transcendentals=0) if cost else None,
    )


def pack_kernel(geometry, tile, straight, diagonal, *refs):
    sides, sems = refs[:-1], refs[-1]
    frame = Frame(*geometry)
    pairs = [
        (tile.at[:, frame.strip_rows(0), :], straight),
        (tile.at[:, frame.strip_rows(1), :], diagonal),
    ]
    for number, side in enumerate(sides):
        pairs.append((tile.at[:, :, frame.side_cols(number)], side))
    for copy in copy_all(pairs, sems):
        copy.wait()


def add_window(acc, channel, parts, row, block, shift):
    edge = parts[0].shape[0]
    lane = lax.broadcasted_iota(jnp.int32, (edge, LANES), 1)
    keep = lane >= shift
    first = pltpu.roll(parts[0], shift, 1)
    second = pltpu.roll(parts[1], shift, 1)
    rows = pl.ds(row, edge)
    zero = jnp.zeros_like(first)
    last = jnp.minimum(block + 2, acc.shape[0] - 1)
    acc[block, channel, rows, :] += jnp.where(keep, first, zero)
    acc[block + 1, channel, rows, :] += jnp.where(keep, second, first)
    acc[last, channel, rows, :] += jnp.where(keep, zero, second)


def slot_body(slot, row, col, ext, acc, sums, probe, amps, rights, lefts):
    edge = probe.shape[-1]
    modes = probe.shape[1]
    half = edge // 2
    block = col // LANES
    shift = col - block * LANES
    lane = lax.broadcasted_iota(jnp.int32, (edge, LANES), 1)
    back_shift = lax.rem(LANES - shift, LANES)
    keep = lane < LANES - shift
    last = jnp.minimum(block + 2, ext.shape[0] - 1)
    patch = []
    for c in range(2):
        rolled = [
            pltpu.roll(ext[b, c, pl.ds(row, edge), :], back_shift, 1) for b in (block, block + 1, last)
        ]
        patch.append([jnp.where(keep, rolled[t], rolled[t + 1]) for t in range(2)])

    def probe_at(c, k, t):
        return probe[c, k, :, pl.ds(t * LANES, LANES)]

    evens, odds = [], []
    for k in range(modes):
        re = [probe_at(0, k, t) * patch[0][t] - probe_at(1, k, t) * patch[1][t] for t in range(2)]
        im = [probe_at(0, k, t) * patch[1][t] + probe_at(1, k, t) * patch[0][t] for t in range(2)]
        evens.append(right_dot(jnp.concatenate([re[0] + re[1], im[0] + im[1]], axis=1), rights[0]))
        odds.append(right_dot(jnp.concatenate([re[0] - re[1], im[0] - im[1]], axis=1), rights[1]))
    far = []
    for k in range(modes):
        re = jnp.concatenate([evens[k][:, :half], odds[k][:, :half]], axis=1)
        im = jnp.concatenate([evens[k][:, half:], odds[k][:, half:]], axis=1)
        plus = jnp.concatenate([re[:half] + re[half:], im[:half] + im[half:]], axis=0)
        minus = jnp.concatenate([re[:half] - re[half:], im[:half] - im[half:]], axis=0)
        far.append([left_dot(lefts[0], plus), left_dot(lefts[1], minus)])
    factor = []
    for p in range(2):
        total = sum(
            far[k][p][:half] * far[k][p][:half] + far[k][p][half:] * far[k][p][half:]
            for k in range(modes)
        )
        amp = amps[slot, pl.ds(p * half, half), :].astype(F32)
        one = amp / jnp.sqrt(jnp.maximum(total, 0.25)) - 1.0
        factor.append(jnp.concatenate([one, one], axis=0))
    update = [[None, None], [None, None]]
    for k in range(modes):
        even = left_dot(lefts[2], far[k][0] * factor[0])
        odd = left_dot(lefts[3], far[k][1] * factor[1])
        plus, minus = even + odd, even - odd
        re = jnp.concatenate([plus[:half], minus[:half]], axis=0)
        im = jnp.concatenate([plus[half:], minus[half:]], axis=0)
        even = right_dot(jnp.concatenate([re[:, :half], im[:, :half]], axis=1), rights[2])
        odd = right_dot(jnp.concatenate([re[:, half:], im[:, half:]], axis=1), rights[3])
        plus, minus = even + odd, even - odd
        back_re = [plus[:, :half], minus[:, :half]]
        back_im = [plus[:, half:], minus[:, half:]]
        for t in range(2):
            pr, pi = probe_at(0, k, t), probe_at(1, k, t)
            u_re = pr * back_re[t] + pi * back_im[t]
            u_im = pr * back_im[t] - pi * back_re[t]
            update[0][t] = u_re if k == 0 else update[0][t] + u_re
            update[1][t] = u_im if k == 0 else update[1][t] + u_im
            lanes = pl.ds(t * LANES, LANES)
            xr, xi = patch[0][t], patch[1][t]
            sums[k, :, lanes] += xr * back_re[t] + xi * back_im[t]
            sums[modes + k, :, lanes] += xr * back_im[t] - xi * back_re[t]
    for t in range(2):
        lanes = pl.ds(t * LANES, LANES)
        sums[2 * modes, :, lanes] += patch[0][t] * patch[0][t] + patch[1][t] * patch[1][t]
    for c in range(2):
        add_window(acc, c, update[c], row, block, shift)


def interior_kernel(geometry, offsets, counts, tile, probe_in, amps_in, rights_in, lefts_in, *refs):
    frame = Frame(*geometry)
    halos = refs[: frame.sides]
    ext, acc, sums, probe, amps, rights, lefts, raw, sems = refs[frame.sides :]
    tiles, body, margin = frame.tiles, frame.body, frame.margin
    edge = probe.shape[-1]
    pairs = [(amps_in.at[0, 0], raw), (probe_in, probe), (rights_in, rights), (lefts_in, lefts)]
    for number, halo in enumerate(halos):
        pairs.append((halo, ext.at[frame.side_block(number), :, body, :]))
    for t in range(tiles):
        pairs.append((tile.at[:, :, pl.ds(t * LANES, LANES)], ext.at[1 + t, :, body, :]))
    copies = copy_all(pairs, sems)
    acc[...] = jnp.zeros_like(acc)
    sums[...] = jnp.zeros_like(sums)
    copies[0].wait()
    out_at = lax.broadcasted_iota(jnp.int32, (edge, edge), 0)
    in_at = lax.broadcasted_iota(jnp.int32, (edge, edge), 1)
    source = jnp.where(out_at < edge // 2, 2 * out_at, 2 * out_at - edge + 1)
    pick = jnp.where(in_at == source, 1.0, 0.0).astype(BF16)

    def reorder(slot, carry):
        half_way = jnp.dot(pick, raw[slot], preferred_element_type=F32).astype(BF16)
        amps[slot] = lax.dot_general(
            half_way, pick, (((1,), (1,)), ((), ())), preferred_element_type=F32
        ).astype(BF16)
        return carry

    lax.fori_loop(0, counts[0, 0], reorder, 0)
    for copy in copies[1:]:
        copy.wait()

    def visit(slot, carry):
        row, col = frame.place_of(offsets, slot)

        @pl.when(jnp.logical_and(row >= margin, row + edge <= margin + frame.tile_rows))
        def _():
            slot_body(slot, row, col, ext, acc, sums, probe, amps, rights, lefts)

        return carry

    lax.fori_loop(0, counts[0, 0], visit, 0)


def boundary_kernel(geometry, offsets, counts, straight, diagonal, *refs):
    frame = Frame(*geometry)
    sides = frame.sides
    corners, refs = refs[:sides], refs[sides:]
    probe, amps, rights, lefts = refs[:4]
    ext, acc, sums, mid, over_straight, over_diagonal = refs[7:13]
    side_outs, refs = refs[13 : 13 + sides], refs[13 + sides :]
    keep, send, sems = refs
    tiles, margin, body = frame.tiles, frame.margin, frame.body
    edge = probe.shape[-1]
    pairs = []
    for number, halo in enumerate((straight, diagonal)):
        for t in range(tiles):
            pairs.append(
                (halo.at[:, :, pl.ds(t * LANES, LANES)], ext.at[1 + t, :, frame.halo_rows(number), :])
            )
        for side, corner in enumerate(corners):
            pairs.append(
                (corner.at[number], ext.at[frame.side_block(side), :, frame.halo_rows(number), :])
            )
    for copy in copy_all(pairs, sems):
        copy.wait()

    def visit(slot, carry):
        row, col = frame.place_of(offsets, slot)

        @pl.when(jnp.logical_or(row < margin, row + edge > margin + frame.tile_rows))
        def _():
            slot_body(slot, row, col, ext, acc, sums, probe, amps, rights, lefts)

        return carry

    lax.fori_loop(0, counts[0, 0], visit, 0)
    out = [(acc.at[1 + t, :, body, :], mid.at[t]) for t in range(tiles)]
    copies = copy_all(out, sems)
    rows = keep.shape[1]
    index = frame.col & 1
    keep[...] = sums[:, aligned(index * rows, rows), :]
    send[...] = sums[:, aligned((1 - index) * rows, rows), :]
    for side, side_out in enumerate(side_outs):
        side_out[...] = acc[frame.side_block(side)]
    for number, over in enumerate((over_straight, over_diagonal)):
        for t in range(tiles):
            over[t] = acc[1 + t, :, frame.halo_rows(number), :]
    for copy in copies:
        copy.wait()


def corner_kernel(geometry, straight, diagonal, *outs):
    frame = Frame(*geometry)
    for side, out in enumerate(outs):
        out[0] = straight[:, :, frame.side_cols(side)]
        out[1] = diagonal[:, :, frame.side_cols(side)]


KERNEL_VMEM = 12 * MIB
SLOT_COST = dict(
    cost_estimate=pl.CostEstimate(flops=int(1e10), bytes_accessed=20_000_000, transcendentals=0),
)


def run_interior(geometry, offsets, counts, tile, probe, amps, tables, halos):
    tile_rows, tile_cols, margin, sides = geometry
    edge = probe.shape[-1]
    modes = probe.shape[1]
    window = shape(tile_cols // LANES + 2, 2, tile_rows + 2 * margin, LANES)
    amp_shape = jax.ShapeDtypeStruct(amps.shape[2:], BF16)
    outs = [window, window, shape(2 * modes + 1, edge, edge), shape(*probe.shape), amp_shape]
    outs += [jax.ShapeDtypeStruct(t.shape, t.dtype) for t in tables]
    return pl.pallas_call(
        functools.partial(interior_kernel, geometry),
        out_shape=outs,
        in_specs=[IN_SMEM] * 2 + [IN_HBM] * 5 + [ANYWHERE] * sides,
        out_specs=[IN_VMEM] * len(outs),
        scratch_shapes=[VMEM(amp_shape.shape, BF16), pltpu.SemaphoreType.DMA((16,))],
        compiler_params=pltpu.CompilerParams(vmem_limit_bytes=KERNEL_VMEM),
        name="slots_interior",
        **SLOT_COST,
    )(offsets, counts, tile, probe, amps, *tables, *halos)


def run_boundary(geometry, offsets, counts, straight, diagonal, corners, consts, ext, acc, sums):
    tile_rows, tile_cols, margin, sides = geometry
    planes, edge = sums.shape[:2]
    tiles = tile_cols // LANES
    part = shape(planes, edge // 2, edge)
    strip = shape(tiles, 2, margin, LANES)
    outs = [shape(*ext.shape), shape(*acc.shape), shape(*sums.shape)]
    outs += [shape(tiles, 2, tile_rows, LANES), strip, strip]
    outs += [shape(*acc.shape[1:])] * sides + [part, part]
    base = 4 + sides + 4
    return pl.pallas_call(
        functools.partial(boundary_kernel, geometry),
        out_shape=outs,
        in_specs=[IN_SMEM] * 2 + [ANYWHERE] * (2 + sides) + [IN_VMEM] * 7,
        out_specs=[IN_VMEM] * 3 + [IN_HBM] + [IN_VMEM] * (len(outs) - 4),
        scratch_shapes=[pltpu.SemaphoreType.DMA((16,))],
        input_output_aliases={base: 0, base + 1: 1, base + 2: 2},
        compiler_params=pltpu.CompilerParams(vmem_limit_bytes=KERNEL_VMEM),
        name="slots_boundary",
        **SLOT_COST,
    )(offsets, counts, straight, diagonal, *corners, *consts, ext, acc, sums)


def fold_kernel(geometry, over_straight, over_diagonal, *refs):
    frame = Frame(*geometry)
    received, outs = refs[: frame.sides], refs[frame.sides : frame.sides + 2]
    for number, (over, out) in enumerate(((over_straight, outs[0]), (over_diagonal, outs[1]))):
        out[...] = over[...]
        for side, value in enumerate(received):
            out[frame.side_target(side) - 1] += value[:, frame.halo_rows(number), :]


def light_kernel(geometry, own, *refs):
    frame = Frame(*geometry)
    others, (probe, out, canvas) = refs[:-3], refs[-3:]
    tiles = frame.tiles
    edge = probe.shape[-1]
    modes = probe.shape[1]
    canvas[...] = jnp.zeros_like(canvas)
    power = [
        sum(
            probe[c, k, :, pl.ds(t * LANES, LANES)] * probe[c, k, :, pl.ds(t * LANES, LANES)]
            for c in range(2)
            for k in range(modes)
        )
        for t in range(2)
    ]

    def add_from(read):
        def visit(slot, carry):
            row = read(0, slot) - frame.row * frame.tile_rows + edge
            col = read(1, slot) - frame.col * frame.tile_cols + edge
            meets = (row > 0) & (row < frame.tile_rows + edge) & (col > 0) & (col < frame.tile_cols + edge)

            @pl.when(meets)
            def _():
                block = col // LANES
                add_window(canvas, 0, power, row, block, col - block * LANES)

            return carry

        lax.fori_loop(0, read(2, 0), visit, 0)

    add_from(lambda plane, slot: own[plane, slot])
    for other in others:
        if len(other.shape) == 2:
            add_from(lambda plane, slot, other=other: other[plane, slot])
        else:
            for tile in range(other.shape[0]):
                add_from(lambda plane, slot, other=other, tile=tile: other[tile, plane, slot])
    for t in range(tiles):
        out[t] = canvas[edge // LANES + t, 0, pl.ds(edge, frame.tile_rows), :]


def object_kernel(geometry, tile, mid, light, from_straight, from_diagonal, *refs):
    frame = Frame(*geometry)
    received, (out, old, stage, sems_in, sems_out) = refs[: frame.sides], refs[frame.sides :]
    tiles = frame.tiles
    loads = []
    for t in range(tiles):
        loads.append(
            (
                pltpu.make_async_copy(
                    tile.at[:, :, pl.ds(t * LANES, LANES)], old.at[t], sems_in.at[2 * t]
                ),
                pltpu.make_async_copy(mid.at[t], stage.at[t], sems_in.at[2 * t + 1]),
            )
        )
        for copy in loads[-1]:
            copy.start()
    copies = []
    for t in range(tiles):
        for copy in loads[t]:
            copy.wait()
        for side, value in enumerate(received):

            @pl.when(frame.side_target(side) == 1 + t)
            def _(value=value, t=t):
                stage[t] += value[:, frame.body, :]

        for number, value in enumerate((from_straight, from_diagonal)):
            stage[t, :, frame.strip_rows(number), :] += value[t]
        scale = 1.0 / (light[t] + 1.0)
        for c in range(2):
            stage[t, c] = old[t, c] + stage[t, c] * scale
        copy = pltpu.make_async_copy(
            stage.at[t], out.at[:, :, pl.ds(t * LANES, LANES)], sems_out.at[t]
        )
        copy.start()
        copies.append(copy)
    for copy in copies:
        copy.wait()


def member_perm(axis, bits, member):
    mask = sum(((member >> position) & 1) << bit for position, bit in enumerate(bits))
    return [(i, i ^ mask) for i in range(lax.axis_size(axis))]


def member_index(axis, bits):
    where = lax.axis_index(axis)
    return sum(((where >> bit) & 1) << position for position, bit in enumerate(bits))


def combine_kernel(inputs, stage, *refs):
    ins, outs = refs[:inputs], refs[inputs:]
    rows = outs[0].shape[1]
    for member, out in enumerate(outs):
        part = slice(None)
        if len(outs) > 1:
            part = aligned(jnp.bitwise_xor(member_index(*stage), member) * rows, rows)
        value = ins[0][:, part, :]
        for other in ins[1:]:
            value = value + other[:, part, :]
        out[...] = value


def combine(stage, parts, group):
    planes, rows, cols = parts[0].shape
    if (rows // group) % 8:
        total = sum(parts[1:], parts[0])
        if group == 1:
            return [total]
        rows = rows // group
        return [
            lax.dynamic_slice_in_dim(
                total, jnp.bitwise_xor(member_index(*stage), m) * rows, rows, axis=1
            )
            for m in range(group)
        ]
    return small_call(
        functools.partial(combine_kernel, len(parts), stage),
        [shape(planes, rows // group, cols)] * group,
        [IN_VMEM] * len(parts),
    )(*parts)


def place_kernel(group, stage, *refs):
    ins, out = refs[:group], refs[group]
    rows = ins[0].shape[1]
    for member, piece in enumerate(ins):
        at = jnp.bitwise_xor(member_index(*stage), member) * rows
        out[:, aligned(at, rows), :] = piece[...]


def place(stage, parts):
    planes, rows, cols = parts[0].shape
    if rows % 8:
        whole = jnp.zeros((planes, rows * len(parts), cols), F32)
        for m, piece in enumerate(parts):
            at = jnp.bitwise_xor(member_index(*stage), m) * rows
            whole = lax.dynamic_update_slice_in_dim(whole, piece, at, axis=1)
        return whole
    return small_call(
        functools.partial(place_kernel, len(parts), stage),
        [shape(planes, rows * len(parts), cols)],
        [IN_VMEM] * len(parts),
    )(*parts)[0]


def shard_start(stages, edge):
    start, rows = jnp.int32(0), edge
    for axis, bits in stages:
        rows = rows >> len(bits)
        start = start + member_index(axis, bits) * rows
    return start


def finish_kernel(stages, edge, probe, *refs):
    ins, out = refs[:-1], refs[-1]
    total = ins[0][...]
    for other in ins[1:]:
        total = total + other[...]
    planes, rows = out.shape[:2]
    old = probe[:, aligned(shard_start(stages, edge), rows), :]
    out[...] = old + total[:planes] / (total[planes:] + 1.0)


def finish(stages, probe, parts):
    planes, rows, cols = parts[0].shape
    edge = probe.shape[1]
    if rows % 8:
        total = sum(parts[1:], parts[0])
        old = lax.dynamic_slice_in_dim(probe, shard_start(stages, edge), rows, axis=1)
        return old + total[:-1] / (total[-1:] + 1.0)
    return small_call(
        functools.partial(finish_kernel, stages, edge),
        [shape(planes - 1, rows, cols)],
        [IN_VMEM] * (1 + len(parts)),
    )(probe, *parts)[0]


def swap_sides(outs):
    count = lax.axis_size("col")
    if len(outs) == 1:
        return [lax.ppermute(outs[0], "col", [(0, 1), (1, 0)])]
    up = [(i, i + 1) for i in range(count - 1)]
    down = [(i + 1, i) for i in range(count - 1)]
    return [lax.ppermute(outs[1], "col", up), lax.ppermute(outs[0], "col", down)]


def swap_rows(value, number):
    count = lax.axis_size("row")
    pairs = []
    for low in range(number, count - 1, 2):
        pairs += [(low, low + 1), (low + 1, low)]
    return lax.ppermute(value, "row", pairs)


def stages_of(rows, cols):
    stages = [("col", (bit,)) for bit in range(cols.bit_length() - 1)]
    bits = list(range(1, rows.bit_length() - 1))
    if len(bits) > 1:
        stages.append(("row", (bits[0], bits[1])))
        bits = bits[2:]
    stages += [("row", (bit,)) for bit in bits]
    return tuple(stages), ("row", (0,))


def step(object_field, probe_modes, scan_offsets, scan_counts, amplitudes):
    tile_rows, tile_cols = object_field.shape[1:]
    modes = probe_modes.shape[1]
    edge = probe_modes.shape[-1]
    margin = edge // 2
    slots = amplitudes.shape[2]
    tiles = tile_cols // LANES
    sides = 1 if lax.axis_size("col") == 2 else 2
    geometry = (tile_rows, tile_cols, margin, sides)
    stages, last = stages_of(lax.axis_size("row"), lax.axis_size("col"))
    tables = tuple(in_hbm(jnp.asarray(t)) for t in dft_tables(edge))
    tile_hbm, probe_hbm, amps_hbm = in_hbm(object_field), in_hbm(probe_modes), in_hbm(amplitudes)

    straight, diagonal, *edges = small_call(
        functools.partial(pack_kernel, geometry),
        [shape(2, margin, tile_cols)] * 2 + [shape(2, tile_rows, margin)] * sides,
        [IN_HBM],
        limit=8 * MIB,
        scratch=(pltpu.SemaphoreType.DMA((4,)),),
    )(tile_hbm)
    straight = swap_rows(straight, 0)
    diagonal = swap_rows(diagonal, 1)
    halos = swap_sides(edges)

    own = jnp.concatenate(
        [scan_offsets[0, 0], jnp.broadcast_to(scan_counts[0], (1, slots))], axis=0
    )
    stacked = jnp.stack([own, swap_rows(own, 0), swap_rows(own, 1)])
    beside = swap_sides([stacked] * sides)

    ext, acc, sums, *consts = run_interior(
        geometry, scan_offsets, scan_counts, tile_hbm, probe_hbm, amps_hbm, tables, halos
    )

    cut = small_call(
        functools.partial(corner_kernel, geometry),
        [shape(2, 2, margin, margin)] * sides,
        [IN_VMEM] * 2,
    )(straight, diagonal)
    corners = swap_sides(cut)

    _, _, _, mid, *rest = run_boundary(
        geometry, scan_offsets, scan_counts, straight, diagonal, corners, consts, ext, acc, sums
    )
    overs, side_outs, (keep, send) = rest[:2], rest[2 : 2 + sides], rest[2 + sides :]

    parts = [keep]
    for number, stage in enumerate(stages):
        axis, bits = stage
        if number:
            mine, *pieces = combine(stage, parts, 1 << len(bits))
        else:
            mine, pieces = keep, [send]
        parts = [mine] + [
            lax.ppermute(piece, axis, member_perm(axis, bits, member + 1))
            for member, piece in enumerate(pieces)
        ]
    total = combine(last, parts, 1)[0]
    parts = [total, lax.ppermute(total, last[0], member_perm(*last, 1))]

    received = swap_sides(side_outs)
    strip = shape(tiles, 2, margin, LANES)
    out_straight, out_diagonal = small_call(
        functools.partial(fold_kernel, geometry), [strip, strip], [IN_VMEM] * (2 + sides)
    )(*overs, *received)
    from_straight = swap_rows(out_straight, 0)
    from_diagonal = swap_rows(out_diagonal, 1)

    flat = probe_modes.reshape(2 * modes, edge, edge)
    shard = finish(stages, flat, parts)
    for number, stage in reversed(list(enumerate(stages))):
        axis, bits = stage
        pieces = [shard] + [
            lax.ppermute(shard, axis, member_perm(axis, bits, member))
            for member in range(1, 1 << len(bits))
        ]
        shard = place(stage, pieces)
    probe_new = shard.reshape(probe_modes.shape)

    light = small_call(
        functools.partial(light_kernel, geometry),
        [shape(tiles, tile_rows, LANES)],
        [IN_SMEM] * (2 + sides) + [IN_VMEM],
        limit=8 * MIB,
        scratch=(VMEM((tiles + 2 * (edge // LANES), 1, tile_rows + 2 * edge, LANES), F32),),
        cost=10_000_000,
    )(own, stacked[1:], *beside, probe_modes)[0]
    object_new = small_call(
        functools.partial(object_kernel, geometry),
        [shape(2, tile_rows, tile_cols)],
        [IN_HBM, ANYWHERE] + [IN_VMEM] * (3 + sides),
        limit=8 * MIB,
        scratch=(
            VMEM((tiles, 2, tile_rows, LANES), F32),
            VMEM((tiles, 2, tile_rows, LANES), F32),
            pltpu.SemaphoreType.DMA((2 * tiles,)),
            pltpu.SemaphoreType.DMA((tiles,)),
        ),
        out_specs=[IN_HBM],
    )(object_field, mid, light, from_straight, from_diagonal, *received)[0]
    return object_new, probe_new


def solution(mesh):
    in_specs = (
        P(None, "row", "col"),
        P(),
        P("row", "col", None, None),
        P("row", "col"),
        P("row", "col", None, None, None),
    )
    out_specs = (P(None, "row", "col"), P())
    return jax.shard_map(step, mesh=mesh, in_specs=in_specs, out_specs=out_specs, check_vma=False)
```

```python
import functools
import math

import jax
import jax.numpy as jnp
import numpy as np
from jax import lax
from jax.experimental import pallas as pl
from jax.experimental.pallas import tpu as pltpu
from jax.sharding import PartitionSpec as P


F32 = jnp.float32
BF16 = jnp.bfloat16
LANES = 128


def split_host(table):
    high = table.astype(BF16)
    low = (table - high.astype(np.float64)).astype(BF16)
    return high, low


def dft_tables(edge):
    half = edge // 2
    scale = 1.0 / math.sqrt(edge)
    n = np.arange(half)[:, None]
    k = np.arange(half)[None, :]
    right, left = [], []
    for parity in (0, 1):
        angle = (n * (2 * k + parity) % edge) * (2.0 * np.pi / edge)
        cosine, sine = np.cos(angle) * scale, np.sin(angle) * scale
        w = np.block([[cosine, -sine], [sine, cosine]])
        right.append(w)
        left.append(w.T)
    mats = [right[0], right[1], left[0], left[1]]
    as_right = []
    as_left = []
    for m in mats:
        high, low = split_host(m)
        as_right.append(np.concatenate([high, high, low], axis=0))
        as_left.append(np.concatenate([high, high, low], axis=1))
    return (
        np.stack([as_right[0], as_right[1], as_right[2], as_right[3]]),
        np.stack([as_left[2], as_left[3], as_left[0], as_left[1]]),
    )


def split_parts(x):
    high = x.astype(BF16)
    low = (x - high.astype(F32)).astype(BF16)
    return high, low


def right_dot(x, table):
    high, low = split_parts(x)
    return jnp.dot(jnp.concatenate([high, low, high], axis=1), table, preferred_element_type=F32)


def left_dot(table, x):
    high, low = split_parts(x)
    return jnp.dot(table, jnp.concatenate([high, low, high], axis=0), preferred_element_type=F32)


VMEM = pltpu.VMEM
ANYWHERE = pl.BlockSpec(memory_space=pl.ANY)
IN_VMEM = pl.BlockSpec(memory_space=pltpu.VMEM)
IN_SMEM = pl.BlockSpec(memory_space=pltpu.SMEM)
MIB = 1024 * 1024
IN_HBM = pl.BlockSpec(memory_space=pltpu.HBM)


def in_hbm(x):
    return pltpu.with_memory_space_constraint(x, pltpu.HBM)


def shape(*dims):
    return jax.ShapeDtypeStruct(dims, F32)


def aligned(start, size):
    return pl.ds(pl.multiple_of(start, size) if size % 8 == 0 else start, size)


def copy_all(pairs, sems):
    copies = []
    for number, (src, dst) in enumerate(pairs):
        copy = pltpu.make_async_copy(src, dst, sems.at[number])
        copy.start()
        copies.append(copy)
    return copies


class Frame:
    def __init__(self, tile_rows, tile_cols, margin, sides):
        self.tile_rows, self.tile_cols, self.margin, self.sides = tile_rows, tile_cols, margin, sides
        self.tiles = tile_cols // LANES
        self.row = lax.axis_index("row")
        self.col = lax.axis_index("col")
        self.body = pl.ds(margin, tile_rows)

    def side_is_east(self, number):
        if self.sides == 2:
            return jnp.int32(number)
        return 1 - (self.col & 1)

    def side_block(self, number):
        return self.side_is_east(number) * (self.tiles + 1)

    def side_target(self, number):
        return 1 + self.side_is_east(number) * (self.tiles - 1)

    def side_cols(self, number):
        start = self.side_is_east(number) * (self.tile_cols - self.margin)
        return pl.ds(pl.multiple_of(start, LANES), self.margin)

    def is_below(self, number):
        return jnp.bitwise_xor(1 - (self.row & 1), number)

    def strip_rows(self, number):
        start = self.is_below(number) * (self.tile_rows - self.margin)
        return pl.ds(pl.multiple_of(start, self.margin), self.margin)

    def halo_rows(self, number):
        start = self.is_below(number) * (self.tile_rows + self.margin)
        return pl.ds(pl.multiple_of(start, self.margin), self.margin)

    def edge_tile(self, number):
        return self.side_is_east(number) * (self.tiles - 1)

    def place_of(self, offsets, slot):
        return (
            offsets[0, 0, 0, slot] - self.row * self.tile_rows + self.margin,
            offsets[0, 0, 1, slot] - self.col * self.tile_cols + self.margin,
        )


def small_call(kernel, outs, in_specs, limit=4 * MIB, scratch=(), out_specs=None, aliases=None, cost=None):
    return pl.pallas_call(
        kernel,
        out_shape=outs,
        in_specs=in_specs,
        out_specs=out_specs if out_specs is not None else [IN_VMEM] * len(outs),
        scratch_shapes=list(scratch),
        input_output_aliases=aliases or {},
        compiler_params=pltpu.CompilerParams(vmem_limit_bytes=limit),
        cost_estimate=pl.CostEstimate(flops=cost, bytes_accessed=1_000_000, transcendentals=0) if cost else None,
    )


WHERE = 8


def where_rows(offsets, counts):
    lane = lax.broadcasted_iota(jnp.int32, (1, LANES), 1)
    rows = []
    for axis in range(2):
        line = jnp.zeros((1, LANES), jnp.int32)
        for slot in range(offsets.shape[-1]):
            line = jnp.where(lane == slot, offsets[0, 0, axis, slot], line)
        rows.append(line)
    rows.append(jnp.zeros((1, LANES), jnp.int32) + counts[0, 0])
    return [row.astype(F32) for row in rows]


def pack_kernel(geometry, offsets, counts, tile, straight, diagonal, *refs):
    sides, sems = refs[:-1], refs[-1]
    frame = Frame(*geometry)
    margin = frame.margin
    pairs = []
    for number, strip in enumerate((straight, diagonal)):
        for t in range(frame.tiles):
            for c in range(2):
                pairs.append(
                    (
                        tile.at[c, frame.strip_rows(number), pl.ds(t * LANES, LANES)],
                        strip.at[pl.ds((2 * t + c) * margin, margin), :],
                    )
                )
    for number, side in enumerate(sides):
        pairs.append((tile.at[:, :, frame.side_cols(number)], side))
    copies = copy_all(pairs, sems)
    rows = where_rows(offsets, counts)
    for strip in (straight, diagonal):
        for number, row in enumerate(rows):
            strip[pl.ds(strip.shape[0] - WHERE + number, 1), :] = row
    for copy in copies:
        copy.wait()


def add_window(acc, channel, parts, row, block, shift):
    edge = parts[0].shape[0]
    lane = lax.broadcasted_iota(jnp.int32, (edge, LANES), 1)
    keep = lane >= shift
    first = pltpu.roll(parts[0], shift, 1)
    second = pltpu.roll(parts[1], shift, 1)
    rows = pl.ds(row, edge)
    zero = jnp.zeros_like(first)
    last = jnp.minimum(block + 2, acc.shape[0] - 1)
    acc[block, channel, rows, :] += jnp.where(keep, first, zero)
    acc[block + 1, channel, rows, :] += jnp.where(keep, second, first)
    acc[last, channel, rows, :] += jnp.where(keep, zero, second)


def slot_body(slot, row, col, ext, acc, sums, probe, amps, rights, lefts):
    edge = probe.shape[-1]
    modes = probe.shape[1]
    half = edge // 2
    block = col // LANES
    shift = col - block * LANES
    lane = lax.broadcasted_iota(jnp.int32, (edge, LANES), 1)
    back_shift = lax.rem(LANES - shift, LANES)
    keep = lane < LANES - shift
    last = jnp.minimum(block + 2, ext.shape[0] - 1)
    patch = []
    for c in range(2):
        rolled = [
            pltpu.roll(ext[b, c, pl.ds(row, edge), :], back_shift, 1) for b in (block, block + 1, last)
        ]
        patch.append([jnp.where(keep, rolled[t], rolled[t + 1]) for t in range(2)])

    def probe_at(c, k, t):
        return probe[c, k, :, pl.ds(t * LANES, LANES)]

    evens, odds = [], []
    for k in range(modes):
        re = [probe_at(0, k, t) * patch[0][t] - probe_at(1, k, t) * patch[1][t] for t in range(2)]
        im = [probe_at(0, k, t) * patch[1][t] + probe_at(1, k, t) * patch[0][t] for t in range(2)]
        evens.append(right_dot(jnp.concatenate([re[0] + re[1], im[0] + im[1]], axis=1), rights[0]))
        odds.append(right_dot(jnp.concatenate([re[0] - re[1], im[0] - im[1]], axis=1), rights[1]))
    far = []
    for k in range(modes):
        re = jnp.concatenate([evens[k][:, :half], odds[k][:, :half]], axis=1)
        im = jnp.concatenate([evens[k][:, half:], odds[k][:, half:]], axis=1)
        plus = jnp.concatenate([re[:half] + re[half:], im[:half] + im[half:]], axis=0)
        minus = jnp.concatenate([re[:half] - re[half:], im[:half] - im[half:]], axis=0)
        far.append([left_dot(lefts[0], plus), left_dot(lefts[1], minus)])
    factor = []
    for p in range(2):
        total = sum(
            far[k][p][:half] * far[k][p][:half] + far[k][p][half:] * far[k][p][half:]
            for k in range(modes)
        )
        amp = amps[slot, pl.ds(p * half, half), :].astype(F32)
        one = amp / jnp.sqrt(jnp.maximum(total, 0.25)) - 1.0
        factor.append(jnp.concatenate([one, one], axis=0))
    update = [[None, None], [None, None]]
    for k in range(modes):
        even = left_dot(lefts[2], far[k][0] * factor[0])
        odd = left_dot(lefts[3], far[k][1] * factor[1])
        plus, minus = even + odd, even - odd
        re = jnp.concatenate([plus[:half], minus[:half]], axis=0)
        im = jnp.concatenate([plus[half:], minus[half:]], axis=0)
        even = right_dot(jnp.concatenate([re[:, :half], im[:, :half]], axis=1), rights[2])
        odd = right_dot(jnp.concatenate([re[:, half:], im[:, half:]], axis=1), rights[3])
        plus, minus = even + odd, even - odd
        back_re = [plus[:, :half], minus[:, :half]]
        back_im = [plus[:, half:], minus[:, half:]]
        for t in range(2):
            pr, pi = probe_at(0, k, t), probe_at(1, k, t)
            u_re = pr * back_re[t] + pi * back_im[t]
            u_im = pr * back_im[t] - pi * back_re[t]
            update[0][t] = u_re if k == 0 else update[0][t] + u_re
            update[1][t] = u_im if k == 0 else update[1][t] + u_im
            lanes = pl.ds(t * LANES, LANES)
            xr, xi = patch[0][t], patch[1][t]
            sums[k, :, lanes] += xr * back_re[t] + xi * back_im[t]
            sums[modes + k, :, lanes] += xr * back_im[t] - xi * back_re[t]
    for t in range(2):
        lanes = pl.ds(t * LANES, LANES)
        sums[2 * modes, :, lanes] += patch[0][t] * patch[0][t] + patch[1][t] * patch[1][t]
    for c in range(2):
        add_window(acc, c, update[c], row, block, shift)


def interior_kernel(geometry, offsets, counts, tile, probe_in, amps_in, rights_in, lefts_in, *refs):
    frame = Frame(*geometry)
    halos = refs[: frame.sides]
    ext, acc, sums, probe, amps, rights, lefts, raw, sems = refs[frame.sides :]
    tiles, body, margin = frame.tiles, frame.body, frame.margin
    edge = probe.shape[-1]
    pairs = [(amps_in.at[0, 0], raw), (probe_in, probe), (rights_in, rights), (lefts_in, lefts)]
    for number, halo in enumerate(halos):
        pairs.append((halo, ext.at[frame.side_block(number), :, body, :]))
    for t in range(tiles):
        pairs.append((tile.at[:, :, pl.ds(t * LANES, LANES)], ext.at[1 + t, :, body, :]))
    copies = copy_all(pairs, sems)
    acc[...] = jnp.zeros_like(acc)
    sums[...] = jnp.zeros_like(sums)
    copies[0].wait()
    out_at = lax.broadcasted_iota(jnp.int32, (edge, edge), 0)
    in_at = lax.broadcasted_iota(jnp.int32, (edge, edge), 1)
    source = jnp.where(out_at < edge // 2, 2 * out_at, 2 * out_at - edge + 1)
    pick = jnp.where(in_at == source, 1.0, 0.0).astype(BF16)

    def reorder(slot, carry):
        half_way = jnp.dot(pick, raw[slot], preferred_element_type=F32).astype(BF16)
        amps[slot] = lax.dot_general(
            half_way, pick, (((1,), (1,)), ((), ())), preferred_element_type=F32
        ).astype(BF16)
        return carry

    lax.fori_loop(0, counts[0, 0], reorder, 0)
    for copy in copies[1:]:
        copy.wait()

    def visit(slot, carry):
        row, col = frame.place_of(offsets, slot)

        @pl.when(jnp.logical_and(row >= margin, row + edge <= margin + frame.tile_rows))
        def _():
            slot_body(slot, row, col, ext, acc, sums, probe, amps, rights, lefts)

        return carry

    lax.fori_loop(0, counts[0, 0], visit, 0)


def boundary_kernel(geometry, offsets, counts, straight, diagonal, *refs):
    frame = Frame(*geometry)
    sides = frame.sides
    corners, refs = refs[:sides], refs[sides:]
    probe, amps, rights, lefts = refs[:4]
    ext, acc, sums, mid, over_straight, over_diagonal = refs[7:13]
    side_outs, refs = refs[13 : 13 + sides], refs[13 + sides :]
    keep, send, sems = refs
    tiles, margin, body = frame.tiles, frame.margin, frame.body
    edge = probe.shape[-1]
    pairs = []
    for number, halo in enumerate((straight, diagonal)):
        for c in range(2):
            for t in range(tiles):
                part = halo.at[pl.ds((2 * t + c) * margin, margin), :]
                pairs.append((part, ext.at[1 + t, c, frame.halo_rows(number), :]))
            for side, corner in enumerate(corners):
                part = corner.at[pl.ds((2 * number + c) * margin, margin), :]
                pairs.append((part, ext.at[frame.side_block(side), c, frame.halo_rows(number), :]))
    for copy in copy_all(pairs, sems):
        copy.wait()

    def visit(slot, carry):
        row, col = frame.place_of(offsets, slot)

        @pl.when(jnp.logical_or(row < margin, row + edge > margin + frame.tile_rows))
        def _():
            slot_body(slot, row, col, ext, acc, sums, probe, amps, rights, lefts)

        return carry

    lax.fori_loop(0, counts[0, 0], visit, 0)
    out = [(acc.at[1 + t, :, body, :], mid.at[t]) for t in range(tiles)]
    copies = copy_all(out, sems)
    rows = keep.shape[1]
    index = frame.col & 1
    keep[...] = sums[:, aligned(index * rows, rows), :]
    send[...] = sums[:, aligned((1 - index) * rows, rows), :]
    for side, side_out in enumerate(side_outs):
        side_out[...] = acc[frame.side_block(side)]
    for number, over in enumerate((over_straight, over_diagonal)):
        for t in range(tiles):
            over[t] = acc[1 + t, :, frame.halo_rows(number), :]
    for copy in copies:
        copy.wait()


def corner_kernel(geometry, offsets, counts, straight, diagonal, *outs):
    frame = Frame(*geometry)
    size = 2 * frame.margin
    rows = where_rows(offsets, counts)
    for side, out in enumerate(outs):
        for number, strip in enumerate((straight, diagonal)):
            edge = frame.edge_tile(side) * size
            out[pl.ds(number * size, size), :] = strip[aligned(edge, size), :]
            out[pl.ds(2 * size + (number + 1) * WHERE, WHERE), :] = strip[
                pl.ds(strip.shape[0] - WHERE, WHERE), :
            ]
        for number, row in enumerate(rows):
            out[pl.ds(2 * size + number, 1), :] = row


KERNEL_VMEM = 12 * MIB
SLOT_COST = dict(
    cost_estimate=pl.CostEstimate(flops=int(1e10), bytes_accessed=20_000_000, transcendentals=0),
)


def run_interior(geometry, offsets, counts, tile, probe, amps, tables, halos):
    tile_rows, tile_cols, margin, sides = geometry
    edge = probe.shape[-1]
    modes = probe.shape[1]
    window = shape(tile_cols // LANES + 2, 2, tile_rows + 2 * margin, LANES)
    amp_shape = jax.ShapeDtypeStruct(amps.shape[2:], BF16)
    outs = [window, window, shape(2 * modes + 1, edge, edge), shape(*probe.shape), amp_shape]
    outs += [jax.ShapeDtypeStruct(t.shape, t.dtype) for t in tables]
    return pl.pallas_call(
        functools.partial(interior_kernel, geometry),
        out_shape=outs,
        in_specs=[IN_SMEM] * 2 + [IN_HBM] * 5 + [ANYWHERE] * sides,
        out_specs=[IN_VMEM] * len(outs),
        scratch_shapes=[VMEM(amp_shape.shape, BF16), pltpu.SemaphoreType.DMA((16,))],
        compiler_params=pltpu.CompilerParams(vmem_limit_bytes=KERNEL_VMEM),
        name="slots_interior",
        **SLOT_COST,
    )(offsets, counts, tile, probe, amps, *tables, *halos)


def run_boundary(geometry, offsets, counts, straight, diagonal, corners, consts, ext, acc, sums):
    tile_rows, tile_cols, margin, sides = geometry
    planes, edge = sums.shape[:2]
    tiles = tile_cols // LANES
    part = shape(planes, edge // 2, edge)
    strip = shape(tiles, 2, margin, LANES)
    outs = [shape(*ext.shape), shape(*acc.shape), shape(*sums.shape)]
    outs += [shape(tiles, 2, tile_rows, LANES), strip, strip]
    outs += [shape(*acc.shape[1:])] * sides + [part, part]
    base = 4 + sides + 4
    return pl.pallas_call(
        functools.partial(boundary_kernel, geometry),
        out_shape=outs,
        in_specs=[IN_SMEM] * 2 + [ANYWHERE] * (2 + sides) + [IN_VMEM] * 7,
        out_specs=[IN_VMEM] * 3 + [IN_HBM] + [IN_VMEM] * (len(outs) - 4),
        scratch_shapes=[pltpu.SemaphoreType.DMA((4 * (tiles + sides),))],
        input_output_aliases={base: 0, base + 1: 1, base + 2: 2},
        compiler_params=pltpu.CompilerParams(vmem_limit_bytes=KERNEL_VMEM),
        name="slots_boundary",
        **SLOT_COST,
    )(offsets, counts, straight, diagonal, *corners, *consts, ext, acc, sums)


def fold_kernel(geometry, over_straight, over_diagonal, *refs):
    frame = Frame(*geometry)
    received, outs = refs[: frame.sides], refs[frame.sides : frame.sides + 2]
    for number, (over, out) in enumerate(((over_straight, outs[0]), (over_diagonal, outs[1]))):
        out[...] = over[...]
        for side, value in enumerate(received):
            out[frame.side_target(side) - 1] += value[:, frame.halo_rows(number), :]


def light_kernel(geometry, offsets, counts, *refs):
    frame = Frame(*geometry)
    others, (probe, out, canvas) = refs[:-3], refs[-3:]
    tiles = frame.tiles
    edge = probe.shape[-1]
    modes = probe.shape[1]
    canvas[...] = jnp.zeros_like(canvas)
    power = [
        sum(
            probe[c, k, :, pl.ds(t * LANES, LANES)] * probe[c, k, :, pl.ds(t * LANES, LANES)]
            for c in range(2)
            for k in range(modes)
        )
        for t in range(2)
    ]

    def add_from(read):
        def visit(slot, carry):
            row = read(0, slot) - frame.row * frame.tile_rows + edge
            col = read(1, slot) - frame.col * frame.tile_cols + edge
            meets = (row > 0) & (row < frame.tile_rows + edge) & (col > 0) & (col < frame.tile_cols + edge)

            @pl.when(meets)
            def _():
                block = col // LANES
                add_window(canvas, 0, power, row, block, col - block * LANES)

            return carry

        lax.fori_loop(0, read(2, 0), visit, 0)

    add_from(lambda plane, slot: counts[0, 0] if plane == 2 else offsets[0, 0, plane, slot])
    for other in others:
        for first in range(0, other.shape[0], WHERE):
            add_from(lambda plane, slot, other=other, first=first: other[first + plane, slot])
    for t in range(tiles):
        out[t] = canvas[edge // LANES + t, 0, pl.ds(edge, frame.tile_rows), :]


def object_kernel(geometry, tile, mid, light, from_straight, from_diagonal, *refs):
    frame = Frame(*geometry)
    received, (out, old, stage, sems_in, sems_out) = refs[: frame.sides], refs[frame.sides :]
    tiles = frame.tiles
    loads = []
    for t in range(tiles):
        loads.append(
            (
                pltpu.make_async_copy(
                    tile.at[:, :, pl.ds(t * LANES, LANES)], old.at[t], sems_in.at[2 * t]
                ),
                pltpu.make_async_copy(mid.at[t], stage.at[t], sems_in.at[2 * t + 1]),
            )
        )
        for copy in loads[-1]:
            copy.start()
    copies = []
    for t in range(tiles):
        for copy in loads[t]:
            copy.wait()
        for side, value in enumerate(received):

            @pl.when(frame.side_target(side) == 1 + t)
            def _(value=value, t=t):
                stage[t] += value[:, frame.body, :]

        for number, value in enumerate((from_straight, from_diagonal)):
            stage[t, :, frame.strip_rows(number), :] += value[t]
        scale = 1.0 / (light[t] + 1.0)
        for c in range(2):
            stage[t, c] = old[t, c] + stage[t, c] * scale
        copy = pltpu.make_async_copy(
            stage.at[t], out.at[:, :, pl.ds(t * LANES, LANES)], sems_out.at[t]
        )
        copy.start()
        copies.append(copy)
    for copy in copies:
        copy.wait()


def member_perm(axis, bits, member):
    mask = sum(((member >> position) & 1) << bit for position, bit in enumerate(bits))
    return [(i, i ^ mask) for i in range(lax.axis_size(axis))]


def member_index(axis, bits):
    where = lax.axis_index(axis)
    return sum(((where >> bit) & 1) << position for position, bit in enumerate(bits))


def combine_kernel(inputs, stage, *refs):
    ins, outs = refs[:inputs], refs[inputs:]
    rows = outs[0].shape[1]
    for member, out in enumerate(outs):
        part = slice(None)
        if len(outs) > 1:
            part = aligned(jnp.bitwise_xor(member_index(*stage), member) * rows, rows)
        value = ins[0][:, part, :]
        for other in ins[1:]:
            value = value + other[:, part, :]
        out[...] = value


def combine(stage, parts, group):
    planes, rows, cols = parts[0].shape
    if (rows // group) % 8:
        total = sum(parts[1:], parts[0])
        if group == 1:
            return [total]
        rows = rows // group
        return [
            lax.dynamic_slice_in_dim(
                total, jnp.bitwise_xor(member_index(*stage), m) * rows, rows, axis=1
            )
            for m in range(group)
        ]
    return small_call(
        functools.partial(combine_kernel, len(parts), stage),
        [shape(planes, rows // group, cols)] * group,
        [IN_VMEM] * len(parts),
    )(*parts)


def place_kernel(group, stage, *refs):
    ins, out = refs[:group], refs[group]
    rows = ins[0].shape[1]
    for member, piece in enumerate(ins):
        at = jnp.bitwise_xor(member_index(*stage), member) * rows
        out[:, aligned(at, rows), :] = piece[...]


def place(stage, parts):
    planes, rows, cols = parts[0].shape
    if rows % 8:
        whole = jnp.zeros((planes, rows * len(parts), cols), F32)
        for m, piece in enumerate(parts):
            at = jnp.bitwise_xor(member_index(*stage), m) * rows
            whole = lax.dynamic_update_slice_in_dim(whole, piece, at, axis=1)
        return whole
    return small_call(
        functools.partial(place_kernel, len(parts), stage),
        [shape(planes, rows * len(parts), cols)],
        [IN_VMEM] * len(parts),
    )(*parts)[0]


def shard_start(stages, edge):
    start, rows = jnp.int32(0), edge
    for axis, bits in stages:
        rows = rows >> len(bits)
        start = start + member_index(axis, bits) * rows
    return start


def finish_kernel(stages, edge, probe, *refs):
    ins, out = refs[:-1], refs[-1]
    total = ins[0][...]
    for other in ins[1:]:
        total = total + other[...]
    planes, rows = out.shape[:2]
    old = probe[:, aligned(shard_start(stages, edge), rows), :]
    out[...] = old + total[:planes] / (total[planes:] + 1.0)


def finish(stages, probe, parts):
    planes, rows, cols = parts[0].shape
    edge = probe.shape[1]
    if rows % 8:
        total = sum(parts[1:], parts[0])
        old = lax.dynamic_slice_in_dim(probe, shard_start(stages, edge), rows, axis=1)
        return old + total[:-1] / (total[-1:] + 1.0)
    return small_call(
        functools.partial(finish_kernel, stages, edge),
        [shape(planes - 1, rows, cols)],
        [IN_VMEM] * (1 + len(parts)),
    )(probe, *parts)[0]


def swap_sides(outs):
    count = lax.axis_size("col")
    if len(outs) == 1:
        return [lax.ppermute(outs[0], "col", [(0, 1), (1, 0)])]
    up = [(i, i + 1) for i in range(count - 1)]
    down = [(i + 1, i) for i in range(count - 1)]
    return [lax.ppermute(outs[1], "col", up), lax.ppermute(outs[0], "col", down)]


def swap_rows(value, number):
    count = lax.axis_size("row")
    pairs = []
    for low in range(number, count - 1, 2):
        pairs += [(low, low + 1), (low + 1, low)]
    return lax.ppermute(value, "row", pairs)


def stages_of(rows, cols):
    stages = [("col", (bit,)) for bit in range(cols.bit_length() - 1)]
    bits = list(range(1, rows.bit_length() - 1))
    if len(bits) > 1:
        stages.append(("row", (bits[0], bits[1])))
        bits = bits[2:]
    stages += [("row", (bit,)) for bit in bits]
    return tuple(stages), ("row", (0,))


def step(object_field, probe_modes, scan_offsets, scan_counts, amplitudes):
    tile_rows, tile_cols = object_field.shape[1:]
    modes = probe_modes.shape[1]
    edge = probe_modes.shape[-1]
    margin = edge // 2
    tiles = tile_cols // LANES
    sides = 1 if lax.axis_size("col") == 2 else 2
    geometry = (tile_rows, tile_cols, margin, sides)
    stages, last = stages_of(lax.axis_size("row"), lax.axis_size("col"))
    tables = tuple(in_hbm(jnp.asarray(t)) for t in dft_tables(edge))
    tile_hbm, probe_hbm, amps_hbm = in_hbm(object_field), in_hbm(probe_modes), in_hbm(amplitudes)

    straight, diagonal, *edges = small_call(
        functools.partial(pack_kernel, geometry),
        [shape(2 * margin * tiles + WHERE, LANES)] * 2 + [shape(2, tile_rows, margin)] * sides,
        [IN_SMEM, IN_SMEM, IN_HBM],
        limit=8 * MIB,
        scratch=(pltpu.SemaphoreType.DMA((4 * tiles + sides,)),),
    )(scan_offsets, scan_counts, tile_hbm)
    straight = swap_rows(straight, 0)
    diagonal = swap_rows(diagonal, 1)
    halos = swap_sides(edges)

    ext, acc, sums, *consts = run_interior(
        geometry, scan_offsets, scan_counts, tile_hbm, probe_hbm, amps_hbm, tables, halos
    )

    cut = small_call(
        functools.partial(corner_kernel, geometry),
        [shape(4 * margin + 3 * WHERE, LANES)] * sides,
        [IN_SMEM] * 2 + [IN_VMEM] * 2,
    )(scan_offsets, scan_counts, straight, diagonal)
    corners = swap_sides(cut)

    _, _, _, mid, *rest = run_boundary(
        geometry, scan_offsets, scan_counts, straight, diagonal, corners, consts, ext, acc, sums
    )
    overs, side_outs, (keep, send) = rest[:2], rest[2 : 2 + sides], rest[2 + sides :]

    parts = [keep]
    for number, stage in enumerate(stages):
        axis, bits = stage
        if number:
            mine, *pieces = combine(stage, parts, 1 << len(bits))
        else:
            mine, pieces = keep, [send]
        parts = [mine] + [
            lax.ppermute(piece, axis, member_perm(axis, bits, member + 1))
            for member, piece in enumerate(pieces)
        ]
    total = combine(last, parts, 1)[0]
    parts = [total, lax.ppermute(total, last[0], member_perm(*last, 1))]

    received = swap_sides(side_outs)
    strip = shape(tiles, 2, margin, LANES)
    out_straight, out_diagonal = small_call(
        functools.partial(fold_kernel, geometry), [strip, strip], [IN_VMEM] * (2 + sides)
    )(*overs, *received)
    from_straight = swap_rows(out_straight, 0)
    from_diagonal = swap_rows(out_diagonal, 1)

    flat = probe_modes.reshape(2 * modes, edge, edge)
    shard = finish(stages, flat, parts)
    for number, stage in reversed(list(enumerate(stages))):
        axis, bits = stage
        pieces = [shard] + [
            lax.ppermute(shard, axis, member_perm(axis, bits, member))
            for member in range(1, 1 << len(bits))
        ]
        shard = place(stage, pieces)
    probe_new = shard.reshape(probe_modes.shape)

    others = [strip[-WHERE:].astype(jnp.int32) for strip in (straight, diagonal)]
    others += [corner[-3 * WHERE :].astype(jnp.int32) for corner in corners]
    light = small_call(
        functools.partial(light_kernel, geometry),
        [shape(tiles, tile_rows, LANES)],
        [IN_SMEM] * (4 + sides) + [IN_VMEM],
        limit=8 * MIB,
        scratch=(VMEM((tiles + 2 * (edge // LANES), 1, tile_rows + 2 * edge, LANES), F32),),
        cost=10_000_000,
    )(scan_offsets, scan_counts, *others, probe_modes)[0]
    object_new = small_call(
        functools.partial(object_kernel, geometry),
        [shape(2, tile_rows, tile_cols)],
        [IN_HBM, ANYWHERE] + [IN_VMEM] * (3 + sides),
        limit=8 * MIB,
        scratch=(
            VMEM((tiles, 2, tile_rows, LANES), F32),
            VMEM((tiles, 2, tile_rows, LANES), F32),
            pltpu.SemaphoreType.DMA((2 * tiles,)),
            pltpu.SemaphoreType.DMA((tiles,)),
        ),
        out_specs=[IN_HBM],
    )(object_field, mid, light, from_straight, from_diagonal, *received)[0]
    return object_new, probe_new


def solution(mesh):
    in_specs = (
        P(None, "row", "col"),
        P(),
        P("row", "col", None, None),
        P("row", "col"),
        P("row", "col", None, None, None),
    )
    out_specs = (P(None, "row", "col"), P())
    return jax.shard_map(step, mesh=mesh, in_specs=in_specs, out_specs=out_specs, check_vma=False)
```

```python
import functools
import math

import jax
import jax.numpy as jnp
import numpy as np
from jax import lax
from jax.experimental import pallas as pl
from jax.experimental.pallas import tpu as pltpu
from jax.sharding import PartitionSpec as P


F32 = jnp.float32
BF16 = jnp.bfloat16
LANES = 128


def split_host(table):
    high = table.astype(BF16)
    low = (table - high.astype(np.float64)).astype(BF16)
    return high, low


def dft_tables(edge):
    half = edge // 2
    scale = 1.0 / math.sqrt(edge)
    n = np.arange(half)[:, None]
    k = np.arange(half)[None, :]
    mats = []
    for parity in (0, 1):
        angle = (n * (2 * k + parity) % edge) * (2.0 * np.pi / edge)
        cosine, sine = np.cos(angle) * scale, np.sin(angle) * scale
        mats.append(np.block([[cosine, -sine], [sine, cosine]]))
    mats += [mats[0].T, mats[1].T]
    return np.stack([np.stack(split_host(m)) for m in mats])


def split_parts(x):
    high = x.astype(BF16)
    low = (x - high.astype(F32)).astype(BF16)
    return high, low


def right_dot(x, table):
    high, low = split_parts(x)
    return jnp.dot(jnp.concatenate([high, low, high], axis=1), table, preferred_element_type=F32)


def left_dot(table, x):
    high, low = split_parts(x)
    return jnp.dot(table, jnp.concatenate([high, low, high], axis=0), preferred_element_type=F32)


VMEM = pltpu.VMEM
ANYWHERE = pl.BlockSpec(memory_space=pl.ANY)
IN_VMEM = pl.BlockSpec(memory_space=pltpu.VMEM)
IN_SMEM = pl.BlockSpec(memory_space=pltpu.SMEM)
MIB = 1024 * 1024
IN_HBM = pl.BlockSpec(memory_space=pltpu.HBM)


def in_hbm(x):
    return pltpu.with_memory_space_constraint(x, pltpu.HBM)


def shape(*dims):
    return jax.ShapeDtypeStruct(dims, F32)


def aligned(start, size):
    return pl.ds(pl.multiple_of(start, size) if size % 8 == 0 else start, size)


def copy_all(pairs, sems):
    copies = []
    for number, (src, dst) in enumerate(pairs):
        copy = pltpu.make_async_copy(src, dst, sems.at[number])
        copy.start()
        copies.append(copy)
    return copies


class Frame:
    def __init__(self, tile_rows, tile_cols, margin, sides):
        self.tile_rows, self.tile_cols, self.margin, self.sides = tile_rows, tile_cols, margin, sides
        self.tiles = tile_cols // LANES
        self.row = lax.axis_index("row")
        self.col = lax.axis_index("col")
        self.body = pl.ds(margin, tile_rows)

    def side_is_east(self, number):
        if self.sides == 2:
            return jnp.int32(number)
        return 1 - (self.col & 1)

    def side_block(self, number):
        return self.side_is_east(number) * (self.tiles + 1)

    def side_target(self, number):
        return 1 + self.side_is_east(number) * (self.tiles - 1)

    def side_cols(self, number):
        start = self.side_is_east(number) * (self.tile_cols - self.margin)
        return pl.ds(pl.multiple_of(start, LANES), self.margin)

    def is_below(self, number):
        return jnp.bitwise_xor(1 - (self.row & 1), number)

    def strip_rows(self, number):
        start = self.is_below(number) * (self.tile_rows - self.margin)
        return pl.ds(pl.multiple_of(start, self.margin), self.margin)

    def halo_rows(self, number):
        start = self.is_below(number) * (self.tile_rows + self.margin)
        return pl.ds(pl.multiple_of(start, self.margin), self.margin)

    def place_of(self, offsets, slot):
        return (
            offsets[0, 0, 0, slot] - self.row * self.tile_rows + self.margin,
            offsets[0, 0, 1, slot] - self.col * self.tile_cols + self.margin,
        )


def small_call(kernel, outs, in_specs, limit=4 * MIB, scratch=(), out_specs=None, aliases=None, cost=None):
    return pl.pallas_call(
        kernel,
        out_shape=outs,
        in_specs=in_specs,
        out_specs=out_specs if out_specs is not None else [IN_VMEM] * len(outs),
        scratch_shapes=list(scratch),
        input_output_aliases=aliases or {},
        compiler_params=pltpu.CompilerParams(vmem_limit_bytes=limit),
        cost_estimate=pl.CostEstimate(flops=cost, bytes_accessed=1_000_000, transcendentals=0) if cost else None,
    )


def pack_kernel(geometry, tile, straight, diagonal, *refs):
    sides, sems = refs[:-1], refs[-1]
    frame = Frame(*geometry)
    pairs = [
        (tile.at[:, frame.strip_rows(0), :], straight),
        (tile.at[:, frame.strip_rows(1), :], diagonal),
    ]
    for number, side in enumerate(sides):
        pairs.append((tile.at[:, :, frame.side_cols(number)], side))
    for copy in copy_all(pairs, sems):
        copy.wait()


def add_window(acc, channel, parts, row, block, shift):
    edge = parts[0].shape[0]
    lane = lax.broadcasted_iota(jnp.int32, (edge, LANES), 1)
    keep = lane >= shift
    first = pltpu.roll(parts[0], shift, 1)
    second = pltpu.roll(parts[1], shift, 1)
    rows = pl.ds(row, edge)
    zero = jnp.zeros_like(first)
    last = jnp.minimum(block + 2, acc.shape[0] - 1)
    acc[block, channel, rows, :] += jnp.where(keep, first, zero)
    acc[block + 1, channel, rows, :] += jnp.where(keep, second, first)
    acc[last, channel, rows, :] += jnp.where(keep, zero, second)


def slot_body(slot, row, col, ext, acc, sums, probe, amps, rights, lefts):
    edge = probe.shape[-1]
    modes = probe.shape[1]
    half = edge // 2
    block = col // LANES
    shift = col - block * LANES
    lane = lax.broadcasted_iota(jnp.int32, (edge, LANES), 1)
    back_shift = lax.rem(LANES - shift, LANES)
    keep = lane < LANES - shift
    last = jnp.minimum(block + 2, ext.shape[0] - 1)
    patch = []
    for c in range(2):
        rolled = [
            pltpu.roll(ext[b, c, pl.ds(row, edge), :], back_shift, 1) for b in (block, block + 1, last)
        ]
        patch.append([jnp.where(keep, rolled[t], rolled[t + 1]) for t in range(2)])

    def probe_at(c, k, t):
        return probe[c, k, :, pl.ds(t * LANES, LANES)]

    evens, odds = [], []
    for k in range(modes):
        re = [probe_at(0, k, t) * patch[0][t] - probe_at(1, k, t) * patch[1][t] for t in range(2)]
        im = [probe_at(0, k, t) * patch[1][t] + probe_at(1, k, t) * patch[0][t] for t in range(2)]
        evens.append(right_dot(jnp.concatenate([re[0] + re[1], im[0] + im[1]], axis=1), rights[0]))
        odds.append(right_dot(jnp.concatenate([re[0] - re[1], im[0] - im[1]], axis=1), rights[1]))
    far = []
    for k in range(modes):
        re = jnp.concatenate([evens[k][:, :half], odds[k][:, :half]], axis=1)
        im = jnp.concatenate([evens[k][:, half:], odds[k][:, half:]], axis=1)
        plus = jnp.concatenate([re[:half] + re[half:], im[:half] + im[half:]], axis=0)
        minus = jnp.concatenate([re[:half] - re[half:], im[:half] - im[half:]], axis=0)
        far.append([left_dot(lefts[0], plus), left_dot(lefts[1], minus)])
    factor = []
    for p in range(2):
        total = sum(
            far[k][p][:half] * far[k][p][:half] + far[k][p][half:] * far[k][p][half:]
            for k in range(modes)
        )
        amp = amps[slot, pl.ds(p * half, half), :].astype(F32)
        one = amp / jnp.sqrt(jnp.maximum(total, 0.25)) - 1.0
        factor.append(jnp.concatenate([one, one], axis=0))
    update = [[None, None], [None, None]]
    for k in range(modes):
        even = left_dot(lefts[2], far[k][0] * factor[0])
        odd = left_dot(lefts[3], far[k][1] * factor[1])
        plus, minus = even + odd, even - odd
        re = jnp.concatenate([plus[:half], minus[:half]], axis=0)
        im = jnp.concatenate([plus[half:], minus[half:]], axis=0)
        even = right_dot(jnp.concatenate([re[:, :half], im[:, :half]], axis=1), rights[2])
        odd = right_dot(jnp.concatenate([re[:, half:], im[:, half:]], axis=1), rights[3])
        plus, minus = even + odd, even - odd
        back_re = [plus[:, :half], minus[:, :half]]
        back_im = [plus[:, half:], minus[:, half:]]
        for t in range(2):
            pr, pi = probe_at(0, k, t), probe_at(1, k, t)
            u_re = pr * back_re[t] + pi * back_im[t]
            u_im = pr * back_im[t] - pi * back_re[t]
            update[0][t] = u_re if k == 0 else update[0][t] + u_re
            update[1][t] = u_im if k == 0 else update[1][t] + u_im
            lanes = pl.ds(t * LANES, LANES)
            xr, xi = patch[0][t], patch[1][t]
            sums[k, :, lanes] += xr * back_re[t] + xi * back_im[t]
            sums[modes + k, :, lanes] += xr * back_im[t] - xi * back_re[t]
    for t in range(2):
        lanes = pl.ds(t * LANES, LANES)
        sums[2 * modes, :, lanes] += patch[0][t] * patch[0][t] + patch[1][t] * patch[1][t]
    for c in range(2):
        add_window(acc, c, update[c], row, block, shift)


def interior_kernel(geometry, offsets, counts, tile, probe_in, amps_in, tables, *refs):
    frame = Frame(*geometry)
    halos = refs[: frame.sides]
    ext, acc, sums, probe, amps, rights, lefts, raw, sems = refs[frame.sides :]
    tiles, body, margin = frame.tiles, frame.body, frame.margin
    edge = probe.shape[-1]
    pairs = [(amps_in.at[0, 0], raw), (probe_in, probe)]
    for m in range(4):
        for third, part in enumerate((0, 0, 1)):
            span = pl.ds(third * edge, edge)
            pairs.append((tables.at[m, part], rights.at[m, span, :]))
            pairs.append((tables.at[(m + 2) % 4, part], lefts.at[m, :, span]))
    for number, halo in enumerate(halos):
        pairs.append((halo, ext.at[frame.side_block(number), :, body, :]))
    for t in range(tiles):
        pairs.append((tile.at[:, :, pl.ds(t * LANES, LANES)], ext.at[1 + t, :, body, :]))
    copies = copy_all(pairs, sems)
    acc[...] = jnp.zeros_like(acc)
    sums[...] = jnp.zeros_like(sums)
    copies[0].wait()
    out_at = lax.broadcasted_iota(jnp.int32, (edge, edge), 0)
    in_at = lax.broadcasted_iota(jnp.int32, (edge, edge), 1)
    source = jnp.where(out_at < edge // 2, 2 * out_at, 2 * out_at - edge + 1)
    pick = jnp.where(in_at == source, 1.0, 0.0).astype(BF16)

    def reorder(slot, carry):
        half_way = jnp.dot(pick, raw[slot], preferred_element_type=F32).astype(BF16)
        amps[slot] = lax.dot_general(
            half_way, pick, (((1,), (1,)), ((), ())), preferred_element_type=F32
        ).astype(BF16)
        return carry

    lax.fori_loop(0, counts[0, 0], reorder, 0)
    for copy in copies[1:]:
        copy.wait()

    def visit(slot, carry):
        row, col = frame.place_of(offsets, slot)

        @pl.when(jnp.logical_and(row >= margin, row + edge <= margin + frame.tile_rows))
        def _():
            slot_body(slot, row, col, ext, acc, sums, probe, amps, rights, lefts)

        return carry

    lax.fori_loop(0, counts[0, 0], visit, 0)


def boundary_kernel(geometry, offsets, counts, straight, diagonal, *refs):
    frame = Frame(*geometry)
    sides = frame.sides
    corners, refs = refs[:sides], refs[sides:]
    probe, amps, rights, lefts = refs[:4]
    ext, acc, sums, mid, over_straight, over_diagonal = refs[7:13]
    side_outs, refs = refs[13 : 13 + sides], refs[13 + sides :]
    keep, send, sems = refs
    tiles, margin, body = frame.tiles, frame.margin, frame.body
    edge = probe.shape[-1]
    pairs = []
    for number, halo in enumerate((straight, diagonal)):
        for t in range(tiles):
            pairs.append(
                (halo.at[:, :, pl.ds(t * LANES, LANES)], ext.at[1 + t, :, frame.halo_rows(number), :])
            )
        for side, corner in enumerate(corners):
            pairs.append(
                (corner.at[number], ext.at[frame.side_block(side), :, frame.halo_rows(number), :])
            )
    for copy in copy_all(pairs, sems):
        copy.wait()

    def visit(slot, carry):
        row, col = frame.place_of(offsets, slot)

        @pl.when(jnp.logical_or(row < margin, row + edge > margin + frame.tile_rows))
        def _():
            slot_body(slot, row, col, ext, acc, sums, probe, amps, rights, lefts)

        return carry

    lax.fori_loop(0, counts[0, 0], visit, 0)
    out = [(acc.at[1 + t, :, body, :], mid.at[t]) for t in range(tiles)]
    copies = copy_all(out, sems)
    rows = keep.shape[1]
    index = frame.col & 1
    keep[...] = sums[:, aligned(index * rows, rows), :]
    send[...] = sums[:, aligned((1 - index) * rows, rows), :]
    for side, side_out in enumerate(side_outs):
        side_out[...] = acc[frame.side_block(side)]
    for number, over in enumerate((over_straight, over_diagonal)):
        for t in range(tiles):
            over[t] = acc[1 + t, :, frame.halo_rows(number), :]
    for copy in copies:
        copy.wait()


def corner_kernel(geometry, straight, diagonal, *outs):
    frame = Frame(*geometry)
    for side, out in enumerate(outs):
        out[0] = straight[:, :, frame.side_cols(side)]
        out[1] = diagonal[:, :, frame.side_cols(side)]


KERNEL_VMEM = 12 * MIB
SLOT_COST = dict(
    cost_estimate=pl.CostEstimate(flops=int(1e10), bytes_accessed=20_000_000, transcendentals=0),
)


def run_interior(geometry, offsets, counts, tile, probe, amps, tables, halos):
    tile_rows, tile_cols, margin, sides = geometry
    edge = probe.shape[-1]
    modes = probe.shape[1]
    window = shape(tile_cols // LANES + 2, 2, tile_rows + 2 * margin, LANES)
    amp_shape = jax.ShapeDtypeStruct(amps.shape[2:], BF16)
    outs = [window, window, shape(2 * modes + 1, edge, edge), shape(*probe.shape), amp_shape]
    outs += [
        jax.ShapeDtypeStruct((4, 3 * edge, edge), BF16),
        jax.ShapeDtypeStruct((4, edge, 3 * edge), BF16),
    ]
    return pl.pallas_call(
        functools.partial(interior_kernel, geometry),
        out_shape=outs,
        in_specs=[IN_SMEM] * 2 + [IN_HBM] * 4 + [ANYWHERE] * sides,
        out_specs=[IN_VMEM] * len(outs),
        scratch_shapes=[
            VMEM(amp_shape.shape, BF16),
            pltpu.SemaphoreType.DMA((26 + sides + tile_cols // LANES,)),
        ],
        compiler_params=pltpu.CompilerParams(vmem_limit_bytes=KERNEL_VMEM),
        name="slots_interior",
        **SLOT_COST,
    )(offsets, counts, tile, probe, amps, tables, *halos)


def run_boundary(geometry, offsets, counts, straight, diagonal, corners, consts, ext, acc, sums):
    tile_rows, tile_cols, margin, sides = geometry
    planes, edge = sums.shape[:2]
    tiles = tile_cols // LANES
    part = shape(planes, edge // 2, edge)
    strip = shape(tiles, 2, margin, LANES)
    outs = [shape(*ext.shape), shape(*acc.shape), shape(*sums.shape)]
    outs += [shape(tiles, 2, tile_rows, LANES), strip, strip]
    outs += [shape(*acc.shape[1:])] * sides + [part, part]
    base = 4 + sides + 4
    return pl.pallas_call(
        functools.partial(boundary_kernel, geometry),
        out_shape=outs,
        in_specs=[IN_SMEM] * 2 + [ANYWHERE] * (2 + sides) + [IN_VMEM] * 7,
        out_specs=[IN_VMEM] * 3 + [IN_HBM] + [IN_VMEM] * (len(outs) - 4),
        scratch_shapes=[pltpu.SemaphoreType.DMA((16,))],
        input_output_aliases={base: 0, base + 1: 1, base + 2: 2},
        compiler_params=pltpu.CompilerParams(vmem_limit_bytes=KERNEL_VMEM),
        name="slots_boundary",
        **SLOT_COST,
    )(offsets, counts, straight, diagonal, *corners, *consts, ext, acc, sums)


def fold_kernel(geometry, over_straight, over_diagonal, *refs):
    frame = Frame(*geometry)
    received, outs = refs[: frame.sides], refs[frame.sides : frame.sides + 2]
    for number, (over, out) in enumerate(((over_straight, outs[0]), (over_diagonal, outs[1]))):
        out[...] = over[...]
        for side, value in enumerate(received):
            out[frame.side_target(side) - 1] += value[:, frame.halo_rows(number), :]


def light_kernel(geometry, own, *refs):
    frame = Frame(*geometry)
    others, (probe, out, canvas) = refs[:-3], refs[-3:]
    tiles = frame.tiles
    edge = probe.shape[-1]
    modes = probe.shape[1]
    canvas[...] = jnp.zeros_like(canvas)
    power = [
        sum(
            probe[c, k, :, pl.ds(t * LANES, LANES)] * probe[c, k, :, pl.ds(t * LANES, LANES)]
            for c in range(2)
            for k in range(modes)
        )
        for t in range(2)
    ]

    def add_from(read):
        def visit(slot, carry):
            row = read(0, slot) - frame.row * frame.tile_rows + edge
            col = read(1, slot) - frame.col * frame.tile_cols + edge
            meets = (row > 0) & (row < frame.tile_rows + edge) & (col > 0) & (col < frame.tile_cols + edge)

            @pl.when(meets)
            def _():
                block = col // LANES
                add_window(canvas, 0, power, row, block, col - block * LANES)

            return carry

        lax.fori_loop(0, read(2, 0), visit, 0)

    add_from(lambda plane, slot: own[plane, slot])
    for other in others:
        if len(other.shape) == 2:
            add_from(lambda plane, slot, other=other: other[plane, slot])
        else:
            for tile in range(other.shape[0]):
                add_from(lambda plane, slot, other=other, tile=tile: other[tile, plane, slot])
    for t in range(tiles):
        out[t] = canvas[edge // LANES + t, 0, pl.ds(edge, frame.tile_rows), :]


def object_kernel(geometry, tile, mid, light, from_straight, from_diagonal, *refs):
    frame = Frame(*geometry)
    received, (out, old, stage, sems_in, sems_out) = refs[: frame.sides], refs[frame.sides :]
    tiles = frame.tiles
    loads = []
    for t in range(tiles):
        loads.append(
            (
                pltpu.make_async_copy(
                    tile.at[:, :, pl.ds(t * LANES, LANES)], old.at[t], sems_in.at[2 * t]
                ),
                pltpu.make_async_copy(mid.at[t], stage.at[t], sems_in.at[2 * t + 1]),
            )
        )
        for copy in loads[-1]:
            copy.start()
    copies = []
    for t in range(tiles):
        for copy in loads[t]:
            copy.wait()
        for side, value in enumerate(received):

            @pl.when(frame.side_target(side) == 1 + t)
            def _(value=value, t=t):
                stage[t] += value[:, frame.body, :]

        for number, value in enumerate((from_straight, from_diagonal)):
            stage[t, :, frame.strip_rows(number), :] += value[t]
        scale = 1.0 / (light[t] + 1.0)
        for c in range(2):
            stage[t, c] = old[t, c] + stage[t, c] * scale
        copy = pltpu.make_async_copy(
            stage.at[t], out.at[:, :, pl.ds(t * LANES, LANES)], sems_out.at[t]
        )
        copy.start()
        copies.append(copy)
    for copy in copies:
        copy.wait()


def member_perm(axis, bits, member):
    mask = sum(((member >> position) & 1) << bit for position, bit in enumerate(bits))
    return [(i, i ^ mask) for i in range(lax.axis_size(axis))]


def member_index(axis, bits):
    where = lax.axis_index(axis)
    return sum(((where >> bit) & 1) << position for position, bit in enumerate(bits))


def combine_kernel(inputs, stage, *refs):
    ins, outs = refs[:inputs], refs[inputs:]
    rows = outs[0].shape[1]
    for member, out in enumerate(outs):
        part = slice(None)
        if len(outs) > 1:
            part = aligned(jnp.bitwise_xor(member_index(*stage), member) * rows, rows)
        value = ins[0][:, part, :]
        for other in ins[1:]:
            value = value + other[:, part, :]
        out[...] = value


def combine(stage, parts, group):
    planes, rows, cols = parts[0].shape
    if (rows // group) % 8:
        total = sum(parts[1:], parts[0])
        if group == 1:
            return [total]
        rows = rows // group
        return [
            lax.dynamic_slice_in_dim(
                total, jnp.bitwise_xor(member_index(*stage), m) * rows, rows, axis=1
            )
            for m in range(group)
        ]
    return small_call(
        functools.partial(combine_kernel, len(parts), stage),
        [shape(planes, rows // group, cols)] * group,
        [IN_VMEM] * len(parts),
    )(*parts)


def place_kernel(group, stage, *refs):
    ins, out = refs[:group], refs[group]
    rows = ins[0].shape[1]
    for member, piece in enumerate(ins):
        at = jnp.bitwise_xor(member_index(*stage), member) * rows
        out[:, aligned(at, rows), :] = piece[...]


def place(stage, parts):
    planes, rows, cols = parts[0].shape
    if rows % 8:
        whole = jnp.zeros((planes, rows * len(parts), cols), F32)
        for m, piece in enumerate(parts):
            at = jnp.bitwise_xor(member_index(*stage), m) * rows
            whole = lax.dynamic_update_slice_in_dim(whole, piece, at, axis=1)
        return whole
    return small_call(
        functools.partial(place_kernel, len(parts), stage),
        [shape(planes, rows * len(parts), cols)],
        [IN_VMEM] * len(parts),
    )(*parts)[0]


def shard_start(stages, edge):
    start, rows = jnp.int32(0), edge
    for axis, bits in stages:
        rows = rows >> len(bits)
        start = start + member_index(axis, bits) * rows
    return start


def finish_kernel(stages, edge, probe, *refs):
    ins, out = refs[:-1], refs[-1]
    total = ins[0][...]
    for other in ins[1:]:
        total = total + other[...]
    planes, rows = out.shape[:2]
    old = probe[:, aligned(shard_start(stages, edge), rows), :]
    out[...] = old + total[:planes] / (total[planes:] + 1.0)


def finish(stages, probe, parts):
    planes, rows, cols = parts[0].shape
    edge = probe.shape[1]
    if rows % 8:
        total = sum(parts[1:], parts[0])
        old = lax.dynamic_slice_in_dim(probe, shard_start(stages, edge), rows, axis=1)
        return old + total[:-1] / (total[-1:] + 1.0)
    return small_call(
        functools.partial(finish_kernel, stages, edge),
        [shape(planes - 1, rows, cols)],
        [IN_VMEM] * (1 + len(parts)),
    )(probe, *parts)[0]


def swap_sides(outs):
    count = lax.axis_size("col")
    if len(outs) == 1:
        return [lax.ppermute(outs[0], "col", [(0, 1), (1, 0)])]
    up = [(i, i + 1) for i in range(count - 1)]
    down = [(i + 1, i) for i in range(count - 1)]
    return [lax.ppermute(outs[1], "col", up), lax.ppermute(outs[0], "col", down)]


def swap_rows(value, number):
    count = lax.axis_size("row")
    pairs = []
    for low in range(number, count - 1, 2):
        pairs += [(low, low + 1), (low + 1, low)]
    return lax.ppermute(value, "row", pairs)


def stages_of(rows, cols):
    stages = [("col", (bit,)) for bit in range(cols.bit_length() - 1)]
    bits = list(range(1, rows.bit_length() - 1))
    if len(bits) > 1:
        stages.append(("row", (bits[0], bits[1])))
        bits = bits[2:]
    stages += [("row", (bit,)) for bit in bits]
    return tuple(stages), ("row", (0,))


def step(object_field, probe_modes, scan_offsets, scan_counts, amplitudes):
    tile_rows, tile_cols = object_field.shape[1:]
    modes = probe_modes.shape[1]
    edge = probe_modes.shape[-1]
    margin = edge // 2
    slots = amplitudes.shape[2]
    tiles = tile_cols // LANES
    sides = 1 if lax.axis_size("col") == 2 else 2
    geometry = (tile_rows, tile_cols, margin, sides)
    stages, last = stages_of(lax.axis_size("row"), lax.axis_size("col"))
    tables = in_hbm(jnp.asarray(dft_tables(edge)))
    tile_hbm, probe_hbm, amps_hbm = in_hbm(object_field), in_hbm(probe_modes), in_hbm(amplitudes)

    straight, diagonal, *edges = small_call(
        functools.partial(pack_kernel, geometry),
        [shape(2, margin, tile_cols)] * 2 + [shape(2, tile_rows, margin)] * sides,
        [IN_HBM],
        limit=8 * MIB,
        scratch=(pltpu.SemaphoreType.DMA((4,)),),
    )(tile_hbm)
    straight = swap_rows(straight, 0)
    diagonal = swap_rows(diagonal, 1)
    halos = swap_sides(edges)

    own = jnp.concatenate(
        [scan_offsets[0, 0], jnp.broadcast_to(scan_counts[0], (1, slots))], axis=0
    )
    stacked = jnp.stack([own, swap_rows(own, 0), swap_rows(own, 1)])
    beside = swap_sides([stacked] * sides)

    ext, acc, sums, *consts = run_interior(
        geometry, scan_offsets, scan_counts, tile_hbm, probe_hbm, amps_hbm, tables, halos
    )

    cut = small_call(
        functools.partial(corner_kernel, geometry),
        [shape(2, 2, margin, margin)] * sides,
        [IN_VMEM] * 2,
    )(straight, diagonal)
    corners = swap_sides(cut)

    _, _, _, mid, *rest = run_boundary(
        geometry, scan_offsets, scan_counts, straight, diagonal, corners, consts, ext, acc, sums
    )
    overs, side_outs, (keep, send) = rest[:2], rest[2 : 2 + sides], rest[2 + sides :]

    parts = [keep]
    for number, stage in enumerate(stages):
        axis, bits = stage
        if number:
            mine, *pieces = combine(stage, parts, 1 << len(bits))
        else:
            mine, pieces = keep, [send]
        parts = [mine] + [
            lax.ppermute(piece, axis, member_perm(axis, bits, member + 1))
            for member, piece in enumerate(pieces)
        ]
    total = combine(last, parts, 1)[0]
    parts = [total, lax.ppermute(total, last[0], member_perm(*last, 1))]

    received = swap_sides(side_outs)
    strip = shape(tiles, 2, margin, LANES)
    out_straight, out_diagonal = small_call(
        functools.partial(fold_kernel, geometry), [strip, strip], [IN_VMEM] * (2 + sides)
    )(*overs, *received)
    from_straight = swap_rows(out_straight, 0)
    from_diagonal = swap_rows(out_diagonal, 1)

    flat = probe_modes.reshape(2 * modes, edge, edge)
    shard = finish(stages, flat, parts)
    for number, stage in reversed(list(enumerate(stages))):
        axis, bits = stage
        pieces = [shard] + [
            lax.ppermute(shard, axis, member_perm(axis, bits, member))
            for member in range(1, 1 << len(bits))
        ]
        shard = place(stage, pieces)
    probe_new = shard.reshape(probe_modes.shape)

    light = small_call(
        functools.partial(light_kernel, geometry),
        [shape(tiles, tile_rows, LANES)],
        [IN_SMEM] * (2 + sides) + [IN_VMEM],
        limit=8 * MIB,
        scratch=(VMEM((tiles + 2 * (edge // LANES), 1, tile_rows + 2 * edge, LANES), F32),),
        cost=10_000_000,
    )(own, stacked[1:], *beside, probe_modes)[0]
    object_new = small_call(
        functools.partial(object_kernel, geometry),
        [shape(2, tile_rows, tile_cols)],
        [IN_HBM, ANYWHERE] + [IN_VMEM] * (3 + sides),
        limit=8 * MIB,
        scratch=(
            VMEM((tiles, 2, tile_rows, LANES), F32),
            VMEM((tiles, 2, tile_rows, LANES), F32),
            pltpu.SemaphoreType.DMA((2 * tiles,)),
            pltpu.SemaphoreType.DMA((tiles,)),
        ),
        out_specs=[IN_HBM],
    )(object_field, mid, light, from_straight, from_diagonal, *received)[0]
    return object_new, probe_new


def solution(mesh):
    in_specs = (
        P(None, "row", "col"),
        P(),
        P("row", "col", None, None),
        P("row", "col"),
        P("row", "col", None, None, None),
    )
    out_specs = (P(None, "row", "col"), P())
    return jax.shard_map(step, mesh=mesh, in_specs=in_specs, out_specs=out_specs, check_vma=False)
```

```python
import functools
import math

import jax
import jax.numpy as jnp
import numpy as np
from jax import lax
from jax.experimental import pallas as pl
from jax.experimental.pallas import tpu as pltpu
from jax.sharding import PartitionSpec as P


F32 = jnp.float32
BF16 = jnp.bfloat16
LANES = 128


def split_host(table):
    high = table.astype(BF16)
    low = (table - high.astype(np.float64)).astype(BF16)
    return high, low


def dft_tables(edge):
    half = edge // 2
    scale = 1.0 / math.sqrt(edge)
    n = np.arange(half)[:, None]
    k = np.arange(half)[None, :]
    mats = []
    for parity in (0, 1):
        angle = (n * (2 * k + parity) % edge) * (2.0 * np.pi / edge)
        cosine, sine = np.cos(angle) * scale, np.sin(angle) * scale
        mats.append(np.block([[cosine, -sine], [sine, cosine]]))
    mats += [mats[0].T, mats[1].T]
    return np.stack([np.stack(split_host(m)) for m in mats])


def split_parts(x):
    high = x.astype(BF16)
    low = (x - high.astype(F32)).astype(BF16)
    return high, low


def right_dot(x, table):
    high, low = split_parts(x)
    return jnp.dot(jnp.concatenate([high, low, high], axis=1), table, preferred_element_type=F32)


def left_dot(table, x):
    high, low = split_parts(x)
    return jnp.dot(table, jnp.concatenate([high, low, high], axis=0), preferred_element_type=F32)


VMEM = pltpu.VMEM
ANYWHERE = pl.BlockSpec(memory_space=pl.ANY)
IN_VMEM = pl.BlockSpec(memory_space=pltpu.VMEM)
IN_SMEM = pl.BlockSpec(memory_space=pltpu.SMEM)
MIB = 1024 * 1024
IN_HBM = pl.BlockSpec(memory_space=pltpu.HBM)


def in_hbm(x):
    return pltpu.with_memory_space_constraint(x, pltpu.HBM)


def shape(*dims):
    return jax.ShapeDtypeStruct(dims, F32)


def aligned(start, size):
    return pl.ds(pl.multiple_of(start, size) if size % 8 == 0 else start, size)


def copy_all(pairs, sems):
    copies = []
    for number, (src, dst) in enumerate(pairs):
        copy = pltpu.make_async_copy(src, dst, sems.at[number])
        copy.start()
        copies.append(copy)
    return copies


class Frame:
    def __init__(self, tile_rows, tile_cols, margin, sides):
        self.tile_rows, self.tile_cols, self.margin, self.sides = tile_rows, tile_cols, margin, sides
        self.tiles = tile_cols // LANES
        self.row = lax.axis_index("row")
        self.col = lax.axis_index("col")
        self.body = pl.ds(margin, tile_rows)

    def side_is_east(self, number):
        if self.sides == 2:
            return jnp.int32(number)
        return 1 - (self.col & 1)

    def side_block(self, number):
        return self.side_is_east(number) * (self.tiles + 1)

    def side_target(self, number):
        return 1 + self.side_is_east(number) * (self.tiles - 1)

    def side_cols(self, number):
        start = self.side_is_east(number) * (self.tile_cols - self.margin)
        return pl.ds(pl.multiple_of(start, LANES), self.margin)

    def is_below(self, number):
        return jnp.bitwise_xor(1 - (self.row & 1), number)

    def strip_rows(self, number):
        start = self.is_below(number) * (self.tile_rows - self.margin)
        return pl.ds(pl.multiple_of(start, self.margin), self.margin)

    def halo_rows(self, number):
        start = self.is_below(number) * (self.tile_rows + self.margin)
        return pl.ds(pl.multiple_of(start, self.margin), self.margin)

    def place_of(self, offsets, slot):
        return (
            offsets[0, 0, 0, slot] - self.row * self.tile_rows + self.margin,
            offsets[0, 0, 1, slot] - self.col * self.tile_cols + self.margin,
        )


def small_call(kernel, outs, in_specs, limit=4 * MIB, scratch=(), out_specs=None, aliases=None, cost=None):
    return pl.pallas_call(
        kernel,
        out_shape=outs,
        in_specs=in_specs,
        out_specs=out_specs if out_specs is not None else [IN_VMEM] * len(outs),
        scratch_shapes=list(scratch),
        input_output_aliases=aliases or {},
        compiler_params=pltpu.CompilerParams(vmem_limit_bytes=limit),
        cost_estimate=pl.CostEstimate(flops=cost, bytes_accessed=1_000_000, transcendentals=0) if cost else None,
    )


def pack_kernel(geometry, first, tile, *refs):
    outs, sems = refs[:-1], refs[-1]
    frame = Frame(*geometry)
    pairs = [(tile.at[:, frame.strip_rows(0 if first else 1), :], outs[0])]
    for number, side in enumerate(outs[1:]):
        pairs.append((tile.at[:, :, frame.side_cols(number)], side))
    for copy in copy_all(pairs, sems):
        copy.wait()


def add_window(acc, channel, parts, row, block, shift):
    edge = parts[0].shape[0]
    lane = lax.broadcasted_iota(jnp.int32, (edge, LANES), 1)
    keep = lane >= shift
    first = pltpu.roll(parts[0], shift, 1)
    second = pltpu.roll(parts[1], shift, 1)
    rows = pl.ds(row, edge)
    zero = jnp.zeros_like(first)
    last = jnp.minimum(block + 2, acc.shape[0] - 1)
    acc[block, channel, rows, :] += jnp.where(keep, first, zero)
    acc[block + 1, channel, rows, :] += jnp.where(keep, second, first)
    acc[last, channel, rows, :] += jnp.where(keep, zero, second)


def slot_stages(slot, row, col, ext, acc, sums, probe, amps, rights, lefts):
    edge = probe.shape[-1]
    modes = probe.shape[1]
    half = edge // 2
    block = col // LANES
    shift = col - block * LANES
    lane = lax.broadcasted_iota(jnp.int32, (edge, LANES), 1)
    back_shift = lax.rem(LANES - shift, LANES)
    keep = lane < LANES - shift
    last = jnp.minimum(block + 2, ext.shape[0] - 1)
    patch = []
    for c in range(2):
        rolled = [
            pltpu.roll(ext[b, c, pl.ds(row, edge), :], back_shift, 1) for b in (block, block + 1, last)
        ]
        patch.append([jnp.where(keep, rolled[t], rolled[t + 1]) for t in range(2)])

    def probe_at(c, k, t):
        return probe[c, k, :, pl.ds(t * LANES, LANES)]

    def both_modes(parts):
        return jnp.concatenate(parts, axis=0)

    yield
    plus, minus = [], []
    for k in range(modes):
        re = [probe_at(0, k, t) * patch[0][t] - probe_at(1, k, t) * patch[1][t] for t in range(2)]
        im = [probe_at(0, k, t) * patch[1][t] + probe_at(1, k, t) * patch[0][t] for t in range(2)]
        plus.append(jnp.concatenate([re[0] + re[1], im[0] + im[1]], axis=1))
        minus.append(jnp.concatenate([re[0] - re[1], im[0] - im[1]], axis=1))
    even = right_dot(both_modes(plus), rights[0])
    yield
    odd = right_dot(both_modes(minus), rights[1])
    yield
    far = []
    for k in range(modes):
        rows = slice(k * edge, (k + 1) * edge)
        re = jnp.concatenate([even[rows, :half], odd[rows, :half]], axis=1)
        im = jnp.concatenate([even[rows, half:], odd[rows, half:]], axis=1)
        plus = jnp.concatenate([re[:half] + re[half:], im[:half] + im[half:]], axis=0)
        minus = jnp.concatenate([re[:half] - re[half:], im[:half] - im[half:]], axis=0)
        far.append([left_dot(lefts[0], plus), left_dot(lefts[1], minus)])
        yield
    factor = []
    for p in range(2):
        total = sum(
            far[k][p][:half] * far[k][p][:half] + far[k][p][half:] * far[k][p][half:]
            for k in range(modes)
        )
        amp = amps[slot, pl.ds(p * half, half), :].astype(F32)
        one = amp * lax.rsqrt(jnp.maximum(total, 0.25)) - 1.0
        factor.append(jnp.concatenate([one, one], axis=0))
    yield
    evens, odds = [], []
    for k in range(modes):
        even = left_dot(lefts[2], far[k][0] * factor[0])
        odd = left_dot(lefts[3], far[k][1] * factor[1])
        plus, minus = even + odd, even - odd
        re = jnp.concatenate([plus[:half], minus[:half]], axis=0)
        im = jnp.concatenate([plus[half:], minus[half:]], axis=0)
        evens.append(jnp.concatenate([re[:, :half], im[:, :half]], axis=1))
        odds.append(jnp.concatenate([re[:, half:], im[:, half:]], axis=1))
        yield
    even = right_dot(both_modes(evens), rights[2])
    yield
    odd = right_dot(both_modes(odds), rights[3])
    plus, minus = even + odd, even - odd
    yield
    update = [[None, None], [None, None]]
    for k in range(modes):
        rows = slice(k * edge, (k + 1) * edge)
        back_re = [plus[rows, :half], minus[rows, :half]]
        back_im = [plus[rows, half:], minus[rows, half:]]
        for t in range(2):
            pr, pi = probe_at(0, k, t), probe_at(1, k, t)
            u_re = pr * back_re[t] + pi * back_im[t]
            u_im = pr * back_im[t] - pi * back_re[t]
            update[0][t] = u_re if k == 0 else update[0][t] + u_re
            update[1][t] = u_im if k == 0 else update[1][t] + u_im
            lanes = pl.ds(t * LANES, LANES)
            xr, xi = patch[0][t], patch[1][t]
            sums[k, :, lanes] += xr * back_re[t] + xi * back_im[t]
            sums[modes + k, :, lanes] += xr * back_im[t] - xi * back_re[t]
        yield
    for t in range(2):
        lanes = pl.ds(t * LANES, LANES)
        power = patch[0][t] * patch[0][t] + patch[1][t] * patch[1][t]
        sums[2 * modes, :, lanes] += power
    for c in range(2):
        add_window(acc, c, update[c], row, block, shift)


def run_stages(works, lag):
    pending = [(number * lag, work) for number, work in enumerate(works)]
    turn = 0
    while pending:
        kept = []
        for start, work in pending:
            if turn >= start and next(work, work) is work:
                continue
            kept.append((start, work))
        pending = kept
        turn += 1


def slot_body(slot, row, col, *refs):
    run_stages([slot_stages(slot, row, col, *refs)], 0)


def interior_kernel(geometry, offsets, counts, tile, probe_in, amps_in, tables, *refs):
    frame = Frame(*geometry)
    halos = refs[: frame.sides]
    ext, acc, sums, probe, amps, rights, lefts, raw, sems = refs[frame.sides :]
    tiles, body, margin = frame.tiles, frame.body, frame.margin
    edge = probe.shape[-1]
    pairs = [(amps_in.at[0, 0], raw), (probe_in, probe)]
    for m in range(4):
        for third, part in enumerate((0, 0, 1)):
            span = pl.ds(third * edge, edge)
            pairs.append((tables.at[m, part], rights.at[m, span, :]))
            pairs.append((tables.at[(m + 2) % 4, part], lefts.at[m, :, span]))
    for number, halo in enumerate(halos):
        pairs.append((halo, ext.at[frame.side_block(number), :, body, :]))
    for t in range(tiles):
        pairs.append((tile.at[:, :, pl.ds(t * LANES, LANES)], ext.at[1 + t, :, body, :]))
    copies = copy_all(pairs, sems)
    acc[...] = jnp.zeros_like(acc)
    sums[...] = jnp.zeros_like(sums)
    copies[0].wait()
    out_at = lax.broadcasted_iota(jnp.int32, (edge, edge), 0)
    in_at = lax.broadcasted_iota(jnp.int32, (edge, edge), 1)
    source = jnp.where(out_at < edge // 2, 2 * out_at, 2 * out_at - edge + 1)
    pick = jnp.where(in_at == source, 1.0, 0.0).astype(BF16)

    def reorder(slot, carry):
        half_way = jnp.dot(pick, raw[slot], preferred_element_type=F32).astype(BF16)
        amps[slot] = lax.dot_general(
            half_way, pick, (((1,), (1,)), ((), ())), preferred_element_type=F32
        ).astype(BF16)
        return carry

    lax.fori_loop(0, counts[0, 0], reorder, 0)
    for copy in copies[1:]:
        copy.wait()

    def visit(slot, carry):
        row, col = frame.place_of(offsets, slot)

        @pl.when(jnp.logical_and(row >= margin, row + edge <= margin + frame.tile_rows))
        def _():
            slot_body(slot, row, col, ext, acc, sums, probe, amps, rights, lefts)

        return carry

    lax.fori_loop(0, counts[0, 0], visit, 0)


def boundary_kernel(geometry, offsets, counts, straight, diagonal, *refs):
    frame = Frame(*geometry)
    sides = frame.sides
    corners, refs = refs[:sides], refs[sides:]
    probe, amps, rights, lefts = refs[:4]
    ext, acc, sums, mid, over_straight, over_diagonal = refs[7:13]
    side_outs, refs = refs[13 : 13 + sides], refs[13 + sides :]
    keep, send, todo, sems = refs
    tiles, margin, body = frame.tiles, frame.margin, frame.body
    edge = probe.shape[-1]
    pairs = []
    for number, halo in enumerate((straight, diagonal)):
        for t in range(tiles):
            pairs.append(
                (halo.at[:, :, pl.ds(t * LANES, LANES)], ext.at[1 + t, :, frame.halo_rows(number), :])
            )
        for side, corner in enumerate(corners):
            pairs.append(
                (corner.at[number], ext.at[frame.side_block(side), :, frame.halo_rows(number), :])
            )
    for copy in copy_all(pairs, sems):
        copy.wait()

    def note(slot, found):
        row, _ = frame.place_of(offsets, slot)
        chosen = jnp.logical_or(row < margin, row + edge > margin + frame.tile_rows)
        todo[found] = slot
        return found + chosen.astype(jnp.int32)

    found = lax.fori_loop(0, counts[0, 0], note, jnp.int32(0))

    shared = (ext, acc, sums, probe, amps, rights, lefts)

    def visit(pair, carry):
        works = []
        for member in range(2):
            slot = todo[2 * pair + member]
            row, col = frame.place_of(offsets, slot)
            works.append(slot_stages(slot, row, col, *shared))
        run_stages(works, LAG)
        return carry

    lax.fori_loop(0, lax.div(found, 2), visit, 0)

    @pl.when(lax.rem(found, 2) == 1)
    def _():
        slot = todo[found - 1]
        row, col = frame.place_of(offsets, slot)
        slot_body(slot, row, col, *shared)

    out = [(acc.at[1 + t, :, body, :], mid.at[t]) for t in range(tiles)]
    copies = copy_all(out, sems)
    rows = keep.shape[1]
    index = frame.col & 1
    keep[...] = sums[:, aligned(index * rows, rows), :]
    send[...] = sums[:, aligned((1 - index) * rows, rows), :]
    for side, side_out in enumerate(side_outs):
        side_out[...] = acc[frame.side_block(side)]
    for number, over in enumerate((over_straight, over_diagonal)):
        for t in range(tiles):
            over[t] = acc[1 + t, :, frame.halo_rows(number), :]
    for copy in copies:
        copy.wait()


def corner_kernel(geometry, straight, diagonal, *outs):
    frame = Frame(*geometry)
    for side, out in enumerate(outs):
        out[0] = straight[:, :, frame.side_cols(side)]
        out[1] = diagonal[:, :, frame.side_cols(side)]


KERNEL_VMEM = 20 * MIB
LAG = 4
SLOT_COST = dict(
    cost_estimate=pl.CostEstimate(flops=int(1e10), bytes_accessed=20_000_000, transcendentals=0),
)


def run_interior(geometry, offsets, counts, tile, probe, amps, tables, halos):
    tile_rows, tile_cols, margin, sides = geometry
    edge = probe.shape[-1]
    modes = probe.shape[1]
    window = shape(tile_cols // LANES + 2, 2, tile_rows + 2 * margin, LANES)
    amp_shape = jax.ShapeDtypeStruct(amps.shape[2:], BF16)
    outs = [window, window, shape(2 * modes + 1, edge, edge), shape(*probe.shape), amp_shape]
    outs += [
        jax.ShapeDtypeStruct((4, 3 * edge, edge), BF16),
        jax.ShapeDtypeStruct((4, edge, 3 * edge), BF16),
    ]
    return pl.pallas_call(
        functools.partial(interior_kernel, geometry),
        out_shape=outs,
        in_specs=[IN_SMEM] * 2 + [IN_HBM] * 4 + [ANYWHERE] * sides,
        out_specs=[IN_VMEM] * len(outs),
        scratch_shapes=[
            VMEM(amp_shape.shape, BF16),
            pltpu.SemaphoreType.DMA((26 + sides + tile_cols // LANES,)),
        ],
        compiler_params=pltpu.CompilerParams(vmem_limit_bytes=KERNEL_VMEM),
        name="slots_interior",
        **SLOT_COST,
    )(offsets, counts, tile, probe, amps, tables, *halos)


def run_boundary(geometry, offsets, counts, straight, diagonal, corners, consts, ext, acc, sums):
    tile_rows, tile_cols, margin, sides = geometry
    planes, edge = sums.shape[:2]
    tiles = tile_cols // LANES
    part = shape(planes, edge // 2, edge)
    strip = shape(tiles, 2, margin, LANES)
    outs = [shape(*ext.shape), shape(*acc.shape), shape(*sums.shape)]
    outs += [shape(tiles, 2, tile_rows, LANES), strip, strip]
    outs += [shape(*acc.shape[1:])] * sides + [part, part]
    base = 4 + sides + 4
    return pl.pallas_call(
        functools.partial(boundary_kernel, geometry),
        out_shape=outs,
        in_specs=[IN_SMEM] * 2 + [ANYWHERE] * (2 + sides) + [IN_VMEM] * 7,
        out_specs=[IN_VMEM] * 3 + [IN_HBM] + [IN_VMEM] * (len(outs) - 4),
        scratch_shapes=[pltpu.SMEM((8,), jnp.int32), pltpu.SemaphoreType.DMA((16,))],
        input_output_aliases={base: 0, base + 1: 1, base + 2: 2},
        compiler_params=pltpu.CompilerParams(vmem_limit_bytes=KERNEL_VMEM),
        name="slots_boundary",
        **SLOT_COST,
    )(offsets, counts, straight, diagonal, *corners, *consts, ext, acc, sums)


def fold_kernel(geometry, over_straight, over_diagonal, *refs):
    frame = Frame(*geometry)
    received, (straight, low, high, diagonal) = refs[: frame.sides], refs[frame.sides :]
    for number, (over, out) in enumerate(((over_straight, straight), (over_diagonal, diagonal))):
        out[...] = over[...]
        for side, value in enumerate(received):
            out[frame.side_target(side) - 1] += value[:, frame.halo_rows(number), :]
    low[...] = diagonal[pl.ds(0, low.shape[0])]
    high[...] = diagonal[pl.ds(low.shape[0], low.shape[0])]


def light_kernel(geometry, own, *refs):
    frame = Frame(*geometry)
    others, (probe, out, canvas) = refs[:-3], refs[-3:]
    tiles = frame.tiles
    edge = probe.shape[-1]
    modes = probe.shape[1]
    canvas[...] = jnp.zeros_like(canvas)
    power = [
        sum(
            probe[c, k, :, pl.ds(t * LANES, LANES)] * probe[c, k, :, pl.ds(t * LANES, LANES)]
            for c in range(2)
            for k in range(modes)
        )
        for t in range(2)
    ]

    def add_from(read):
        def visit(slot, carry):
            row = read(0, slot) - frame.row * frame.tile_rows + edge
            col = read(1, slot) - frame.col * frame.tile_cols + edge
            meets = (row > 0) & (row < frame.tile_rows + edge) & (col > 0) & (col < frame.tile_cols + edge)

            @pl.when(meets)
            def _():
                block = col // LANES
                add_window(canvas, 0, power, row, block, col - block * LANES)

            return carry

        lax.fori_loop(0, read(2, 0), visit, 0)

    add_from(lambda plane, slot: own[plane, slot])
    for other in others:
        if len(other.shape) == 2:
            add_from(lambda plane, slot, other=other: other[plane, slot])
        else:
            for tile in range(other.shape[0]):
                add_from(lambda plane, slot, other=other, tile=tile: other[tile, plane, slot])
    for t in range(tiles):
        out[t] = canvas[edge // LANES + t, 0, pl.ds(edge, frame.tile_rows), :]


def object_kernel(geometry, tile, mid, light, from_straight, from_low, from_high, *refs):
    frame = Frame(*geometry)
    received, (out, old, stage, sems_in, sems_out) = refs[: frame.sides], refs[frame.sides :]
    tiles = frame.tiles
    loads = []
    for t in range(tiles):
        loads.append(
            (
                pltpu.make_async_copy(
                    tile.at[:, :, pl.ds(t * LANES, LANES)], old.at[t], sems_in.at[2 * t]
                ),
                pltpu.make_async_copy(mid.at[t], stage.at[t], sems_in.at[2 * t + 1]),
            )
        )
        for copy in loads[-1]:
            copy.start()
    copies = []
    for t in range(tiles):
        for copy in loads[t]:
            copy.wait()
        for side, value in enumerate(received):

            @pl.when(frame.side_target(side) == 1 + t)
            def _(value=value, t=t):
                stage[t] += value[:, frame.body, :]

        stage[t, :, frame.strip_rows(0), :] += from_straight[t]
        half = from_low.shape[0]
        stage[t, :, frame.strip_rows(1), :] += from_low[t] if t < half else from_high[t - half]
        scale = 1.0 / (light[t] + 1.0)
        for c in range(2):
            stage[t, c] = old[t, c] + stage[t, c] * scale
        copy = pltpu.make_async_copy(
            stage.at[t], out.at[:, :, pl.ds(t * LANES, LANES)], sems_out.at[t]
        )
        copy.start()
        copies.append(copy)
    for copy in copies:
        copy.wait()


def member_perm(axis, bits, member):
    mask = sum(((member >> position) & 1) << bit for position, bit in enumerate(bits))
    return [(i, i ^ mask) for i in range(lax.axis_size(axis))]


def member_index(axis, bits):
    where = lax.axis_index(axis)
    return sum(((where >> bit) & 1) << position for position, bit in enumerate(bits))


def combine_kernel(inputs, stage, *refs):
    ins, outs = refs[:inputs], refs[inputs:]
    rows = outs[0].shape[1]
    for member, out in enumerate(outs):
        part = slice(None)
        if len(outs) > 1:
            part = aligned(jnp.bitwise_xor(member_index(*stage), member) * rows, rows)
        value = ins[0][:, part, :]
        for other in ins[1:]:
            value = value + other[:, part, :]
        out[...] = value


def combine(stage, parts, group):
    planes, rows, cols = parts[0].shape
    if (rows // group) % 8:
        total = sum(parts[1:], parts[0])
        if group == 1:
            return [total]
        rows = rows // group
        return [
            lax.dynamic_slice_in_dim(
                total, jnp.bitwise_xor(member_index(*stage), m) * rows, rows, axis=1
            )
            for m in range(group)
        ]
    return small_call(
        functools.partial(combine_kernel, len(parts), stage),
        [shape(planes, rows // group, cols)] * group,
        [IN_VMEM] * len(parts),
    )(*parts)


def place_kernel(group, stage, *refs):
    ins, out = refs[:group], refs[group]
    rows = ins[0].shape[1]
    for member, piece in enumerate(ins):
        at = jnp.bitwise_xor(member_index(*stage), member) * rows
        out[:, aligned(at, rows), :] = piece[...]


def place(stage, parts):
    planes, rows, cols = parts[0].shape
    if rows % 8:
        whole = jnp.zeros((planes, rows * len(parts), cols), F32)
        for m, piece in enumerate(parts):
            at = jnp.bitwise_xor(member_index(*stage), m) * rows
            whole = lax.dynamic_update_slice_in_dim(whole, piece, at, axis=1)
        return whole
    return small_call(
        functools.partial(place_kernel, len(parts), stage),
        [shape(planes, rows * len(parts), cols)],
        [IN_VMEM] * len(parts),
    )(*parts)[0]


def shard_start(stages, edge):
    start, rows = jnp.int32(0), edge
    for axis, bits in stages:
        rows = rows >> len(bits)
        start = start + member_index(axis, bits) * rows
    return start


def finish_kernel(stages, edge, probe, *refs):
    ins, out = refs[:-1], refs[-1]
    total = ins[0][...]
    for other in ins[1:]:
        total = total + other[...]
    planes, rows = out.shape[:2]
    old = probe[:, aligned(shard_start(stages, edge), rows), :]
    out[...] = old + total[:planes] / (total[planes:] + 1.0)


def finish(stages, probe, parts):
    planes, rows, cols = parts[0].shape
    edge = probe.shape[1]
    if rows % 8:
        total = sum(parts[1:], parts[0])
        old = lax.dynamic_slice_in_dim(probe, shard_start(stages, edge), rows, axis=1)
        return old + total[:-1] / (total[-1:] + 1.0)
    return small_call(
        functools.partial(finish_kernel, stages, edge),
        [shape(planes - 1, rows, cols)],
        [IN_VMEM] * (1 + len(parts)),
    )(probe, *parts)[0]


def swap_sides(outs):
    count = lax.axis_size("col")
    if len(outs) == 1:
        return [lax.ppermute(outs[0], "col", [(0, 1), (1, 0)])]
    up = [(i, i + 1) for i in range(count - 1)]
    down = [(i + 1, i) for i in range(count - 1)]
    return [lax.ppermute(outs[1], "col", up), lax.ppermute(outs[0], "col", down)]


def swap_rows(value, number):
    count = lax.axis_size("row")
    pairs = []
    for low in range(number, count - 1, 2):
        pairs += [(low, low + 1), (low + 1, low)]
    return lax.ppermute(value, "row", pairs)


def stages_of(rows, cols):
    stages = [("col", (bit,)) for bit in range(cols.bit_length() - 1)]
    bits = list(range(1, rows.bit_length() - 1))
    if len(bits) > 1:
        stages.append(("row", (bits[0], bits[1])))
        bits = bits[2:]
    stages += [("row", (bit,)) for bit in bits]
    return tuple(stages), ("row", (0,))


def step(object_field, probe_modes, scan_offsets, scan_counts, amplitudes):
    tile_rows, tile_cols = object_field.shape[1:]
    modes = probe_modes.shape[1]
    edge = probe_modes.shape[-1]
    margin = edge // 2
    slots = amplitudes.shape[2]
    tiles = tile_cols // LANES
    sides = 1 if lax.axis_size("col") == 2 else 2
    geometry = (tile_rows, tile_cols, margin, sides)
    stages, last = stages_of(lax.axis_size("row"), lax.axis_size("col"))
    tables = in_hbm(jnp.asarray(dft_tables(edge)))
    tile_hbm, probe_hbm, amps_hbm = in_hbm(object_field), in_hbm(probe_modes), in_hbm(amplitudes)

    def pack(first, outs):
        return small_call(
            functools.partial(pack_kernel, geometry, first),
            outs,
            [IN_HBM],
            limit=8 * MIB,
            scratch=(pltpu.SemaphoreType.DMA((3,)),),
        )(tile_hbm)

    strip = shape(2, margin, tile_cols)
    straight = swap_rows(pack(True, [strip])[0], 0)
    packed, *edges = pack(False, [strip] + [shape(2, tile_rows, margin)] * sides)
    diagonal = swap_rows(packed, 1)
    halos = swap_sides(edges)

    own = jnp.concatenate(
        [scan_offsets[0, 0], jnp.broadcast_to(scan_counts[0], (1, slots))], axis=0
    )
    stacked = jnp.stack([own, swap_rows(own, 0), swap_rows(own, 1)])
    beside = swap_sides([stacked] * sides)

    ext, acc, sums, *consts = run_interior(
        geometry, scan_offsets, scan_counts, tile_hbm, probe_hbm, amps_hbm, tables, halos
    )

    cut = small_call(
        functools.partial(corner_kernel, geometry),
        [shape(2, 2, margin, margin)] * sides,
        [IN_VMEM] * 2,
    )(straight, diagonal)
    corners = swap_sides(cut)

    _, _, _, mid, *rest = run_boundary(
        geometry, scan_offsets, scan_counts, straight, diagonal, corners, consts, ext, acc, sums
    )
    overs, side_outs, (keep, send) = rest[:2], rest[2 : 2 + sides], rest[2 + sides :]

    parts = [keep]
    for number, stage in enumerate(stages):
        axis, bits = stage
        if number:
            mine, *pieces = combine(stage, parts, 1 << len(bits))
        else:
            mine, pieces = keep, [send]
        parts = [mine] + [
            lax.ppermute(piece, axis, member_perm(axis, bits, member + 1))
            for member, piece in enumerate(pieces)
        ]
    total = combine(last, parts, 1)[0]
    parts = [total, lax.ppermute(total, last[0], member_perm(*last, 1))]

    received = swap_sides(side_outs)
    strip = shape(tiles, 2, margin, LANES)
    chunk = shape(tiles // 2, 2, margin, LANES)
    out_straight, out_low, out_high = small_call(
        functools.partial(fold_kernel, geometry),
        [strip, chunk, chunk],
        [IN_VMEM] * (2 + sides),
        scratch=(VMEM(strip.shape, F32),),
    )(*overs, *received)
    from_straight = swap_rows(out_straight, 0)
    from_low = swap_rows(out_low, 1)
    from_high = swap_rows(out_high, 1)

    flat = probe_modes.reshape(2 * modes, edge, edge)
    shard = finish(stages, flat, parts)
    for number, stage in reversed(list(enumerate(stages))):
        axis, bits = stage
        pieces = [shard] + [
            lax.ppermute(shard, axis, member_perm(axis, bits, member))
            for member in range(1, 1 << len(bits))
        ]
        shard = place(stage, pieces)
    probe_new = shard.reshape(probe_modes.shape)

    light = small_call(
        functools.partial(light_kernel, geometry),
        [shape(tiles, tile_rows, LANES)],
        [IN_SMEM] * (2 + sides) + [IN_VMEM],
        limit=8 * MIB,
        scratch=(VMEM((tiles + 2 * (edge // LANES), 1, tile_rows + 2 * edge, LANES), F32),),
        cost=10_000_000,
    )(own, stacked[1:], *beside, probe_modes)[0]
    object_new = small_call(
        functools.partial(object_kernel, geometry),
        [shape(2, tile_rows, tile_cols)],
        [IN_HBM, ANYWHERE] + [IN_VMEM] * (4 + sides),
        limit=8 * MIB,
        scratch=(
            VMEM((tiles, 2, tile_rows, LANES), F32),
            VMEM((tiles, 2, tile_rows, LANES), F32),
            pltpu.SemaphoreType.DMA((2 * tiles,)),
            pltpu.SemaphoreType.DMA((tiles,)),
        ),
        out_specs=[IN_HBM],
    )(object_field, mid, light, from_straight, from_low, from_high, *received)[0]
    return object_new, probe_new


def solution(mesh):
    in_specs = (
        P(None, "row", "col"),
        P(),
        P("row", "col", None, None),
        P("row", "col"),
        P("row", "col", None, None, None),
    )
    out_specs = (P(None, "row", "col"), P())
    return jax.shard_map(step, mesh=mesh, in_specs=in_specs, out_specs=out_specs, check_vma=False)
```

```python
import functools
import math

import jax
import jax.numpy as jnp
import numpy as np
from jax import lax
from jax.experimental import pallas as pl
from jax.experimental.pallas import tpu as pltpu
from jax.sharding import PartitionSpec as P


F32 = jnp.float32
BF16 = jnp.bfloat16
LANES = 128


def split_host(table):
    high = table.astype(BF16)
    low = (table - high.astype(np.float64)).astype(BF16)
    return high, low


def dft_tables(edge):
    half = edge // 2
    scale = 1.0 / math.sqrt(edge)
    n = np.arange(half)[:, None]
    k = np.arange(half)[None, :]
    mats = []
    for parity in (0, 1):
        angle = (n * (2 * k + parity) % edge) * (2.0 * np.pi / edge)
        cosine, sine = np.cos(angle) * scale, np.sin(angle) * scale
        mats.append(np.block([[cosine, -sine], [sine, cosine]]))
    mats += [mats[0].T, mats[1].T]
    return np.stack([np.stack(split_host(m)) for m in mats])


def split_parts(x):
    high = x.astype(BF16)
    low = (x - high.astype(F32)).astype(BF16)
    return high, low


def right_dot(x, table):
    high, low = split_parts(x)
    return jnp.dot(jnp.concatenate([high, low, high], axis=1), table, preferred_element_type=F32)


def left_dot(table, x):
    high, low = split_parts(x)
    return jnp.dot(table, jnp.concatenate([high, low, high], axis=0), preferred_element_type=F32)


VMEM = pltpu.VMEM
ANYWHERE = pl.BlockSpec(memory_space=pl.ANY)
IN_VMEM = pl.BlockSpec(memory_space=pltpu.VMEM)
IN_SMEM = pl.BlockSpec(memory_space=pltpu.SMEM)
MIB = 1024 * 1024
IN_HBM = pl.BlockSpec(memory_space=pltpu.HBM)


def in_hbm(x):
    return pltpu.with_memory_space_constraint(x, pltpu.HBM)


def shape(*dims):
    return jax.ShapeDtypeStruct(dims, F32)


def aligned(start, size):
    return pl.ds(pl.multiple_of(start, size) if size % 8 == 0 else start, size)


def copy_all(pairs, sems):
    copies = []
    for number, (src, dst) in enumerate(pairs):
        copy = pltpu.make_async_copy(src, dst, sems.at[number])
        copy.start()
        copies.append(copy)
    return copies


class Frame:
    def __init__(self, tile_rows, tile_cols, margin, sides):
        self.tile_rows, self.tile_cols, self.margin, self.sides = tile_rows, tile_cols, margin, sides
        self.tiles = tile_cols // LANES
        self.row = lax.axis_index("row")
        self.col = lax.axis_index("col")
        self.body = pl.ds(margin, tile_rows)

    def side_is_east(self, number):
        if self.sides == 2:
            return jnp.int32(number)
        return 1 - (self.col & 1)

    def side_block(self, number):
        return self.side_is_east(number) * (self.tiles + 1)

    def side_target(self, number):
        return 1 + self.side_is_east(number) * (self.tiles - 1)

    def side_cols(self, number):
        start = self.side_is_east(number) * (self.tile_cols - self.margin)
        return pl.ds(pl.multiple_of(start, LANES), self.margin)

    def is_below(self, number):
        return jnp.bitwise_xor(1 - (self.row & 1), number)

    def strip_rows(self, number):
        start = self.is_below(number) * (self.tile_rows - self.margin)
        return pl.ds(pl.multiple_of(start, self.margin), self.margin)

    def halo_rows(self, number):
        start = self.is_below(number) * (self.tile_rows + self.margin)
        return pl.ds(pl.multiple_of(start, self.margin), self.margin)

    def place_of(self, offsets, slot):
        return (
            offsets[0, 0, 0, slot] - self.row * self.tile_rows + self.margin,
            offsets[0, 0, 1, slot] - self.col * self.tile_cols + self.margin,
        )


def small_call(kernel, outs, in_specs, limit=4 * MIB, scratch=(), out_specs=None, aliases=None, cost=None):
    return pl.pallas_call(
        kernel,
        out_shape=outs,
        in_specs=in_specs,
        out_specs=out_specs if out_specs is not None else [IN_VMEM] * len(outs),
        scratch_shapes=list(scratch),
        input_output_aliases=aliases or {},
        compiler_params=pltpu.CompilerParams(vmem_limit_bytes=limit),
        cost_estimate=pl.CostEstimate(flops=cost, bytes_accessed=1_000_000, transcendentals=0) if cost else None,
    )


def pack_kernel(geometry, first, tile, *refs):
    outs, sems = refs[:-1], refs[-1]
    frame = Frame(*geometry)
    pairs = [(tile.at[:, frame.strip_rows(0 if first else 1), :], outs[0])]
    for number, side in enumerate(outs[1:]):
        pairs.append((tile.at[:, :, frame.side_cols(number)], side))
    for copy in copy_all(pairs, sems):
        copy.wait()


def add_window(acc, channel, parts, row, block, shift):
    edge = parts[0].shape[0]
    lane = lax.broadcasted_iota(jnp.int32, (edge, LANES), 1)
    keep = lane >= shift
    first = pltpu.roll(parts[0], shift, 1)
    second = pltpu.roll(parts[1], shift, 1)
    rows = pl.ds(row, edge)
    zero = jnp.zeros_like(first)
    last = jnp.minimum(block + 2, acc.shape[0] - 1)
    acc[block, channel, rows, :] += jnp.where(keep, first, zero)
    acc[block + 1, channel, rows, :] += jnp.where(keep, second, first)
    acc[last, channel, rows, :] += jnp.where(keep, zero, second)


def slot_stages(slot, row, col, ext, acc, sums, probe, amps, rights, lefts):
    edge = probe.shape[-1]
    modes = probe.shape[1]
    half = edge // 2
    block = col // LANES
    shift = col - block * LANES
    lane = lax.broadcasted_iota(jnp.int32, (edge, LANES), 1)
    back_shift = lax.rem(LANES - shift, LANES)
    keep = lane < LANES - shift
    last = jnp.minimum(block + 2, ext.shape[0] - 1)
    patch = []
    for c in range(2):
        rolled = [
            pltpu.roll(ext[b, c, pl.ds(row, edge), :], back_shift, 1) for b in (block, block + 1, last)
        ]
        patch.append([jnp.where(keep, rolled[t], rolled[t + 1]) for t in range(2)])

    def probe_at(c, k, t):
        return probe[c, k, :, pl.ds(t * LANES, LANES)]

    def both_modes(parts):
        return jnp.concatenate(parts, axis=0)

    yield
    plus, minus = [], []
    for k in range(modes):
        re = [probe_at(0, k, t) * patch[0][t] - probe_at(1, k, t) * patch[1][t] for t in range(2)]
        im = [probe_at(0, k, t) * patch[1][t] + probe_at(1, k, t) * patch[0][t] for t in range(2)]
        plus.append(jnp.concatenate([re[0] + re[1], im[0] + im[1]], axis=1))
        minus.append(jnp.concatenate([re[0] - re[1], im[0] - im[1]], axis=1))
    even = right_dot(both_modes(plus), rights[0])
    yield
    odd = right_dot(both_modes(minus), rights[1])
    yield
    far = []
    for k in range(modes):
        rows = slice(k * edge, (k + 1) * edge)
        re = jnp.concatenate([even[rows, :half], odd[rows, :half]], axis=1)
        im = jnp.concatenate([even[rows, half:], odd[rows, half:]], axis=1)
        plus = jnp.concatenate([re[:half] + re[half:], im[:half] + im[half:]], axis=0)
        minus = jnp.concatenate([re[:half] - re[half:], im[:half] - im[half:]], axis=0)
        far.append([left_dot(lefts[0], plus), left_dot(lefts[1], minus)])
        yield
    factor = []
    for p in range(2):
        total = sum(
            far[k][p][:half] * far[k][p][:half] + far[k][p][half:] * far[k][p][half:]
            for k in range(modes)
        )
        amp = amps[slot, pl.ds(p * half, half), :].astype(F32)
        one = amp * lax.rsqrt(jnp.maximum(total, 0.25)) - 1.0
        factor.append(jnp.concatenate([one, one], axis=0))
    yield
    evens, odds = [], []
    for k in range(modes):
        even = left_dot(lefts[2], far[k][0] * factor[0])
        odd = left_dot(lefts[3], far[k][1] * factor[1])
        plus, minus = even + odd, even - odd
        re = jnp.concatenate([plus[:half], minus[:half]], axis=0)
        im = jnp.concatenate([plus[half:], minus[half:]], axis=0)
        evens.append(jnp.concatenate([re[:, :half], im[:, :half]], axis=1))
        odds.append(jnp.concatenate([re[:, half:], im[:, half:]], axis=1))
        yield
    even = right_dot(both_modes(evens), rights[2])
    yield
    odd = right_dot(both_modes(odds), rights[3])
    plus, minus = even + odd, even - odd
    yield
    update = [[None, None], [None, None]]
    for k in range(modes):
        rows = slice(k * edge, (k + 1) * edge)
        back_re = [plus[rows, :half], minus[rows, :half]]
        back_im = [plus[rows, half:], minus[rows, half:]]
        for t in range(2):
            pr, pi = probe_at(0, k, t), probe_at(1, k, t)
            u_re = pr * back_re[t] + pi * back_im[t]
            u_im = pr * back_im[t] - pi * back_re[t]
            update[0][t] = u_re if k == 0 else update[0][t] + u_re
            update[1][t] = u_im if k == 0 else update[1][t] + u_im
            lanes = pl.ds(t * LANES, LANES)
            xr, xi = patch[0][t], patch[1][t]
            sums[k, :, lanes] += xr * back_re[t] + xi * back_im[t]
            sums[modes + k, :, lanes] += xr * back_im[t] - xi * back_re[t]
        yield
    for t in range(2):
        lanes = pl.ds(t * LANES, LANES)
        power = patch[0][t] * patch[0][t] + patch[1][t] * patch[1][t]
        sums[2 * modes, :, lanes] += power
    for c in range(2):
        add_window(acc, c, update[c], row, block, shift)


def run_stages(works, lag):
    pending = [(number * lag, work) for number, work in enumerate(works)]
    turn = 0
    while pending:
        kept = []
        for start, work in pending:
            if turn >= start and next(work, work) is work:
                continue
            kept.append((start, work))
        pending = kept
        turn += 1


def slot_body(slot, row, col, *refs):
    run_stages([slot_stages(slot, row, col, *refs)], 0)


def interior_kernel(geometry, offsets, counts, tile, probe_in, amps_in, tables, *refs):
    frame = Frame(*geometry)
    halos = refs[: frame.sides]
    ext, acc, sums, probe, amps, rights, lefts, raw, sems = refs[frame.sides :]
    tiles, body, margin = frame.tiles, frame.body, frame.margin
    edge = probe.shape[-1]
    pairs = [(amps_in.at[0, 0], raw), (probe_in, probe)]
    for m in range(4):
        for third, part in enumerate((0, 0, 1)):
            span = pl.ds(third * edge, edge)
            pairs.append((tables.at[m, part], rights.at[m, span, :]))
            pairs.append((tables.at[(m + 2) % 4, part], lefts.at[m, :, span]))
    for number, halo in enumerate(halos):
        pairs.append((halo, ext.at[frame.side_block(number), :, body, :]))
    for t in range(tiles):
        pairs.append((tile.at[:, :, pl.ds(t * LANES, LANES)], ext.at[1 + t, :, body, :]))
    copies = copy_all(pairs, sems)
    acc[...] = jnp.zeros_like(acc)
    sums[...] = jnp.zeros_like(sums)
    copies[0].wait()
    out_at = lax.broadcasted_iota(jnp.int32, (edge, edge), 0)
    in_at = lax.broadcasted_iota(jnp.int32, (edge, edge), 1)
    source = jnp.where(out_at < edge // 2, 2 * out_at, 2 * out_at - edge + 1)
    pick = jnp.where(in_at == source, 1.0, 0.0).astype(BF16)

    def reorder(slot, carry):
        half_way = jnp.dot(pick, raw[slot], preferred_element_type=F32).astype(BF16)
        amps[slot] = lax.dot_general(
            half_way, pick, (((1,), (1,)), ((), ())), preferred_element_type=F32
        ).astype(BF16)
        return carry

    lax.fori_loop(0, counts[0, 0], reorder, 0)
    for copy in copies[1:]:
        copy.wait()

    def visit(slot, carry):
        row, col = frame.place_of(offsets, slot)

        @pl.when(jnp.logical_and(row >= margin, row + edge <= margin + frame.tile_rows))
        def _():
            slot_body(slot, row, col, ext, acc, sums, probe, amps, rights, lefts)

        return carry

    lax.fori_loop(0, counts[0, 0], visit, 0)


def boundary_kernel(geometry, offsets, counts, straight, diagonal, *refs):
    frame = Frame(*geometry)
    sides = frame.sides
    corners, refs = refs[:sides], refs[sides:]
    probe, amps, rights, lefts = refs[:4]
    ext, acc, sums, mid, over_straight, over_diagonal = refs[7:13]
    side_outs, refs = refs[13 : 13 + sides], refs[13 + sides :]
    keep, send, todo, sems = refs
    tiles, margin, body = frame.tiles, frame.margin, frame.body
    edge = probe.shape[-1]
    pairs = []
    for number, halo in enumerate((straight, diagonal)):
        for t in range(tiles):
            pairs.append(
                (halo.at[:, :, pl.ds(t * LANES, LANES)], ext.at[1 + t, :, frame.halo_rows(number), :])
            )
        for side, corner in enumerate(corners):
            pairs.append(
                (corner.at[number], ext.at[frame.side_block(side), :, frame.halo_rows(number), :])
            )
    for copy in copy_all(pairs, sems):
        copy.wait()

    def note(slot, found):
        row, _ = frame.place_of(offsets, slot)
        chosen = jnp.logical_or(row < margin, row + edge > margin + frame.tile_rows)
        todo[found] = slot
        return found + chosen.astype(jnp.int32)

    found = lax.fori_loop(0, counts[0, 0], note, jnp.int32(0))

    shared = (ext, acc, sums, probe, amps, rights, lefts)

    def visit(pair, carry):
        works = []
        for member in range(2):
            slot = todo[2 * pair + member]
            row, col = frame.place_of(offsets, slot)
            works.append(slot_stages(slot, row, col, *shared))
        run_stages(works, LAG)
        return carry

    lax.fori_loop(0, lax.div(found, 2), visit, 0)

    @pl.when(lax.rem(found, 2) == 1)
    def _():
        slot = todo[found - 1]
        row, col = frame.place_of(offsets, slot)
        slot_body(slot, row, col, *shared)

    out = [(acc.at[1 + t, :, body, :], mid.at[t]) for t in range(tiles)]
    copies = copy_all(out, sems)
    rows = keep.shape[1]
    index = frame.col & 1
    keep[...] = sums[:, aligned(index * rows, rows), :]
    send[...] = sums[:, aligned((1 - index) * rows, rows), :]
    for side, side_out in enumerate(side_outs):
        side_out[...] = acc[frame.side_block(side)]
    for number, over in enumerate((over_straight, over_diagonal)):
        for t in range(tiles):
            over[t] = acc[1 + t, :, frame.halo_rows(number), :]
    for copy in copies:
        copy.wait()


def corner_kernel(geometry, straight, diagonal, *outs):
    frame = Frame(*geometry)
    for side, out in enumerate(outs):
        out[0] = straight[:, :, frame.side_cols(side)]
        out[1] = diagonal[:, :, frame.side_cols(side)]


KERNEL_VMEM = 20 * MIB
LAG = 4
SLOT_COST = dict(
    cost_estimate=pl.CostEstimate(flops=int(1e10), bytes_accessed=20_000_000, transcendentals=0),
)


def run_interior(geometry, offsets, counts, tile, probe, amps, tables, halos):
    tile_rows, tile_cols, margin, sides = geometry
    edge = probe.shape[-1]
    modes = probe.shape[1]
    window = shape(tile_cols // LANES + 2, 2, tile_rows + 2 * margin, LANES)
    amp_shape = jax.ShapeDtypeStruct(amps.shape[2:], BF16)
    outs = [window, window, shape(2 * modes + 1, edge, edge), shape(*probe.shape), amp_shape]
    outs += [
        jax.ShapeDtypeStruct((4, 3 * edge, edge), BF16),
        jax.ShapeDtypeStruct((4, edge, 3 * edge), BF16),
    ]
    return pl.pallas_call(
        functools.partial(interior_kernel, geometry),
        out_shape=outs,
        in_specs=[IN_SMEM] * 2 + [IN_HBM] * 4 + [ANYWHERE] * sides,
        out_specs=[IN_VMEM] * len(outs),
        scratch_shapes=[
            VMEM(amp_shape.shape, BF16),
            pltpu.SemaphoreType.DMA((26 + sides + tile_cols // LANES,)),
        ],
        compiler_params=pltpu.CompilerParams(vmem_limit_bytes=KERNEL_VMEM),
        name="slots_interior",
        **SLOT_COST,
    )(offsets, counts, tile, probe, amps, tables, *halos)


def run_boundary(geometry, offsets, counts, straight, diagonal, corners, consts, ext, acc, sums):
    tile_rows, tile_cols, margin, sides = geometry
    planes, edge = sums.shape[:2]
    tiles = tile_cols // LANES
    part = shape(planes, edge // 2, edge)
    strip = shape(tiles, 2, margin, LANES)
    outs = [shape(*ext.shape), shape(*acc.shape), shape(*sums.shape)]
    outs += [shape(tiles, 2, tile_rows, LANES), strip, strip]
    outs += [shape(*acc.shape[1:])] * sides + [part, part]
    base = 4 + sides + 4
    return pl.pallas_call(
        functools.partial(boundary_kernel, geometry),
        out_shape=outs,
        in_specs=[IN_SMEM] * 2 + [ANYWHERE] * (2 + sides) + [IN_VMEM] * 7,
        out_specs=[IN_VMEM] * 3 + [IN_HBM] + [IN_VMEM] * (len(outs) - 4),
        scratch_shapes=[pltpu.SMEM((8,), jnp.int32), pltpu.SemaphoreType.DMA((16,))],
        input_output_aliases={base: 0, base + 1: 1, base + 2: 2},
        compiler_params=pltpu.CompilerParams(vmem_limit_bytes=KERNEL_VMEM),
        name="slots_boundary",
        **SLOT_COST,
    )(offsets, counts, straight, diagonal, *corners, *consts, ext, acc, sums)


def fold_kernel(geometry, over_straight, over_diagonal, *refs):
    frame = Frame(*geometry)
    received, (straight, low, high, diagonal) = refs[: frame.sides], refs[frame.sides :]
    for number, (over, out) in enumerate(((over_straight, straight), (over_diagonal, diagonal))):
        out[...] = over[...]
        for side, value in enumerate(received):
            out[frame.side_target(side) - 1] += value[:, frame.halo_rows(number), :]
    low[...] = diagonal[pl.ds(0, low.shape[0])]
    high[...] = diagonal[pl.ds(low.shape[0], low.shape[0])]


def light_kernel(geometry, own, *refs):
    frame = Frame(*geometry)
    others, (probe, out, canvas) = refs[:-3], refs[-3:]
    tiles = frame.tiles
    edge = probe.shape[-1]
    modes = probe.shape[1]
    canvas[...] = jnp.zeros_like(canvas)
    power = [
        sum(
            probe[c, k, :, pl.ds(t * LANES, LANES)] * probe[c, k, :, pl.ds(t * LANES, LANES)]
            for c in range(2)
            for k in range(modes)
        )
        for t in range(2)
    ]

    def add_from(read):
        def visit(slot, carry):
            row = read(0, slot) - frame.row * frame.tile_rows + edge
            col = read(1, slot) - frame.col * frame.tile_cols + edge
            meets = (row > 0) & (row < frame.tile_rows + edge) & (col > 0) & (col < frame.tile_cols + edge)

            @pl.when(meets)
            def _():
                block = col // LANES
                add_window(canvas, 0, power, row, block, col - block * LANES)

            return carry

        lax.fori_loop(0, read(2, 0), visit, 0)

    add_from(lambda plane, slot: own[plane, slot])
    for other in others:
        if len(other.shape) == 2:
            add_from(lambda plane, slot, other=other: other[plane, slot])
        else:
            for tile in range(other.shape[0]):
                add_from(lambda plane, slot, other=other, tile=tile: other[tile, plane, slot])
    for t in range(tiles):
        out[t] = canvas[edge // LANES + t, 0, pl.ds(edge, frame.tile_rows), :]


def object_kernel(geometry, tile, mid, light, from_straight, from_low, from_high, *refs):
    frame = Frame(*geometry)
    received, (out, old, stage, sems_in, sems_out) = refs[: frame.sides], refs[frame.sides :]
    tiles = frame.tiles
    loads = []
    for t in range(tiles):
        loads.append(
            (
                pltpu.make_async_copy(
                    tile.at[:, :, pl.ds(t * LANES, LANES)], old.at[t], sems_in.at[2 * t]
                ),
                pltpu.make_async_copy(mid.at[t], stage.at[t], sems_in.at[2 * t + 1]),
            )
        )
        for copy in loads[-1]:
            copy.start()
    copies = []
    for t in range(tiles):
        for copy in loads[t]:
            copy.wait()
        for side, value in enumerate(received):

            @pl.when(frame.side_target(side) == 1 + t)
            def _(value=value, t=t):
                stage[t] += value[:, frame.body, :]

        stage[t, :, frame.strip_rows(0), :] += from_straight[t]
        half = from_low.shape[0]
        stage[t, :, frame.strip_rows(1), :] += from_low[t] if t < half else from_high[t - half]
        scale = 1.0 / (light[t] + 1.0)
        for c in range(2):
            stage[t, c] = old[t, c] + stage[t, c] * scale
        copy = pltpu.make_async_copy(
            stage.at[t], out.at[:, :, pl.ds(t * LANES, LANES)], sems_out.at[t]
        )
        copy.start()
        copies.append(copy)
    for copy in copies:
        copy.wait()


def member_perm(axis, bits, member):
    mask = sum(((member >> position) & 1) << bit for position, bit in enumerate(bits))
    return [(i, i ^ mask) for i in range(lax.axis_size(axis))]


def member_index(axis, bits):
    where = lax.axis_index(axis)
    return sum(((where >> bit) & 1) << position for position, bit in enumerate(bits))


def combine_kernel(inputs, stage, *refs):
    ins, outs = refs[:inputs], refs[inputs:]
    rows = outs[0].shape[1]
    for member, out in enumerate(outs):
        part = slice(None)
        if len(outs) > 1:
            part = aligned(jnp.bitwise_xor(member_index(*stage), member) * rows, rows)
        value = ins[0][:, part, :]
        for other in ins[1:]:
            value = value + other[:, part, :]
        out[...] = value


def combine(stage, parts, group):
    planes, rows, cols = parts[0].shape
    if (rows // group) % 8:
        total = sum(parts[1:], parts[0])
        if group == 1:
            return [total]
        rows = rows // group
        return [
            lax.dynamic_slice_in_dim(
                total, jnp.bitwise_xor(member_index(*stage), m) * rows, rows, axis=1
            )
            for m in range(group)
        ]
    return small_call(
        functools.partial(combine_kernel, len(parts), stage),
        [shape(planes, rows // group, cols)] * group,
        [IN_VMEM] * len(parts),
    )(*parts)


def place_kernel(group, stage, *refs):
    ins, out = refs[:group], refs[group]
    rows = ins[0].shape[1]
    for member, piece in enumerate(ins):
        at = jnp.bitwise_xor(member_index(*stage), member) * rows
        out[:, aligned(at, rows), :] = piece[...]


def place(stage, parts):
    planes, rows, cols = parts[0].shape
    if rows % 8:
        whole = jnp.zeros((planes, rows * len(parts), cols), F32)
        for m, piece in enumerate(parts):
            at = jnp.bitwise_xor(member_index(*stage), m) * rows
            whole = lax.dynamic_update_slice_in_dim(whole, piece, at, axis=1)
        return whole
    return small_call(
        functools.partial(place_kernel, len(parts), stage),
        [shape(planes, rows * len(parts), cols)],
        [IN_VMEM] * len(parts),
    )(*parts)[0]


def shard_start(stages, edge):
    start, rows = jnp.int32(0), edge
    for axis, bits in stages:
        rows = rows >> len(bits)
        start = start + member_index(axis, bits) * rows
    return start


def finish_kernel(stages, edge, probe, *refs):
    ins, out = refs[:-1], refs[-1]
    total = ins[0][...]
    for other in ins[1:]:
        total = total + other[...]
    planes, rows = out.shape[:2]
    old = probe[:, aligned(shard_start(stages, edge), rows), :]
    out[...] = old + total[:planes] / (total[planes:] + 1.0)


def finish(stages, probe, parts):
    planes, rows, cols = parts[0].shape
    edge = probe.shape[1]
    if rows % 8:
        total = sum(parts[1:], parts[0])
        old = lax.dynamic_slice_in_dim(probe, shard_start(stages, edge), rows, axis=1)
        return old + total[:-1] / (total[-1:] + 1.0)
    return small_call(
        functools.partial(finish_kernel, stages, edge),
        [shape(planes - 1, rows, cols)],
        [IN_VMEM] * (1 + len(parts)),
    )(probe, *parts)[0]


def swap_sides(outs):
    count = lax.axis_size("col")
    if len(outs) == 1:
        return [lax.ppermute(outs[0], "col", [(0, 1), (1, 0)])]
    up = [(i, i + 1) for i in range(count - 1)]
    down = [(i + 1, i) for i in range(count - 1)]
    return [lax.ppermute(outs[1], "col", up), lax.ppermute(outs[0], "col", down)]


def swap_rows(value, number):
    count = lax.axis_size("row")
    pairs = []
    for low in range(number, count - 1, 2):
        pairs += [(low, low + 1), (low + 1, low)]
    return lax.ppermute(value, "row", pairs)


def stages_of(rows, cols):
    stages = [("col", (bit,)) for bit in range(cols.bit_length() - 1)]
    bits = list(range(1, rows.bit_length() - 1)) + [0]
    while bits:
        stages.append(("row", tuple(bits[:2])))
        bits = bits[2:]
    return tuple(stages)


def step(object_field, probe_modes, scan_offsets, scan_counts, amplitudes):
    tile_rows, tile_cols = object_field.shape[1:]
    modes = probe_modes.shape[1]
    edge = probe_modes.shape[-1]
    margin = edge // 2
    slots = amplitudes.shape[2]
    tiles = tile_cols // LANES
    sides = 1 if lax.axis_size("col") == 2 else 2
    geometry = (tile_rows, tile_cols, margin, sides)
    stages = stages_of(lax.axis_size("row"), lax.axis_size("col"))
    tables = in_hbm(jnp.asarray(dft_tables(edge)))
    tile_hbm, probe_hbm, amps_hbm = in_hbm(object_field), in_hbm(probe_modes), in_hbm(amplitudes)

    def pack(first, outs):
        return small_call(
            functools.partial(pack_kernel, geometry, first),
            outs,
            [IN_HBM],
            limit=8 * MIB,
            scratch=(pltpu.SemaphoreType.DMA((3,)),),
        )(tile_hbm)

    strip = shape(2, margin, tile_cols)
    straight = swap_rows(pack(True, [strip])[0], 0)
    packed, *edges = pack(False, [strip] + [shape(2, tile_rows, margin)] * sides)
    diagonal = swap_rows(packed, 1)
    halos = swap_sides(edges)

    own = jnp.concatenate(
        [scan_offsets[0, 0], jnp.broadcast_to(scan_counts[0], (1, slots))], axis=0
    )
    stacked = jnp.stack([own, swap_rows(own, 0), swap_rows(own, 1)])
    beside = swap_sides([stacked] * sides)

    ext, acc, sums, *consts = run_interior(
        geometry, scan_offsets, scan_counts, tile_hbm, probe_hbm, amps_hbm, tables, halos
    )

    cut = small_call(
        functools.partial(corner_kernel, geometry),
        [shape(2, 2, margin, margin)] * sides,
        [IN_VMEM] * 2,
    )(straight, diagonal)
    corners = swap_sides(cut)

    _, _, _, mid, *rest = run_boundary(
        geometry, scan_offsets, scan_counts, straight, diagonal, corners, consts, ext, acc, sums
    )
    overs, side_outs, (keep, send) = rest[:2], rest[2 : 2 + sides], rest[2 + sides :]

    parts = [keep]
    for number, stage in enumerate(stages):
        axis, bits = stage
        if number:
            mine, *pieces = combine(stage, parts, 1 << len(bits))
        else:
            mine, pieces = keep, [send]
        parts = [mine] + [
            lax.ppermute(piece, axis, member_perm(axis, bits, member + 1))
            for member, piece in enumerate(pieces)
        ]
    received = swap_sides(side_outs)
    strip = shape(tiles, 2, margin, LANES)
    chunk = shape(tiles // 2, 2, margin, LANES)
    out_straight, out_low, out_high = small_call(
        functools.partial(fold_kernel, geometry),
        [strip, chunk, chunk],
        [IN_VMEM] * (2 + sides),
        scratch=(VMEM(strip.shape, F32),),
    )(*overs, *received)
    from_straight = swap_rows(out_straight, 0)
    from_low = swap_rows(out_low, 1)
    from_high = swap_rows(out_high, 1)

    flat = probe_modes.reshape(2 * modes, edge, edge)
    shard = finish(stages, flat, parts)
    for number, stage in reversed(list(enumerate(stages))):
        axis, bits = stage
        pieces = [shard] + [
            lax.ppermute(shard, axis, member_perm(axis, bits, member))
            for member in range(1, 1 << len(bits))
        ]
        shard = place(stage, pieces)
    probe_new = shard.reshape(probe_modes.shape)

    light = small_call(
        functools.partial(light_kernel, geometry),
        [shape(tiles, tile_rows, LANES)],
        [IN_SMEM] * (2 + sides) + [IN_VMEM],
        limit=8 * MIB,
        scratch=(VMEM((tiles + 2 * (edge // LANES), 1, tile_rows + 2 * edge, LANES), F32),),
        cost=10_000_000,
    )(own, stacked[1:], *beside, probe_modes)[0]
    object_new = small_call(
        functools.partial(object_kernel, geometry),
        [shape(2, tile_rows, tile_cols)],
        [IN_HBM, ANYWHERE] + [IN_VMEM] * (4 + sides),
        limit=8 * MIB,
        scratch=(
            VMEM((tiles, 2, tile_rows, LANES), F32),
            VMEM((tiles, 2, tile_rows, LANES), F32),
            pltpu.SemaphoreType.DMA((2 * tiles,)),
            pltpu.SemaphoreType.DMA((tiles,)),
        ),
        out_specs=[IN_HBM],
    )(object_field, mid, light, from_straight, from_low, from_high, *received)[0]
    return object_new, probe_new


def solution(mesh):
    in_specs = (
        P(None, "row", "col"),
        P(),
        P("row", "col", None, None),
        P("row", "col"),
        P("row", "col", None, None, None),
    )
    out_specs = (P(None, "row", "col"), P())
    return jax.shard_map(step, mesh=mesh, in_specs=in_specs, out_specs=out_specs, check_vma=False)
```

```python
import functools
import math

import jax
import jax.numpy as jnp
import numpy as np
from jax import lax
from jax.experimental import pallas as pl
from jax.experimental.pallas import tpu as pltpu
from jax.sharding import PartitionSpec as P


F32 = jnp.float32
BF16 = jnp.bfloat16
LANES = 128


def split_host(table):
    high = table.astype(BF16)
    low = (table - high.astype(np.float64)).astype(BF16)
    return high, low


def dft_tables(edge):
    half = edge // 2
    scale = 1.0 / math.sqrt(edge)
    n = np.arange(half)[:, None]
    k = np.arange(half)[None, :]
    mats = []
    for parity in (0, 1):
        angle = (n * (2 * k + parity) % edge) * (2.0 * np.pi / edge)
        cosine, sine = np.cos(angle) * scale, np.sin(angle) * scale
        mats.append(np.block([[cosine, -sine], [sine, cosine]]))
    mats += [mats[0].T, mats[1].T]
    return np.stack([np.stack(split_host(m)) for m in mats])


def split_parts(x):
    high = x.astype(BF16)
    low = (x - high.astype(F32)).astype(BF16)
    return high, low


def right_dot(x, table):
    high, low = split_parts(x)
    return jnp.dot(jnp.concatenate([high, low, high], axis=1), table, preferred_element_type=F32)


def left_dot(table, x):
    high, low = split_parts(x)
    return jnp.dot(table, jnp.concatenate([high, low, high], axis=0), preferred_element_type=F32)


VMEM = pltpu.VMEM
ANYWHERE = pl.BlockSpec(memory_space=pl.ANY)
IN_VMEM = pl.BlockSpec(memory_space=pltpu.VMEM)
IN_SMEM = pl.BlockSpec(memory_space=pltpu.SMEM)
MIB = 1024 * 1024
IN_HBM = pl.BlockSpec(memory_space=pltpu.HBM)


def in_hbm(x):
    return pltpu.with_memory_space_constraint(x, pltpu.HBM)


def shape(*dims):
    return jax.ShapeDtypeStruct(dims, F32)


def aligned(start, size):
    return pl.ds(pl.multiple_of(start, size) if size % 8 == 0 else start, size)


def copy_all(pairs, sems):
    copies = []
    for number, (src, dst) in enumerate(pairs):
        copy = pltpu.make_async_copy(src, dst, sems.at[number])
        copy.start()
        copies.append(copy)
    return copies


class Frame:
    def __init__(self, tile_rows, tile_cols, margin, sides):
        self.tile_rows, self.tile_cols, self.margin, self.sides = tile_rows, tile_cols, margin, sides
        self.tiles = tile_cols // LANES
        self.row = lax.axis_index("row")
        self.col = lax.axis_index("col")
        self.body = pl.ds(margin, tile_rows)

    def side_is_east(self, number):
        if self.sides == 2:
            return jnp.int32(number)
        return 1 - (self.col & 1)

    def side_block(self, number):
        return self.side_is_east(number) * (self.tiles + 1)

    def side_target(self, number):
        return 1 + self.side_is_east(number) * (self.tiles - 1)

    def side_cols(self, number):
        start = self.side_is_east(number) * (self.tile_cols - self.margin)
        return pl.ds(pl.multiple_of(start, LANES), self.margin)

    def is_below(self, number):
        return jnp.bitwise_xor(1 - (self.row & 1), number)

    def strip_rows(self, number):
        start = self.is_below(number) * (self.tile_rows - self.margin)
        return pl.ds(pl.multiple_of(start, self.margin), self.margin)

    def halo_rows(self, number):
        start = self.is_below(number) * (self.tile_rows + self.margin)
        return pl.ds(pl.multiple_of(start, self.margin), self.margin)

    def place_of(self, offsets, slot):
        return (
            offsets[0, 0, 0, slot] - self.row * self.tile_rows + self.margin,
            offsets[0, 0, 1, slot] - self.col * self.tile_cols + self.margin,
        )


def small_call(kernel, outs, in_specs, limit=4 * MIB, scratch=(), out_specs=None, aliases=None, cost=None):
    return pl.pallas_call(
        kernel,
        out_shape=outs,
        in_specs=in_specs,
        out_specs=out_specs if out_specs is not None else [IN_VMEM] * len(outs),
        scratch_shapes=list(scratch),
        input_output_aliases=aliases or {},
        compiler_params=pltpu.CompilerParams(vmem_limit_bytes=limit),
        cost_estimate=pl.CostEstimate(flops=cost, bytes_accessed=1_000_000, transcendentals=0) if cost else None,
    )


def pack_kernel(geometry, first, tile, *refs):
    outs, sems = refs[:-1], refs[-1]
    frame = Frame(*geometry)
    pairs = [(tile.at[:, frame.strip_rows(0 if first else 1), :], outs[0])]
    for number, side in enumerate(outs[1:]):
        pairs.append((tile.at[:, :, frame.side_cols(number)], side))
    for copy in copy_all(pairs, sems):
        copy.wait()


def add_window(acc, channel, parts, row, block, shift):
    edge = parts[0].shape[0]
    lane = lax.broadcasted_iota(jnp.int32, (edge, LANES), 1)
    keep = lane >= shift
    first = pltpu.roll(parts[0], shift, 1)
    second = pltpu.roll(parts[1], shift, 1)
    rows = pl.ds(row, edge)
    zero = jnp.zeros_like(first)
    last = jnp.minimum(block + 2, acc.shape[0] - 1)
    acc[block, channel, rows, :] += jnp.where(keep, first, zero)
    acc[block + 1, channel, rows, :] += jnp.where(keep, second, first)
    acc[last, channel, rows, :] += jnp.where(keep, zero, second)


def slot_stages(slot, row, col, ext, acc, sums, probe, amps, rights, lefts):
    edge = probe.shape[-1]
    modes = probe.shape[1]
    half = edge // 2
    block = col // LANES
    shift = col - block * LANES
    lane = lax.broadcasted_iota(jnp.int32, (edge, LANES), 1)
    back_shift = lax.rem(LANES - shift, LANES)
    keep = lane < LANES - shift
    last = jnp.minimum(block + 2, ext.shape[0] - 1)
    patch = []
    for c in range(2):
        rolled = [
            pltpu.roll(ext[b, c, pl.ds(row, edge), :], back_shift, 1) for b in (block, block + 1, last)
        ]
        patch.append([jnp.where(keep, rolled[t], rolled[t + 1]) for t in range(2)])

    def probe_at(c, k, t):
        return probe[c, k, :, pl.ds(t * LANES, LANES)]

    def both_modes(parts):
        return jnp.concatenate(parts, axis=0)

    yield
    plus, minus = [], []
    for k in range(modes):
        re = [probe_at(0, k, t) * patch[0][t] - probe_at(1, k, t) * patch[1][t] for t in range(2)]
        im = [probe_at(0, k, t) * patch[1][t] + probe_at(1, k, t) * patch[0][t] for t in range(2)]
        plus.append(jnp.concatenate([re[0] + re[1], im[0] + im[1]], axis=1))
        minus.append(jnp.concatenate([re[0] - re[1], im[0] - im[1]], axis=1))
    even = right_dot(both_modes(plus), rights[0])
    yield
    odd = right_dot(both_modes(minus), rights[1])
    yield
    far = []
    for k in range(modes):
        rows = slice(k * edge, (k + 1) * edge)
        re = jnp.concatenate([even[rows, :half], odd[rows, :half]], axis=1)
        im = jnp.concatenate([even[rows, half:], odd[rows, half:]], axis=1)
        plus = jnp.concatenate([re[:half] + re[half:], im[:half] + im[half:]], axis=0)
        minus = jnp.concatenate([re[:half] - re[half:], im[:half] - im[half:]], axis=0)
        far.append([left_dot(lefts[0], plus), left_dot(lefts[1], minus)])
        yield
    factor = []
    for p in range(2):
        total = sum(
            far[k][p][:half] * far[k][p][:half] + far[k][p][half:] * far[k][p][half:]
            for k in range(modes)
        )
        amp = amps[slot, pl.ds(p * half, half), :].astype(F32)
        one = amp * lax.rsqrt(jnp.maximum(total, 0.25)) - 1.0
        factor.append(jnp.concatenate([one, one], axis=0))
    yield
    evens, odds = [], []
    for k in range(modes):
        even = left_dot(lefts[2], far[k][0] * factor[0])
        odd = left_dot(lefts[3], far[k][1] * factor[1])
        plus, minus = even + odd, even - odd
        re = jnp.concatenate([plus[:half], minus[:half]], axis=0)
        im = jnp.concatenate([plus[half:], minus[half:]], axis=0)
        evens.append(jnp.concatenate([re[:, :half], im[:, :half]], axis=1))
        odds.append(jnp.concatenate([re[:, half:], im[:, half:]], axis=1))
        yield
    even = right_dot(both_modes(evens), rights[2])
    yield
    odd = right_dot(both_modes(odds), rights[3])
    plus, minus = even + odd, even - odd
    yield
    update = [[None, None], [None, None]]
    for k in range(modes):
        rows = slice(k * edge, (k + 1) * edge)
        back_re = [plus[rows, :half], minus[rows, :half]]
        back_im = [plus[rows, half:], minus[rows, half:]]
        for t in range(2):
            pr, pi = probe_at(0, k, t), probe_at(1, k, t)
            u_re = pr * back_re[t] + pi * back_im[t]
            u_im = pr * back_im[t] - pi * back_re[t]
            update[0][t] = u_re if k == 0 else update[0][t] + u_re
            update[1][t] = u_im if k == 0 else update[1][t] + u_im
            lanes = pl.ds(t * LANES, LANES)
            xr, xi = patch[0][t], patch[1][t]
            sums[k, :, lanes] += xr * back_re[t] + xi * back_im[t]
            sums[modes + k, :, lanes] += xr * back_im[t] - xi * back_re[t]
        yield
    for t in range(2):
        lanes = pl.ds(t * LANES, LANES)
        power = patch[0][t] * patch[0][t] + patch[1][t] * patch[1][t]
        sums[2 * modes, :, lanes] += power
    for c in range(2):
        add_window(acc, c, update[c], row, block, shift)


def run_stages(works, lag):
    pending = [(number * lag, work) for number, work in enumerate(works)]
    turn = 0
    while pending:
        kept = []
        for start, work in pending:
            if turn >= start and next(work, work) is work:
                continue
            kept.append((start, work))
        pending = kept
        turn += 1


def slot_body(slot, row, col, *refs):
    run_stages([slot_stages(slot, row, col, *refs)], 0)


def interior_kernel(geometry, offsets, counts, tile, probe_in, amps_in, tables, *refs):
    frame = Frame(*geometry)
    halos = refs[: frame.sides]
    ext, acc, sums, probe, amps, rights, lefts, raw, sems = refs[frame.sides :]
    tiles, body, margin = frame.tiles, frame.body, frame.margin
    edge = probe.shape[-1]
    pairs = [(amps_in.at[0, 0], raw), (probe_in, probe)]
    for m in range(4):
        for third, part in enumerate((0, 0, 1)):
            span = pl.ds(third * edge, edge)
            pairs.append((tables.at[m, part], rights.at[m, span, :]))
            pairs.append((tables.at[(m + 2) % 4, part], lefts.at[m, :, span]))
    for number, halo in enumerate(halos):
        pairs.append((halo, ext.at[frame.side_block(number), :, body, :]))
    for t in range(tiles):
        pairs.append((tile.at[:, :, pl.ds(t * LANES, LANES)], ext.at[1 + t, :, body, :]))
    copies = copy_all(pairs, sems)
    acc[...] = jnp.zeros_like(acc)
    sums[...] = jnp.zeros_like(sums)
    copies[0].wait()
    out_at = lax.broadcasted_iota(jnp.int32, (edge, edge), 0)
    in_at = lax.broadcasted_iota(jnp.int32, (edge, edge), 1)
    source = jnp.where(out_at < edge // 2, 2 * out_at, 2 * out_at - edge + 1)
    pick = jnp.where(in_at == source, 1.0, 0.0).astype(BF16)

    def reorder(slot, carry):
        half_way = jnp.dot(pick, raw[slot], preferred_element_type=F32).astype(BF16)
        amps[slot] = lax.dot_general(
            half_way, pick, (((1,), (1,)), ((), ())), preferred_element_type=F32
        ).astype(BF16)
        return carry

    lax.fori_loop(0, counts[0, 0], reorder, 0)
    for copy in copies[1:]:
        copy.wait()

    def visit(slot, carry):
        row, col = frame.place_of(offsets, slot)

        @pl.when(jnp.logical_and(row >= margin, row + edge <= margin + frame.tile_rows))
        def _():
            slot_body(slot, row, col, ext, acc, sums, probe, amps, rights, lefts)

        return carry

    lax.fori_loop(0, counts[0, 0], visit, 0)


def boundary_kernel(geometry, offsets, counts, straight, diagonal, *refs):
    frame = Frame(*geometry)
    sides = frame.sides
    corners, refs = refs[:sides], refs[sides:]
    probe, amps, rights, lefts = refs[:4]
    ext, acc, sums, mid, over_straight, over_diagonal = refs[7:13]
    side_outs, refs = refs[13 : 13 + sides], refs[13 + sides :]
    keep, send, todo, sems = refs
    tiles, margin, body = frame.tiles, frame.margin, frame.body
    edge = probe.shape[-1]
    pairs = []
    for number, halo in enumerate((straight, diagonal)):
        for t in range(tiles):
            pairs.append(
                (halo.at[:, :, pl.ds(t * LANES, LANES)], ext.at[1 + t, :, frame.halo_rows(number), :])
            )
        for side, corner in enumerate(corners):
            pairs.append(
                (corner.at[number], ext.at[frame.side_block(side), :, frame.halo_rows(number), :])
            )
    for copy in copy_all(pairs, sems):
        copy.wait()

    def note(slot, found):
        row, _ = frame.place_of(offsets, slot)
        chosen = jnp.logical_or(row < margin, row + edge > margin + frame.tile_rows)
        todo[found] = slot
        return found + chosen.astype(jnp.int32)

    found = lax.fori_loop(0, counts[0, 0], note, jnp.int32(0))

    shared = (ext, acc, sums, probe, amps, rights, lefts)

    def visit(pair, carry):
        works = []
        for member in range(2):
            slot = todo[2 * pair + member]
            row, col = frame.place_of(offsets, slot)
            works.append(slot_stages(slot, row, col, *shared))
        run_stages(works, LAG)
        return carry

    lax.fori_loop(0, lax.div(found, 2), visit, 0)

    @pl.when(lax.rem(found, 2) == 1)
    def _():
        slot = todo[found - 1]
        row, col = frame.place_of(offsets, slot)
        slot_body(slot, row, col, *shared)

    out = [(acc.at[1 + t, :, body, :], mid.at[t]) for t in range(tiles)]
    copies = copy_all(out, sems)
    rows = keep.shape[1]
    index = frame.col & 1
    keep[...] = sums[:, aligned(index * rows, rows), :]
    send[...] = sums[:, aligned((1 - index) * rows, rows), :]
    for side, side_out in enumerate(side_outs):
        side_out[...] = acc[frame.side_block(side)]
    for number, over in enumerate((over_straight, over_diagonal)):
        for t in range(tiles):
            over[t] = acc[1 + t, :, frame.halo_rows(number), :]
    for copy in copies:
        copy.wait()


def corner_kernel(geometry, straight, diagonal, *outs):
    frame = Frame(*geometry)
    for side, out in enumerate(outs):
        out[0] = straight[:, :, frame.side_cols(side)]
        out[1] = diagonal[:, :, frame.side_cols(side)]


KERNEL_VMEM = 20 * MIB
LAG = 4
SLOT_COST = dict(
    cost_estimate=pl.CostEstimate(flops=int(1e10), bytes_accessed=20_000_000, transcendentals=0),
)


def run_interior(geometry, offsets, counts, tile, probe, amps, tables, halos):
    tile_rows, tile_cols, margin, sides = geometry
    edge = probe.shape[-1]
    modes = probe.shape[1]
    window = shape(tile_cols // LANES + 2, 2, tile_rows + 2 * margin, LANES)
    amp_shape = jax.ShapeDtypeStruct(amps.shape[2:], BF16)
    outs = [window, window, shape(2 * modes + 1, edge, edge), shape(*probe.shape), amp_shape]
    outs += [
        jax.ShapeDtypeStruct((4, 3 * edge, edge), BF16),
        jax.ShapeDtypeStruct((4, edge, 3 * edge), BF16),
    ]
    return pl.pallas_call(
        functools.partial(interior_kernel, geometry),
        out_shape=outs,
        in_specs=[IN_SMEM] * 2 + [IN_HBM] * 4 + [ANYWHERE] * sides,
        out_specs=[IN_VMEM] * len(outs),
        scratch_shapes=[
            VMEM(amp_shape.shape, BF16),
            pltpu.SemaphoreType.DMA((26 + sides + tile_cols // LANES,)),
        ],
        compiler_params=pltpu.CompilerParams(vmem_limit_bytes=KERNEL_VMEM),
        name="slots_interior",
        **SLOT_COST,
    )(offsets, counts, tile, probe, amps, tables, *halos)


def run_boundary(geometry, offsets, counts, straight, diagonal, corners, consts, ext, acc, sums):
    tile_rows, tile_cols, margin, sides = geometry
    planes, edge = sums.shape[:2]
    tiles = tile_cols // LANES
    part = shape(planes, edge // 2, edge)
    strip = shape(tiles, 2, margin, LANES)
    outs = [shape(*ext.shape), shape(*acc.shape), shape(*sums.shape)]
    outs += [shape(tiles, 2, tile_rows, LANES), strip, strip]
    outs += [shape(*acc.shape[1:])] * sides + [part, part]
    base = 4 + sides + 4
    return pl.pallas_call(
        functools.partial(boundary_kernel, geometry),
        out_shape=outs,
        in_specs=[IN_SMEM] * 2 + [ANYWHERE] * (2 + sides) + [IN_VMEM] * 7,
        out_specs=[IN_VMEM] * 3 + [IN_HBM] + [IN_VMEM] * (len(outs) - 4),
        scratch_shapes=[pltpu.SMEM((8,), jnp.int32), pltpu.SemaphoreType.DMA((16,))],
        input_output_aliases={base: 0, base + 1: 1, base + 2: 2},
        compiler_params=pltpu.CompilerParams(vmem_limit_bytes=KERNEL_VMEM),
        name="slots_boundary",
        **SLOT_COST,
    )(offsets, counts, straight, diagonal, *corners, *consts, ext, acc, sums)


def fold_kernel(geometry, over_straight, over_diagonal, *refs):
    frame = Frame(*geometry)
    received, (straight, low, high, diagonal) = refs[: frame.sides], refs[frame.sides :]
    for number, (over, out) in enumerate(((over_straight, straight), (over_diagonal, diagonal))):
        out[...] = over[...]
        for side, value in enumerate(received):
            out[frame.side_target(side) - 1] += value[:, frame.halo_rows(number), :]
    low[...] = diagonal[pl.ds(0, low.shape[0])]
    high[...] = diagonal[pl.ds(low.shape[0], low.shape[0])]


def light_kernel(geometry, own, *refs):
    frame = Frame(*geometry)
    others, (probe, out, canvas) = refs[:-3], refs[-3:]
    tiles = frame.tiles
    edge = probe.shape[-1]
    modes = probe.shape[1]
    canvas[...] = jnp.zeros_like(canvas)
    power = [
        sum(
            probe[c, k, :, pl.ds(t * LANES, LANES)] * probe[c, k, :, pl.ds(t * LANES, LANES)]
            for c in range(2)
            for k in range(modes)
        )
        for t in range(2)
    ]

    def add_from(read):
        def visit(slot, carry):
            row = read(0, slot) - frame.row * frame.tile_rows + edge
            col = read(1, slot) - frame.col * frame.tile_cols + edge
            meets = (row > 0) & (row < frame.tile_rows + edge) & (col > 0) & (col < frame.tile_cols + edge)

            @pl.when(meets)
            def _():
                block = col // LANES
                add_window(canvas, 0, power, row, block, col - block * LANES)

            return carry

        lax.fori_loop(0, read(2, 0), visit, 0)

    add_from(lambda plane, slot: own[plane, slot])
    for other in others:
        if len(other.shape) == 2:
            add_from(lambda plane, slot, other=other: other[plane, slot])
        else:
            for tile in range(other.shape[0]):
                add_from(lambda plane, slot, other=other, tile=tile: other[tile, plane, slot])
    for t in range(tiles):
        out[t] = canvas[edge // LANES + t, 0, pl.ds(edge, frame.tile_rows), :]


def object_kernel(geometry, tile, mid, light, from_straight, from_low, from_high, *refs):
    frame = Frame(*geometry)
    received, (out, stage, sems) = refs[: frame.sides], refs[frame.sides :]
    half = from_low.shape[0]
    copies = []
    for t in range(frame.tiles):
        stage[t] = mid[t]
        for side, value in enumerate(received):

            @pl.when(frame.side_target(side) == 1 + t)
            def _(value=value, t=t):
                stage[t] += value[:, frame.body, :]

        stage[t, :, frame.strip_rows(0), :] += from_straight[t]
        stage[t, :, frame.strip_rows(1), :] += from_low[t] if t < half else from_high[t - half]
        scale = 1.0 / (light[t] + 1.0)
        cols = pl.ds(t * LANES, LANES)
        for c in range(2):
            stage[t, c] = tile[c, :, cols] + stage[t, c] * scale
        copy = pltpu.make_async_copy(stage.at[t], out.at[:, :, cols], sems.at[t])
        copy.start()
        copies.append(copy)
    for copy in copies:
        copy.wait()


def member_perm(axis, bits, member):
    mask = sum(((member >> position) & 1) << bit for position, bit in enumerate(bits))
    return [(i, i ^ mask) for i in range(lax.axis_size(axis))]


def member_index(axis, bits):
    where = lax.axis_index(axis)
    return sum(((where >> bit) & 1) << position for position, bit in enumerate(bits))


def combine_kernel(inputs, stage, *refs):
    ins, outs = refs[:inputs], refs[inputs:]
    rows = outs[0].shape[1]
    for member, out in enumerate(outs):
        part = slice(None)
        if len(outs) > 1:
            part = aligned(jnp.bitwise_xor(member_index(*stage), member) * rows, rows)
        value = ins[0][:, part, :]
        for other in ins[1:]:
            value = value + other[:, part, :]
        out[...] = value


def combine(stage, parts, group):
    planes, rows, cols = parts[0].shape
    if (rows // group) % 8:
        total = sum(parts[1:], parts[0])
        if group == 1:
            return [total]
        rows = rows // group
        return [
            lax.dynamic_slice_in_dim(
                total, jnp.bitwise_xor(member_index(*stage), m) * rows, rows, axis=1
            )
            for m in range(group)
        ]
    return small_call(
        functools.partial(combine_kernel, len(parts), stage),
        [shape(planes, rows // group, cols)] * group,
        [IN_VMEM] * len(parts),
    )(*parts)


def place_kernel(group, stage, *refs):
    ins, out = refs[:group], refs[group]
    rows = ins[0].shape[1]
    for member, piece in enumerate(ins):
        at = jnp.bitwise_xor(member_index(*stage), member) * rows
        out[:, aligned(at, rows), :] = piece[...]


def place(stage, parts):
    planes, rows, cols = parts[0].shape
    if rows % 8:
        whole = jnp.zeros((planes, rows * len(parts), cols), F32)
        for m, piece in enumerate(parts):
            at = jnp.bitwise_xor(member_index(*stage), m) * rows
            whole = lax.dynamic_update_slice_in_dim(whole, piece, at, axis=1)
        return whole
    return small_call(
        functools.partial(place_kernel, len(parts), stage),
        [shape(planes, rows * len(parts), cols)],
        [IN_VMEM] * len(parts),
    )(*parts)[0]


def shard_start(stages, edge):
    start, rows = jnp.int32(0), edge
    for axis, bits in stages:
        rows = rows >> len(bits)
        start = start + member_index(axis, bits) * rows
    return start


def finish_kernel(stages, edge, probe, *refs):
    ins, out = refs[:-1], refs[-1]
    total = ins[0][...]
    for other in ins[1:]:
        total = total + other[...]
    planes, rows = out.shape[:2]
    old = probe[:, aligned(shard_start(stages, edge), rows), :]
    out[...] = old + total[:planes] / (total[planes:] + 1.0)


def finish(stages, probe, parts):
    planes, rows, cols = parts[0].shape
    edge = probe.shape[1]
    if rows % 8:
        total = sum(parts[1:], parts[0])
        old = lax.dynamic_slice_in_dim(probe, shard_start(stages, edge), rows, axis=1)
        return old + total[:-1] / (total[-1:] + 1.0)
    return small_call(
        functools.partial(finish_kernel, stages, edge),
        [shape(planes - 1, rows, cols)],
        [IN_VMEM] * (1 + len(parts)),
    )(probe, *parts)[0]


def swap_sides(outs):
    count = lax.axis_size("col")
    if len(outs) == 1:
        return [lax.ppermute(outs[0], "col", [(0, 1), (1, 0)])]
    up = [(i, i + 1) for i in range(count - 1)]
    down = [(i + 1, i) for i in range(count - 1)]
    return [lax.ppermute(outs[1], "col", up), lax.ppermute(outs[0], "col", down)]


def swap_rows(value, number):
    count = lax.axis_size("row")
    pairs = []
    for low in range(number, count - 1, 2):
        pairs += [(low, low + 1), (low + 1, low)]
    return lax.ppermute(value, "row", pairs)


def stages_of(rows, cols):
    stages = [("col", (bit,)) for bit in range(cols.bit_length() - 1)]
    bits = list(range(1, rows.bit_length() - 1)) + [0]
    while bits:
        stages.append(("row", tuple(bits[:2])))
        bits = bits[2:]
    return tuple(stages)


def step(object_field, probe_modes, scan_offsets, scan_counts, amplitudes):
    tile_rows, tile_cols = object_field.shape[1:]
    modes = probe_modes.shape[1]
    edge = probe_modes.shape[-1]
    margin = edge // 2
    slots = amplitudes.shape[2]
    tiles = tile_cols // LANES
    sides = 1 if lax.axis_size("col") == 2 else 2
    geometry = (tile_rows, tile_cols, margin, sides)
    stages = stages_of(lax.axis_size("row"), lax.axis_size("col"))
    tables = in_hbm(jnp.asarray(dft_tables(edge)))
    tile_hbm, probe_hbm, amps_hbm = in_hbm(object_field), in_hbm(probe_modes), in_hbm(amplitudes)

    def pack(first, outs):
        return small_call(
            functools.partial(pack_kernel, geometry, first),
            outs,
            [IN_HBM],
            limit=8 * MIB,
            scratch=(pltpu.SemaphoreType.DMA((3,)),),
        )(tile_hbm)

    strip = shape(2, margin, tile_cols)
    straight = swap_rows(pack(True, [strip])[0], 0)
    packed, *edges = pack(False, [strip] + [shape(2, tile_rows, margin)] * sides)
    diagonal = swap_rows(packed, 1)
    halos = swap_sides(edges)

    own = jnp.concatenate(
        [scan_offsets[0, 0], jnp.broadcast_to(scan_counts[0], (1, slots))], axis=0
    )
    stacked = jnp.stack([own, swap_rows(own, 0), swap_rows(own, 1)])
    beside = swap_sides([stacked] * sides)

    ext, acc, sums, *consts = run_interior(
        geometry, scan_offsets, scan_counts, tile_hbm, probe_hbm, amps_hbm, tables, halos
    )

    cut = small_call(
        functools.partial(corner_kernel, geometry),
        [shape(2, 2, margin, margin)] * sides,
        [IN_VMEM] * 2,
    )(straight, diagonal)
    corners = swap_sides(cut)

    _, _, _, mid, *rest = run_boundary(
        geometry, scan_offsets, scan_counts, straight, diagonal, corners, consts, ext, acc, sums
    )
    overs, side_outs, (keep, send) = rest[:2], rest[2 : 2 + sides], rest[2 + sides :]

    parts = [keep]
    for number, stage in enumerate(stages):
        axis, bits = stage
        if number:
            mine, *pieces = combine(stage, parts, 1 << len(bits))
        else:
            mine, pieces = keep, [send]
        parts = [mine] + [
            lax.ppermute(piece, axis, member_perm(axis, bits, member + 1))
            for member, piece in enumerate(pieces)
        ]
    received = swap_sides(side_outs)
    strip = shape(tiles, 2, margin, LANES)
    chunk = shape(tiles // 2, 2, margin, LANES)
    out_straight, out_low, out_high = small_call(
        functools.partial(fold_kernel, geometry),
        [strip, chunk, chunk],
        [IN_VMEM] * (2 + sides),
        scratch=(VMEM(strip.shape, F32),),
    )(*overs, *received)
    from_straight = swap_rows(out_straight, 0)
    from_low = swap_rows(out_low, 1)
    from_high = swap_rows(out_high, 1)

    flat = probe_modes.reshape(2 * modes, edge, edge)
    shard = finish(stages, flat, parts)
    for number, stage in reversed(list(enumerate(stages))):
        axis, bits = stage
        pieces = [shard] + [
            lax.ppermute(shard, axis, member_perm(axis, bits, member))
            for member in range(1, 1 << len(bits))
        ]
        shard = place(stage, pieces)
    probe_new = shard.reshape(probe_modes.shape)

    light = small_call(
        functools.partial(light_kernel, geometry),
        [shape(tiles, tile_rows, LANES)],
        [IN_SMEM] * (2 + sides) + [IN_VMEM],
        limit=8 * MIB,
        scratch=(VMEM((tiles + 2 * (edge // LANES), 1, tile_rows + 2 * edge, LANES), F32),),
        cost=10_000_000,
    )(own, stacked[1:], *beside, probe_modes)[0]
    object_new = small_call(
        functools.partial(object_kernel, geometry),
        [shape(2, tile_rows, tile_cols)],
        [IN_VMEM] * (6 + sides),
        limit=8 * MIB,
        scratch=(
            VMEM((tiles, 2, tile_rows, LANES), F32),
            pltpu.SemaphoreType.DMA((tiles,)),
        ),
        out_specs=[IN_HBM],
    )(object_field, mid, light, from_straight, from_low, from_high, *received)[0]
    return object_new, probe_new


def solution(mesh):
    in_specs = (
        P(None, "row", "col"),
        P(),
        P("row", "col", None, None),
        P("row", "col"),
        P("row", "col", None, None, None),
    )
    out_specs = (P(None, "row", "col"), P())
    return jax.shard_map(step, mesh=mesh, in_specs=in_specs, out_specs=out_specs, check_vma=False)
```
